32 devices in a mesh: head: 4 (over z), tok: 8 (over y, x, core).
Axes of the slice: x: 2, y: 2, z: 4, core: 2. Of those that a mesh axis runs over, the one named last changes fastest.
Arguments:
- teacher_q: bfloat16 [1024, 1024], P('tok', 'head'), may hold values from -48 to 48
- student_q: bfloat16 [1024, 1024], P('tok', 'head'), may hold values from -48 to 48
- owner_table: int32 [8, 8], replicated, may hold values from -1 to 7, as said below
Outputs:
- student_grad: bfloat16 [1024, 1024], P('tok', 'head')
- divergence: float32 [16], P('head')
The draws below stay inside these ranges and needn't reach their ends.
Inputs may be any that keep to these rules, and one draw needn't show every extreme that they name: `owner_table`: Symmetric; every diagonal entry is an owner; an owner is a tok index; each tok index owns at most 2 pairs i <= j, and some tok index owns exactly 2 in every draw.
All inputs are finite; a program needn't handle non-finite values.
Results may differ from the reference program's by a relative error of at most 0.0049.
Values may be sent and summed in bfloat16 or wider, within the bound.
A program may use at most 64 MiB of HBM per device.

```python
import jax
import jax.numpy as jnp
import numpy as np
from jax import lax

HEAD_DIM = 64
TOK_DEV = 128
REL_HEADS = 16
TOKENS = 1024
BLOCKS = 8
PAIR_MOST = 2


def draw_queries(key):
    base = jnp.clip(jax.random.normal(key, (TOKENS, REL_HEADS, HEAD_DIM)), -6.0, 6.0)
    return base.reshape(TOKENS, REL_HEADS * HEAD_DIM).astype(jnp.bfloat16)


def draw_teacher_q(key, part):
    return draw_queries(jax.random.fold_in(key, 11))


def draw_student_q(key, part):
    return draw_queries(jax.random.fold_in(key, 23))


def draw_owner_table(key, part):
    upper_rows, upper_cols = np.triu_indices(BLOCKS)
    every_place = np.arange(upper_rows.shape[0])
    diagonal_places = every_place[upper_rows == upper_cols]
    other_places = every_place[upper_rows != upper_cols]
    key_diag, key_other, key_caps, key_owner = jax.random.split(jax.random.fold_in(key, 7), 4)
    ordering = jnp.concatenate([jax.random.permutation(key_diag, jnp.asarray(diagonal_places, jnp.int32)), jax.random.permutation(key_other, jnp.asarray(other_places, jnp.int32))])
    capacity = jax.random.randint(key_caps, (BLOCKS,), 1, PAIR_MOST + 1).astype(jnp.int32).at[0].set(PAIR_MOST)
    owners_order = jax.random.permutation(key_owner, BLOCKS).astype(jnp.int32)
    bounds = jnp.cumsum(capacity)
    positions = jnp.arange(upper_rows.shape[0], dtype=jnp.int32)
    which = jnp.sum((bounds[None, :] <= positions[:, None]).astype(jnp.int32), axis=1)
    owners = jnp.where(which < BLOCKS, owners_order[jnp.minimum(which, BLOCKS - 1)], -1)
    pair_rows = jnp.asarray(upper_rows, jnp.int32)[ordering]
    pair_cols = jnp.asarray(upper_cols, jnp.int32)[ordering]
    table = jnp.full((BLOCKS, BLOCKS), -1, jnp.int32)
    table = table.at[pair_rows, pair_cols].set(owners)
    return table.at[pair_cols, pair_rows].set(owners)


def setup_inputs(seed: int = 0) -> dict:
    splits = jax.random.split(jax.random.key(seed), 4)
    teacher_q = draw_teacher_q(jax.random.fold_in(splits[3], 71), 0)
    student_q = draw_student_q(jax.random.fold_in(splits[3], 71), 0)
    owner_table = draw_owner_table(jax.random.fold_in(splits[3], 71), 0)
    return {"teacher_q": teacher_q, "student_q": student_q, "owner_table": owner_table}


floor_value = -1e+30
distill_weight = 32.0

def reference(teacher_q, student_q, owner_table):
    scale = HEAD_DIM ** (-0.5)
    length = teacher_q.shape[0]
    inside = jnp.repeat(jnp.repeat(owner_table >= 0, TOK_DEV, axis=0), TOK_DEV, axis=1)
    heads_teacher = teacher_q.reshape(length, REL_HEADS, HEAD_DIM).transpose(1, 0, 2)
    heads_student = student_q.reshape(length, REL_HEADS, HEAD_DIM).transpose(1, 0, 2)

    def logsum(scores):
        masked = jnp.where(inside, scores, floor_value)
        highest = jnp.max(masked, axis=1)
        return highest + jnp.log(jnp.sum(jnp.exp(masked - highest[:, None]), axis=1))

    def one_head(queries):
        teacher_head, student_head = queries
        teacher_scores = jnp.dot(teacher_head.astype(jnp.float32), teacher_head.T.astype(jnp.float32), preferred_element_type=jnp.float32) * scale
        student_scores = jnp.dot(student_head.astype(jnp.float32), student_head.T.astype(jnp.float32), preferred_element_type=jnp.float32) * scale
        teacher_logsum = logsum(teacher_scores)
        student_logsum = logsum(student_scores)
        teacher_prob = jnp.where(inside, jnp.exp(teacher_scores - teacher_logsum[:, None]), 0.0)
        student_prob = jnp.where(inside, jnp.exp(student_scores - student_logsum[:, None]), 0.0)
        row_div = jnp.sum(teacher_prob * (teacher_scores - student_scores), axis=1) - teacher_logsum + student_logsum
        score_gap = student_prob - teacher_prob
        symmetric = (score_gap + score_gap.T).astype(jnp.bfloat16)
        gradient = jnp.dot(symmetric.astype(jnp.float32), student_head.astype(jnp.float32), preferred_element_type=jnp.float32) * (scale * distill_weight)
        return (gradient.astype(jnp.bfloat16), jnp.mean(row_div))
    gradients, divergence = lax.map(one_head, (heads_teacher, heads_student))
    return (gradients.transpose(1, 0, 2).reshape(length, REL_HEADS * HEAD_DIM), divergence)
```

```python
import functools
import math

import jax
import jax.numpy as jnp
from jax import lax
from jax.experimental import pallas as pl
from jax.experimental.pallas import tpu as pltpu
from jax.sharding import PartitionSpec as P

HEAD_DIM = 64
LANES = 128
floor_value = -1e30
distill_weight = 32.0
score_factor = HEAD_DIM ** (-0.5) * math.log2(math.e)
MESH = pl.DeviceIdType.MESH


def repeat(count, body, init=None):
    if count <= 8:
        for step in range(count):
            init = body(step, init)
        return init
    return lax.fori_loop(0, count, body, init)


def kernel(
    n, teacher_hbm, student_hbm, table_hbm, in_grad, in_div,
    teacher, student, outbox, inbox, own, scores, top, logs, row_part, stats,
    out_grad, out_div, local_sem, send_sem, recv_sem, stat_send, stat_recv, back_send, back_recv, table, tab_sem,
):
    rows, width = teacher_hbm.shape
    pairs = width // LANES
    heads = width // HEAD_DIM
    group = LANES // HEAD_DIM
    parts = n // heads
    chips = n // 2
    side = math.isqrt(chips)
    side = side if side * side == chips else 1
    span = chips // side
    half = rows // 2
    own_rows = heads * rows
    me = lax.axis_index("tok")
    head_at = lax.axis_index("head")
    chip, core = me // 2, me % 2
    head, part = me // parts, me % parts

    def spot(tok):
        return (head_at, tok)

    def shifted(k, sign):
        high = (chip // span + sign * (k // span) + side) % side
        low = (chip % span + sign * (k % span) + span) % span
        return high * span + low

    def remote(src, dst, send, recv, target):
        return pltpu.make_async_remote_copy(
            src_ref=src, dst_ref=dst, send_sem=send, recv_sem=recv,
            device_id=spot(target), device_id_type=MESH,
        )

    barrier = pltpu.get_barrier_semaphore()
    loads = [
        pltpu.make_async_copy(teacher_hbm, teacher, local_sem.at[0]),
        pltpu.make_async_copy(student_hbm, student, local_sem.at[1]),
    ]
    for load in loads:
        load.start()
    tload = pltpu.make_async_copy(table_hbm, table, tab_sem)
    tload.start()

    def greet(d, carry):
        pl.semaphore_signal(barrier, inc=1, device_id=spot((me + d + 1) % n), device_id_type=MESH)
        return carry

    repeat(n - 1, greet)
    for load in loads:
        load.wait()
    lane = lax.broadcasted_iota(jnp.int32, (rows, LANES), 1)
    lower = lane < HEAD_DIM
    for pair in range(pairs):
        columns = pl.ds(pair * LANES, LANES)
        t_pair = teacher[:, columns].astype(jnp.float32)
        s_pair = student[:, columns].astype(jnp.float32)
        outbox[pair * group] = jnp.where(lower, t_pair, pltpu.roll(s_pair, HEAD_DIM, 1)).astype(
            jnp.bfloat16
        )
        outbox[pair * group + 1] = jnp.where(
            lower, pltpu.roll(t_pair, HEAD_DIM, 1), s_pair
        ).astype(jnp.bfloat16)
    inbox[pl.ds(me * rows, rows), :] = outbox[head]
    pl.semaphore_wait(barrier, n - 1)

    def query_copy(k, other, target):
        return remote(
            outbox.at[target // parts],
            inbox.at[pl.ds(me * rows, rows), :],
            send_sem.at[k, other],
            recv_sem.at[k, other],
            target,
        )

    def away(k, other, sign):
        return shifted(k, sign) * 2 + (1 - core if other else core)

    def send_queries(step, carry):
        k = chips - 1 - step
        for other in range(2):
            query_copy(k, other, away(k, other, 1)).start()
        return carry

    repeat(chips - 1, send_queries)
    query_copy(0, 1, away(0, 1, 1)).start()

    query_copy(0, 1, away(0, 1, -1)).wait_recv()

    def take_queries(step, carry):
        for other in range(2):
            query_copy(step + 1, other, away(step + 1, other, -1)).wait_recv()
        return carry

    repeat(chips - 1, take_queries)

    none = jnp.zeros((), jnp.bfloat16)
    for place in range(heads):
        block = inbox[pl.ds((part * heads + place) * rows, rows), :]
        own[pl.ds(place * rows, rows), :] = jnp.where(lower, block, none)
        own[pl.ds(own_rows + place * rows, rows), :] = jnp.where(lower, none, block)

    tload.wait()
    top[...] = jnp.full(top.shape, 2 * floor_value, jnp.float32)

    def score_turn(step, carry):
        right = inbox[pl.ds(step * 2 * rows, 2 * rows), :]
        raw = lax.dot_general(
            own[...], right, (((1,), (1,)), ((), ())), preferred_element_type=jnp.float32
        )
        for place in range(heads):
            for near in range(2):
                block = step * 2 + near
                bias = jnp.where(table[part * heads + place, block] >= 0, 0.0, floor_value)
                for which in range(2):
                    begin = which * own_rows + place * rows
                    at = pl.ds(begin, rows)
                    tile = (
                        raw[begin : begin + rows, near * rows : (near + 1) * rows] * score_factor
                        + bias.astype(jnp.float32)
                    )
                    scores[block, at, :] = tile
                    top[at, :] = jnp.maximum(top[at, :], tile)
        return carry

    repeat(n // 2, score_turn)

    wide = jnp.zeros((rows, LANES), jnp.float32)
    for place in range(heads):
        t_at, s_at = pl.ds(place * rows, rows), pl.ds(own_rows + place * rows, rows)
        t_high = jnp.max(top[t_at, :], axis=1, keepdims=True)
        s_high = jnp.max(top[s_at, :], axis=1, keepdims=True)
        blank = jnp.zeros((rows, LANES), jnp.float32)

        def sum_turn(block, carry):
            t_sum, s_sum, gap_sum = carry
            t_tile, s_tile = scores[block, t_at, :], scores[block, s_at, :]
            t_exp = jnp.exp2(t_tile - t_high)
            return (
                t_sum + t_exp,
                s_sum + jnp.exp2(s_tile - s_high),
                gap_sum + t_exp * (t_tile - s_tile),
            )

        t_sum, s_sum, gap_sum = [
            jnp.sum(piece, axis=1, keepdims=True)
            for piece in repeat(n, sum_turn, (blank, blank, blank))
        ]
        t_line = t_high + jnp.log2(t_sum)
        s_line = s_high + jnp.log2(s_sum)
        div_line = gap_sum / t_sum - t_line + s_line
        logs[t_at, :] = jnp.broadcast_to(t_line, (rows, LANES))
        logs[s_at, :] = jnp.broadcast_to(s_line, (rows, LANES))
        wide = jnp.where(lane == place, t_line, wide)
        wide = jnp.where(lane == heads + place, s_line, wide)
        wide = jnp.where(lane == 2 * heads + place, div_line, wide)
    stats[part] = wide.T[: stats.shape[1]]

    def stat_copy(step, target):
        return remote(
            stats.at[part], stats.at[part], stat_send.at[step], stat_recv.at[step], target
        )

    def send_stats(step, carry):
        stat_copy(step, head * parts + (part + step + 1) % parts).start()
        return carry

    repeat(parts - 1, send_stats)

    def row_turn(block, carry):
        for place in range(heads):
            t_at, s_at = pl.ds(place * rows, rows), pl.ds(own_rows + place * rows, rows)
            row_part[block, t_at, :] = jnp.exp2(scores[block, s_at, :] - logs[s_at, :]) - jnp.exp2(
                scores[block, t_at, :] - logs[t_at, :]
            )
        return carry

    repeat(n, row_turn)

    def take_stats(step, carry):
        stat_copy(step, head * parts + (part - step - 1 + parts) % parts).wait_recv()
        return carry

    repeat(parts - 1, take_stats)

    def div_turn(step, carry):
        return carry + stats[step, pl.ds(2 * heads, heads), :]

    div_sum = repeat(parts, div_turn, jnp.zeros((heads, rows), jnp.float32))
    div_sum = jnp.sum(jnp.sum(div_sum, axis=0, keepdims=True), axis=1, keepdims=True)
    out_div[...] = jnp.broadcast_to(div_sum * (math.log(2.0) / (rows * n)), out_div.shape)

    def div_copy(place, slot, target):
        return remote(out_div, in_div.at[head], back_send.at[1, place], back_recv.at[1, slot], target)

    def grad_copy(place, slot, target):
        return remote(
            out_grad.at[place], in_grad.at[head], back_send.at[0, place], back_recv.at[0, slot], target
        )

    for place in range(heads):
        target = part * heads + place

        @pl.when(target != me)
        def send_div():
            div_copy(place, head, target).start()

        @pl.when(target == me)
        def keep_div():
            keep = pltpu.make_async_copy(out_div, in_div.at[head], local_sem.at[0])
            keep.start()
            keep.wait()

    half_lower = lax.broadcasted_iota(jnp.int32, (half, LANES), 1) < HEAD_DIM
    run = heads // 2
    for turn in range(2):
        place_base = (chip + 1 + turn) % 2 * run

        def gradient_turn(step, carry):
            lines = []
            for inner in range(run):
                place = place_base + inner
                t_at = pl.ds(pl.multiple_of(place * rows, rows), rows)
                s_at = pl.ds(pl.multiple_of(own_rows + place * rows, rows), rows)
                pieces = []
                for near in range(2):
                    block = step * 2 + near
                    line = stats.at[block // heads]
                    t_line = line[pl.ds(block % heads, 1), :]
                    s_line = line[pl.ds(heads + block % heads, 1), :]
                    column_part = jnp.exp2(scores[block, s_at, :] - s_line) - jnp.exp2(
                        scores[block, t_at, :] - t_line
                    )
                    pieces.append((row_part[block, t_at, :] + column_part).astype(jnp.bfloat16))
                lines.append(jnp.concatenate(pieces, axis=1))
            return carry + jnp.dot(
                jnp.concatenate(lines, axis=0),
                inbox[pl.ds(step * 2 * rows, 2 * rows), :],
                preferred_element_type=jnp.float32,
            )

        total = repeat(n // 2, gradient_turn, jnp.zeros((run * rows, LANES), jnp.float32))
        for inner in range(run):
            place = place_base + inner
            target = part * heads + place
            upper_rows = total[inner * rows : inner * rows + half]
            lower_rows = total[inner * rows + half : (inner + 1) * rows]
            out_grad[place] = (
                jnp.where(half_lower, pltpu.roll(upper_rows, HEAD_DIM, 1), lower_rows)
                * (distill_weight * HEAD_DIM ** (-0.5))
            ).astype(jnp.bfloat16)

            @pl.when(target != me)
            def send_grad():
                grad_copy(place, head, target).start()

    @pl.when(part == me // heads)
    def keep_grad():
        keep = pltpu.make_async_copy(out_grad.at[me % heads], in_grad.at[head], local_sem.at[1])
        keep.start()
        keep.wait()

    for slot in range(heads):
        source = slot * parts + me // heads

        @pl.when(source != me)
        def take_back():
            div_copy(0, slot, source).wait_recv()
            grad_copy(0, slot, source).wait_recv()

    query_copy(0, 1, away(0, 1, 1)).wait_send()

    def drain(step, carry):
        for other in range(2):
            query_copy(step + 1, other, away(step + 1, other, 1)).wait_send()
        return carry

    repeat(chips - 1, drain)

    def drain_stats(step, carry):
        stat_copy(step, head * parts + (part + step + 1) % parts).wait_send()
        return carry

    repeat(parts - 1, drain_stats)
    for place in range(heads):
        target = part * heads + place

        @pl.when(target != me)
        def drain_back():
            div_copy(place, head, target).wait_send()
            grad_copy(place, head, target).wait_send()


def unpack(in_grad, in_div, grad_ref, div_ref):
    heads, half = in_grad.shape[:2]
    group = LANES // HEAD_DIM
    half_lower = lax.broadcasted_iota(jnp.int32, (half, LANES), 1) < HEAD_DIM
    for pair in range(heads // group):
        first = in_grad[pair * group].astype(jnp.float32)
        second = in_grad[pair * group + 1].astype(jnp.float32)
        columns = pl.ds(pair * LANES, LANES)
        grad_ref[pl.ds(0, half), columns] = jnp.where(
            half_lower, first, pltpu.roll(second, HEAD_DIM, 1)
        ).astype(jnp.bfloat16)
        grad_ref[pl.ds(half, half), columns] = jnp.where(
            half_lower, pltpu.roll(first, HEAD_DIM, 1), second
        ).astype(jnp.bfloat16)
    div_lane = lax.broadcasted_iota(jnp.int32, (1, LANES), 1)
    div_row = jnp.zeros((1, LANES), jnp.float32)
    for slot in range(heads):
        div_row = jnp.where(div_lane == slot, in_div[slot, pl.ds(0, 1), :], div_row)
    div_ref[...] = div_row[:, :heads]


def per_device(n, teacher_q, student_q, owner_table):
    rows, width = teacher_q.shape
    heads = width // HEAD_DIM
    chips = n // 2
    parts = n // heads
    stat_rows = -(-3 * heads // 8) * 8
    hbm = pl.BlockSpec(memory_space=pl.ANY)
    packed = pl.pallas_call(
        functools.partial(kernel, n),
        out_shape=(
            pltpu.VMEM((heads, rows // 2, LANES), jnp.bfloat16),
            pltpu.VMEM((heads, 8, LANES), jnp.float32),
        ),
        in_specs=[pl.BlockSpec(memory_space=pltpu.HBM)] * 3,
        out_specs=(pl.BlockSpec(memory_space=pl.ANY),) * 2,
        scratch_shapes=[
            pltpu.VMEM((rows, width), jnp.bfloat16),
            pltpu.VMEM((rows, width), jnp.bfloat16),
            pltpu.VMEM((heads, rows, LANES), jnp.bfloat16),
            pltpu.VMEM((n * rows, LANES), jnp.bfloat16),
            pltpu.VMEM((2 * heads * rows, LANES), jnp.bfloat16),
            pltpu.VMEM((n, 2 * heads * rows, rows), jnp.float32),
            pltpu.VMEM((2 * heads * rows, rows), jnp.float32),
            pltpu.VMEM((2 * heads * rows, LANES), jnp.float32),
            pltpu.VMEM((n, heads * rows, rows), jnp.float32),
            pltpu.VMEM((parts, stat_rows, rows), jnp.float32),
            pltpu.VMEM((heads, rows // 2, LANES), jnp.bfloat16),
            pltpu.VMEM((8, LANES), jnp.float32),
            pltpu.SemaphoreType.DMA((2,)),
            pltpu.SemaphoreType.DMA((chips, 2)),
            pltpu.SemaphoreType.DMA((chips, 2)),
            pltpu.SemaphoreType.DMA((parts,)),
            pltpu.SemaphoreType.DMA((parts,)),
            pltpu.SemaphoreType.DMA((2, heads)),
            pltpu.SemaphoreType.DMA((2, heads)),
            pltpu.SMEM((n, n), jnp.int32),
            pltpu.SemaphoreType.DMA,
        ],
        compiler_params=pltpu.CompilerParams(
            collective_id=0, has_side_effects=True, vmem_limit_bytes=60 * 1024 * 1024
        ),
        name="distill",
    )(*[pltpu.with_memory_space_constraint(x, pltpu.HBM) for x in (teacher_q, student_q, owner_table)])
    grad, divergence = pl.pallas_call(
        unpack,
        out_shape=(
            jax.ShapeDtypeStruct((rows, width), jnp.bfloat16),
            jax.ShapeDtypeStruct((1, heads), jnp.float32),
        ),
        in_specs=[pl.BlockSpec(memory_space=pltpu.VMEM)] * 2,
        out_specs=(pl.BlockSpec(memory_space=pltpu.VMEM),) * 2,
        compiler_params=pltpu.CompilerParams(vmem_limit_bytes=4 * 1024 * 1024),
        name="unpack",
    )(*packed)
    return (grad, divergence.reshape(heads))


def solution(mesh):
    placed = (P("tok", "head"), P("tok", "head"), P())
    return jax.shard_map(
        functools.partial(per_device, mesh.shape["tok"]),
        mesh=mesh,
        in_specs=placed,
        out_specs=(P("tok", "head"), P("head")),
        check_vma=False,
    )
```

```python
import functools
import math

import jax
import jax.numpy as jnp
from jax import lax
from jax.experimental import pallas as pl
from jax.experimental.pallas import tpu as pltpu
from jax.sharding import PartitionSpec as P

HEAD_DIM = 64
LANES = 128
NOTE_ROWS = 16
KEEP_BYTES = 16 * 1024 * 1024
floor_value = -3e38
distill_weight = 32.0
score_factor = HEAD_DIM ** (-0.5) * math.log2(math.e)
MESH = pl.DeviceIdType.MESH


def repeat(count, body, init=None):
    if count <= 16:
        for step in range(count):
            init = body(step, init)
        return init
    return lax.fori_loop(0, count, body, init)


def kernel(
    n, most, keep, teacher_hbm, student_hbm, table_hbm, in_grad,
    teacher, student, outbox, inbox, left, turned, table, before, following,
    edge_row, edge_col, edge_back, edge_tag, tags, stats, weights, exps, gaps,
    running, diagonal, out_grad, load_sem, table_sem, send_sem, recv_sem, back_send, back_recv,
):
    rows, width = teacher_hbm.shape
    pairs = width // LANES
    heads = width // HEAD_DIM
    group = LANES // HEAD_DIM
    parts = n // heads
    chips = n // 2
    side = math.isqrt(chips)
    side = side if side * side == chips else 1
    span = chips // side
    me = lax.axis_index("tok")
    head_at = lax.axis_index("head")
    chip, core = me // 2, me % 2
    head = me // parts
    is_worker = me % parts == 0

    def place(step):
        shift, flip = step // 2, step % 2
        high = (chip // span + shift // span) % side
        low = (chip % span + shift % span) % span
        return (high * span + low) * 2 + (core + flip) % 2

    def place_in(worker):
        worker_chip = worker // 2
        high = (chip // span - worker_chip // span + side) % side
        low = (chip % span - worker_chip % span + span) % span
        return (high * span + low) * 2 + (core - worker % 2 + 2) % 2

    def remote(src, dst, send, recv, target):
        return pltpu.make_async_remote_copy(
            src_ref=src, dst_ref=dst, send_sem=send, recv_sem=recv,
            device_id=(head_at, target), device_id_type=MESH,
        )

    barrier = pltpu.get_barrier_semaphore()
    loads = [
        pltpu.make_async_copy(teacher_hbm, teacher, load_sem.at[0]),
        pltpu.make_async_copy(student_hbm, student, load_sem.at[1]),
    ]
    for load in loads:
        load.start()
    table_load = pltpu.make_async_copy(table_hbm, table, table_sem)
    table_load.start()

    def greet(target):
        pl.semaphore_signal(barrier, inc=1, device_id=(head_at, target), device_id_type=MESH)

    @pl.when(is_worker)
    def greet_all():
        def greet_one(step, carry):
            greet(place(n - 1 - step))
            return carry

        repeat(n - 1, greet_one)

    @pl.when(jnp.logical_not(is_worker))
    def greet_workers():
        for step in range(heads):
            greet((head + heads - 1 - step) % heads * parts)

    for load in loads:
        load.wait()
    lane = lax.broadcasted_iota(jnp.int32, (rows, LANES), 1)
    lower = lane < HEAD_DIM
    for pair in range(pairs):
        columns = pl.ds(pair * LANES, LANES)
        t_pair = teacher[:, columns].astype(jnp.float32)
        s_pair = student[:, columns].astype(jnp.float32)
        outbox[pair * group] = jnp.where(lower, t_pair, pltpu.roll(s_pair, HEAD_DIM, 1)).astype(
            jnp.bfloat16
        )
        outbox[pair * group + 1] = jnp.where(
            lower, pltpu.roll(t_pair, HEAD_DIM, 1), s_pair
        ).astype(jnp.bfloat16)

    def query_copy(to_head, slot):
        return remote(
            outbox.at[to_head], inbox.at[slot], send_sem.at[to_head], recv_sem.at[slot],
            to_head * parts,
        )

    def send_queries():
        for step in range(heads - 1, 0, -1):
            to_head = (head + step) % heads
            query_copy(to_head, place_in(to_head * parts)).start()

    def drain_queries():
        for step in range(heads - 1, 0, -1):
            query_copy((head + step) % heads, 0).wait_send()

    def grad_copy(slot, target):
        return remote(
            out_grad.at[slot], in_grad.at[head], back_send.at[slot], back_recv.at[head], target
        )

    def take_grads(own):
        for step in range(heads):
            from_head = (head + step) % heads
            if step == 0 and own:
                continue
            remote(
                out_grad.at[0], in_grad.at[from_head], back_send.at[0], back_recv.at[from_head],
                from_head * parts,
            ).wait_recv()

    @pl.when(jnp.logical_not(is_worker))
    def serve():
        pl.semaphore_wait(barrier, heads)
        send_queries()
        query_copy(head, place_in(head * parts)).start()
        drain_queries()
        query_copy(head, 0).wait_send()
        table_load.wait()
        take_grads(False)

    @pl.when(is_worker)
    def work():
        inbox[0] = outbox[head]
        pl.semaphore_wait(barrier, n - 1)
        send_queries()
        table_load.wait()
        codes = n * n

        def count_row(rank, count):
            row = n - 1 - rank
            row_at = place(row)

            def count_cell(col, count):
                inside = jnp.logical_and(table[row_at, place(col)] >= 0, col != row)
                before[rank * n + col] = count
                return count + jnp.where(inside, 1, 0)

            return repeat(n, count_cell, count)

        before[codes] = repeat(n, count_row, jnp.int32(0))
        following[codes] = jnp.int32(codes)
        following[codes + 1] = jnp.int32(codes)

        def link_row(step, after):
            rank = n - 1 - step
            row = step
            row_at = place(row)

            def link_cell(back, after):
                col = n - 1 - back
                inside = jnp.logical_and(table[row_at, place(col)] >= 0, col != row)
                after = jnp.where(inside, rank * n + col, after)
                following[rank * n + col] = after
                return after

            return repeat(n, link_cell, after)

        repeat(n, link_row, jnp.int32(codes))

        def list_edge(edge, code):
            code = following[code + 1]
            held = jnp.minimum(code, codes - 1)
            row, col = n - 1 - held // n, held % n
            edge_row[edge] = row
            edge_col[edge] = col
            edge_back[edge] = jnp.minimum(before[(n - 1 - col) * n + row], most - 1)
            tag = jnp.where(code < codes, row, -1)
            edge_tag[edge] = tag
            tags[pl.ds(edge, 1), :] = jnp.full((1, LANES), tag, jnp.int32)
            return code

        repeat(most, list_edge, jnp.int32(-1))

        def tag_diagonal(slot, carry):
            tags[pl.ds(most + slot, 1), :] = jnp.full((1, LANES), slot, jnp.int32)
            return carry

        repeat(n, tag_diagonal)

        def scores(col, row):
            raw = lax.dot_general(
                left[col], inbox[row], (((1,), (1,)), ((), ())),
                preferred_element_type=jnp.float32,
            )
            return raw[:rows], raw[rows:]

        def measure(entry, col, row):
            t_raw, s_raw = scores(col, row)
            t_top = jnp.max(t_raw, axis=0, keepdims=True)
            s_top = jnp.max(s_raw, axis=0, keepdims=True)
            t_exp = jnp.exp2((t_raw - t_top) * score_factor)
            s_exp = jnp.exp2((s_raw - s_top) * score_factor)
            at = pl.ds(entry, 1)
            stats[0, at, :] = t_top
            stats[1, at, :] = s_top
            stats[2, at, :] = jnp.sum(t_exp, axis=0, keepdims=True)
            stats[3, at, :] = jnp.sum(s_exp, axis=0, keepdims=True)
            stats[4, at, :] = jnp.sum(t_exp * (t_raw - s_raw), axis=0, keepdims=True)
            if keep:
                exps[entry, 0] = t_exp
                exps[entry, 1] = s_exp

        none = jnp.zeros((), jnp.bfloat16)

        def take_block(slot, carry):
            @pl.when(slot > 0)
            def wait_block():
                remote(
                    outbox.at[0], inbox.at[slot], send_sem.at[0], recv_sem.at[slot], place(slot)
                ).wait_recv()

            block = inbox[slot]
            left[slot, pl.ds(0, rows), :] = jnp.where(lower, block, none)
            left[slot, pl.ds(rows, rows), :] = jnp.where(lower, none, block)
            turned[slot] = block.T[HEAD_DIM:]
            measure(most + slot, slot, slot)
            return carry

        repeat(n, take_block)

        def measure_edge(edge, carry):
            measure(edge, edge_col[edge], edge_row[edge])
            return carry

        repeat(most, measure_edge)

        weights[...] = jnp.zeros(weights.shape, jnp.float32)

        def combine(slot, total):
            mine = tags[...] == slot
            tops, sums = [], []
            for which in range(2):
                peak = stats[which]
                top = jnp.max(jnp.where(mine, peak, floor_value), axis=0, keepdims=True)
                part = jnp.exp2(jnp.where(mine, (peak - top) * score_factor, floor_value))
                amount = jnp.sum(part * stats[2 + which], axis=0, keepdims=True)
                inverse = 1.0 / amount
                weights[which] = jnp.where(mine, part * inverse, weights[which])
                if which == 0:
                    cross = jnp.sum(part * stats[4], axis=0, keepdims=True) * inverse
                tops.append(top)
                sums.append(amount)
            return (
                total
                + (cross - tops[0] + tops[1]) * score_factor
                - jnp.log2(sums[0])
                + jnp.log2(sums[1])
            )

        total = repeat(n, combine, jnp.zeros((1, LANES), jnp.float32))
        total = jnp.sum(total, axis=1, keepdims=True) * (math.log(2.0) / (rows * n))
        first = total.astype(jnp.bfloat16).astype(jnp.float32)
        second = (total - first).astype(jnp.bfloat16).astype(jnp.float32)
        note_row = lax.broadcasted_iota(jnp.int32, (NOTE_ROWS, LANES), 0)
        note = jnp.where(
            note_row == 0,
            first,
            jnp.where(
                note_row == 1, second, jnp.where(note_row == 2, total - first - second, 0.0)
            ),
        ).astype(jnp.bfloat16)

        def gap_of(entry, col, row):
            at = pl.ds(entry, 1)
            if keep:
                t_exp, s_exp = exps[entry, 0], exps[entry, 1]
            else:
                t_raw, s_raw = scores(col, row)
                t_exp = jnp.exp2((t_raw - stats[0, at, :]) * score_factor)
                s_exp = jnp.exp2((s_raw - stats[1, at, :]) * score_factor)
            gaps[entry] = (s_exp * weights[1, at, :] - t_exp * weights[0, at, :]).astype(
                jnp.bfloat16
            )

        def gap_edge(edge, carry):
            gap_of(edge, edge_col[edge], edge_row[edge])
            return carry

        def gap_diagonal(slot, carry):
            gap_of(most + slot, slot, slot)
            return carry

        repeat(most, gap_edge)
        repeat(n, gap_diagonal)

        def product(col, entry, back):
            query = turned[col]
            return jnp.dot(
                query, gaps[entry], preferred_element_type=jnp.float32
            ) + lax.dot_general(
                query, gaps[back], (((1,), (1,)), ((), ())), preferred_element_type=jnp.float32
            )

        def add_edge(edge, carry):
            line, last = carry
            tag = edge_tag[edge]
            fresh = product(edge_col[edge], edge, edge_back[edge])
            line = jnp.where(tag == last, line, 0.0) + fresh
            running[edge] = line
            return line, tag

        repeat(most, add_edge, (jnp.zeros((HEAD_DIM, rows), jnp.float32), jnp.int32(-1)))

        def finish(step, carry):
            slot = n - 1 - step
            start, stop = before[step * n], before[(step + 1) * n]
            line = product(slot, most + slot, most + slot) + jnp.where(
                stop > start, running[jnp.clip(stop - 1, 0, most - 1)], 0.0
            )
            out_grad[slot, pl.ds(0, HEAD_DIM), :] = (
                line * (distill_weight * HEAD_DIM ** (-0.5))
            ).astype(jnp.bfloat16)
            out_grad[slot, pl.ds(HEAD_DIM, NOTE_ROWS), :] = note

            @pl.when(slot > 0)
            def send_grad():
                grad_copy(slot, place(slot)).start()

            return carry

        repeat(n, finish)
        in_grad[head] = out_grad[0]
        drain_queries()
        take_grads(True)

        def drain_grads(step, carry):
            grad_copy(step + 1, place(step + 1)).wait_send()
            return carry

        repeat(n - 1, drain_grads)


def unpack(in_grad, grad_ref, div_ref):
    heads = in_grad.shape[0]
    group = LANES // HEAD_DIM
    for pair in range(heads // group):
        both = jnp.concatenate(
            [in_grad[pair * group + inner, pl.ds(0, HEAD_DIM), :] for inner in range(group)], axis=0
        )
        grad_ref[:, pl.ds(pair * LANES, LANES)] = both.T
    div_lane = lax.broadcasted_iota(jnp.int32, (1, LANES), 1)
    div_row = jnp.zeros((1, LANES), jnp.float32)
    for slot in range(heads):
        note = in_grad[slot, pl.ds(HEAD_DIM, NOTE_ROWS), :].astype(jnp.float32)
        div_row = jnp.where(div_lane == slot, jnp.sum(note, axis=0, keepdims=True), div_row)
    div_ref[...] = div_row[:, :heads]


def per_device(n, teacher_q, student_q, owner_table):
    rows, width = teacher_q.shape
    heads = width // HEAD_DIM
    owned = n // heads
    most = 2 * (n * owned - n)
    entries = most + n
    keep = entries * 2 * rows * rows * 4 <= KEEP_BYTES
    hbm = pl.BlockSpec(memory_space=pl.ANY)
    message = HEAD_DIM + NOTE_ROWS
    packed = pl.pallas_call(
        functools.partial(kernel, n, most, keep),
        out_shape=pltpu.VMEM((heads, message, rows), jnp.bfloat16),
        in_specs=[hbm, hbm, hbm],
        out_specs=pl.BlockSpec(memory_space=pltpu.VMEM),
        scratch_shapes=[
            pltpu.VMEM((rows, width), jnp.bfloat16),
            pltpu.VMEM((rows, width), jnp.bfloat16),
            pltpu.VMEM((heads, rows, LANES), jnp.bfloat16),
            pltpu.VMEM((n, rows, LANES), jnp.bfloat16),
            pltpu.VMEM((n, 2 * rows, LANES), jnp.bfloat16),
            pltpu.VMEM((n, HEAD_DIM, rows), jnp.bfloat16),
            pltpu.SMEM((n, n), jnp.int32),
            pltpu.SMEM((n * n + 1,), jnp.int32),
            pltpu.SMEM((n * n + 2,), jnp.int32),
            pltpu.SMEM((most,), jnp.int32),
            pltpu.SMEM((most,), jnp.int32),
            pltpu.SMEM((most,), jnp.int32),
            pltpu.SMEM((most,), jnp.int32),
            pltpu.VMEM((entries, rows), jnp.int32),
            pltpu.VMEM((5, entries, rows), jnp.float32),
            pltpu.VMEM((2, entries, rows), jnp.float32),
            pltpu.VMEM((entries if keep else 1, 2, rows, rows), jnp.float32),
            pltpu.VMEM((entries, rows, rows), jnp.bfloat16),
            pltpu.VMEM((most, HEAD_DIM, rows), jnp.float32),
            pltpu.VMEM((8, LANES), jnp.float32),
            pltpu.VMEM((n, message, rows), jnp.bfloat16),
            pltpu.SemaphoreType.DMA((2,)),
            pltpu.SemaphoreType.DMA,
            pltpu.SemaphoreType.DMA((heads,)),
            pltpu.SemaphoreType.DMA((n,)),
            pltpu.SemaphoreType.DMA((n,)),
            pltpu.SemaphoreType.DMA((heads,)),
        ],
        compiler_params=pltpu.CompilerParams(
            collective_id=0, has_side_effects=True, vmem_limit_bytes=60 * 1024 * 1024
        ),
        name="distill",
    )(*[pltpu.with_memory_space_constraint(x, pltpu.HBM) for x in (teacher_q, student_q, owner_table)])
    grad, divergence = pl.pallas_call(
        unpack,
        out_shape=(
            jax.ShapeDtypeStruct((rows, width), jnp.bfloat16),
            jax.ShapeDtypeStruct((1, heads), jnp.float32),
        ),
        in_specs=[pl.BlockSpec(memory_space=pltpu.VMEM)],
        out_specs=(pl.BlockSpec(memory_space=pltpu.VMEM),) * 2,
        compiler_params=pltpu.CompilerParams(vmem_limit_bytes=4 * 1024 * 1024),
        name="unpack",
    )(packed)
    return (grad, divergence.reshape(heads))


def solution(mesh):
    placed = (P("tok", "head"), P("tok", "head"), P())
    return jax.shard_map(
        functools.partial(per_device, mesh.shape["tok"]),
        mesh=mesh,
        in_specs=placed,
        out_specs=(P("tok", "head"), P("head")),
        check_vma=False,
    )
```

```python
import functools
import math

import jax
import jax.numpy as jnp
from jax import lax
from jax.experimental import pallas as pl
from jax.experimental.pallas import tpu as pltpu
from jax.sharding import PartitionSpec as P

HEAD_DIM = 64
LANES = 128
NOTE_ROWS = 16
KEEP_BYTES = 16 * 1024 * 1024
floor_value = -3e38
distill_weight = 32.0
score_factor = HEAD_DIM ** (-0.5) * math.log2(math.e)
MESH = pl.DeviceIdType.MESH


def repeat(count, body, init=None):
    if count <= 16:
        for step in range(count):
            init = body(step, init)
        return init
    return lax.fori_loop(0, count, body, init)


def kernel(
    n, most, keep, teacher_hbm, student_hbm, table_hbm, in_grad,
    teacher, student, outbox, inbox, turned, table, following, edge_of,
    edge_row, edge_col, edge_tag, stats, peaks, inverses, weights, exps, shares,
    out_grad, load_sem, table_sem, send_sem, recv_sem, back_send, back_recv,
):
    rows, width = teacher_hbm.shape
    pairs = width // LANES
    heads = width // HEAD_DIM
    group = LANES // HEAD_DIM
    parts = n // heads
    chips = n // 2
    side = math.isqrt(chips)
    side = side if side * side == chips else 1
    span = chips // side
    me = lax.axis_index("tok")
    head_at = lax.axis_index("head")
    chip, core = me // 2, me % 2
    head = me // parts
    is_worker = me % parts == 0

    def place(step):
        shift, flip = step // 2, step % 2
        high = (chip // span + shift // span) % side
        low = (chip % span + shift % span) % span
        return (high * span + low) * 2 + (core + flip) % 2

    def place_in(worker):
        worker_chip = worker // 2
        high = (chip // span - worker_chip // span + side) % side
        low = (chip % span - worker_chip % span + span) % span
        return (high * span + low) * 2 + (core - worker % 2 + 2) % 2

    def remote(src, dst, send, recv, target):
        return pltpu.make_async_remote_copy(
            src_ref=src, dst_ref=dst, send_sem=send, recv_sem=recv,
            device_id=(head_at, target), device_id_type=MESH,
        )

    barrier = pltpu.get_barrier_semaphore()
    loads = [
        pltpu.make_async_copy(teacher_hbm, teacher, load_sem.at[0]),
        pltpu.make_async_copy(student_hbm, student, load_sem.at[1]),
    ]
    for load in loads:
        load.start()
    table_load = pltpu.make_async_copy(table_hbm, table, table_sem)
    table_load.start()

    def greet(target):
        pl.semaphore_signal(barrier, inc=1, device_id=(head_at, target), device_id_type=MESH)

    @pl.when(is_worker)
    def greet_all():
        def greet_one(step, carry):
            greet(place(n - 1 - step))
            return carry

        repeat(n - 1, greet_one)

    @pl.when(jnp.logical_not(is_worker))
    def greet_workers():
        for step in range(heads):
            greet((head + heads - 1 - step) % heads * parts)

    for load in loads:
        load.wait()
    lane = lax.broadcasted_iota(jnp.int32, (rows, LANES), 1)
    lower = lane < HEAD_DIM
    for pair in range(pairs):
        columns = pl.ds(pair * LANES, LANES)
        t_pair = teacher[:, columns].astype(jnp.float32)
        s_pair = student[:, columns].astype(jnp.float32)
        outbox[pair * group] = jnp.where(lower, t_pair, pltpu.roll(s_pair, HEAD_DIM, 1)).astype(
            jnp.bfloat16
        )
        outbox[pair * group + 1] = jnp.where(
            lower, pltpu.roll(t_pair, HEAD_DIM, 1), s_pair
        ).astype(jnp.bfloat16)

    def query_copy(to_head, slot):
        return remote(
            outbox.at[to_head], inbox.at[slot], send_sem.at[to_head], recv_sem.at[slot],
            to_head * parts,
        )

    def send_queries():
        for step in range(heads - 1, 0, -1):
            to_head = (head + step) % heads
            query_copy(to_head, place_in(to_head * parts)).start()

    def drain_queries():
        for step in range(heads - 1, 0, -1):
            query_copy((head + step) % heads, 0).wait_send()

    def grad_copy(slot, target):
        return remote(
            out_grad.at[slot], in_grad.at[head], back_send.at[slot], back_recv.at[head], target
        )

    def take_grads(own):
        for step in range(heads):
            from_head = (head + step) % heads
            if step == 0 and own:
                continue
            remote(
                out_grad.at[0], in_grad.at[from_head], back_send.at[0], back_recv.at[from_head],
                from_head * parts,
            ).wait_recv()

    @pl.when(jnp.logical_not(is_worker))
    def serve():
        pl.semaphore_wait(barrier, heads)
        send_queries()
        query_copy(head, place_in(head * parts)).start()
        drain_queries()
        query_copy(head, 0).wait_send()
        table_load.wait()
        take_grads(False)

    @pl.when(is_worker)
    def work():
        inbox[0] = outbox[head]
        pl.semaphore_wait(barrier, n - 1)
        send_queries()
        table_load.wait()
        codes = n * n
        blank = most
        own = most + 1

        def count_row(row, count):
            row_at = place(row)

            def count_cell(col, count):
                inside = table[row_at, place(col)] >= 0
                edge = jnp.minimum(2 * count, most - 2)
                edge_of[row * n + col] = jnp.where(inside, edge, blank)
                edge_of[col * n + row] = jnp.where(inside, edge + 1, blank)
                return count + jnp.where(inside, 1, 0)

            return lower_cells(row, count_cell, count)

        def lower_cells(row, body, init):
            if isinstance(row, int):
                for col in range(row):
                    init = body(col, init)
                return init
            return lax.fori_loop(0, row, body, init)

        repeat(n, count_row, jnp.int32(0))
        following[codes] = jnp.int32(codes)
        following[codes + 1] = jnp.int32(codes)

        def link_row(step, after):
            row = n - 1 - step
            row_at = place(row)
            following[row * n + row] = after

            def link_cell(back, after):
                col = row - 1 - back
                code = row * n + col
                after = jnp.where(table[row_at, place(col)] >= 0, code, after)
                following[code] = after
                return after

            return lower_cells(row, link_cell, after)

        repeat(n, link_row, jnp.int32(codes))

        def list_pair(pair, code):
            code = following[code]
            held = jnp.minimum(code, codes - 1)
            high, low = held // n, held % n
            edge_row[2 * pair] = high
            edge_col[2 * pair] = low
            edge_tag[2 * pair] = jnp.where(code < codes, high, -1)
            edge_row[2 * pair + 1] = low
            edge_col[2 * pair + 1] = high
            edge_tag[2 * pair + 1] = jnp.where(code < codes, low, -1)
            return code + 1

        repeat(most // 2, list_pair, jnp.int32(0))
        shares[blank] = jnp.zeros((HEAD_DIM, rows), jnp.float32)

        none = jnp.zeros((), jnp.bfloat16)

        def scores(col, row):
            block = inbox[col]
            masked = jnp.concatenate(
                [jnp.where(lower, block, none), jnp.where(lower, none, block)], axis=0
            )
            raw = lax.dot_general(
                masked, inbox[row], (((1,), (1,)), ((), ())), preferred_element_type=jnp.float32
            )
            return raw[:rows], raw[rows:]

        def measure(entry, col, row):
            t_raw, s_raw = scores(col, row)
            t_top = jnp.max(t_raw, axis=0, keepdims=True)
            s_top = jnp.max(s_raw, axis=0, keepdims=True)
            t_exp = jnp.exp2((t_raw - t_top) * score_factor)
            s_exp = jnp.exp2((s_raw - s_top) * score_factor)
            at = pl.ds(entry, 1)
            stats[0, at, :] = t_top
            stats[1, at, :] = s_top
            stats[2, at, :] = jnp.sum(t_exp, axis=0, keepdims=True)
            stats[3, at, :] = jnp.sum(s_exp, axis=0, keepdims=True)
            stats[4, at, :] = jnp.sum(t_exp * (t_raw - s_raw), axis=0, keepdims=True)
            if keep:
                exps[entry, 0] = t_exp
                exps[entry, 1] = s_exp

        def take_chip(shift, carry):
            for inner in range(2):
                slot = 2 * shift + inner

                @pl.when(slot > 0)
                def wait_block():
                    remote(
                        outbox.at[0], inbox.at[slot], send_sem.at[0], recv_sem.at[slot], place(slot)
                    ).wait_recv()

            for inner in range(2):
                slot = 2 * shift + inner
                turned[slot] = inbox[slot].T[HEAD_DIM:]
                measure(own + slot, slot, slot)
            return carry

        repeat(chips, take_chip)

        def measure_edge(edge, carry):
            measure(edge, edge_col[edge], edge_row[edge])
            return carry

        repeat(most, measure_edge)

        every = pl.ds(own, n)
        slot_row = lax.broadcasted_iota(jnp.int32, (n, rows), 0)

        def raise_peaks(edge, carry):
            mine = slot_row == edge_tag[edge]
            at = pl.ds(edge, 1)
            return tuple(
                jnp.maximum(peak, jnp.where(mine, stats[which, at, :], floor_value))
                for which, peak in enumerate(carry)
            )

        tops = repeat(most, raise_peaks, (stats[0, every, :], stats[1, every, :]))
        for which in range(2):
            peaks[which] = tops[which]

        def scaled(which, at):
            return [stats[2 + which, at, :]] + ([stats[4, at, :]] if which == 0 else [])

        parts_own = [
            jnp.exp2((stats[which, every, :] - tops[which]) * score_factor) for which in range(2)
        ]
        sums = tuple(
            parts_own[which] * amount for which in range(2) for amount in scaled(which, every)
        )

        def add_edge(edge, carry):
            tag = edge_tag[edge]
            mine = slot_row == tag
            at = pl.ds(edge, 1)
            fresh = []
            for which in range(2):
                peak = peaks[which, pl.ds(jnp.maximum(tag, 0), 1), :]
                part = jnp.exp2(jnp.minimum((stats[which, at, :] - peak) * score_factor, 0.0))
                weights[which, at, :] = part
                fresh += [part * amount for amount in scaled(which, at)]
            return tuple(
                total + jnp.where(mine, piece, 0.0)
                for total, piece in zip(carry, fresh, strict=True)
            )

        t_sum, cross, s_sum = repeat(most, add_edge, sums)
        t_inverse, s_inverse = 1.0 / t_sum, 1.0 / s_sum
        inverses[0] = t_inverse
        inverses[1] = s_inverse
        weights[0, every, :] = parts_own[0] * t_inverse
        weights[1, every, :] = parts_own[1] * s_inverse

        def weigh_edge(edge, carry):
            tag = edge_tag[edge]
            at, mine_at = pl.ds(edge, 1), pl.ds(jnp.maximum(tag, 0), 1)
            valid = jnp.where(tag >= 0, 1.0, 0.0)
            for which in range(2):
                weights[which, at, :] = weights[which, at, :] * (
                    inverses[which, mine_at, :] * valid
                )
            return carry

        repeat(most, weigh_edge)
        total = (
            (cross * t_inverse - tops[0] + tops[1]) * score_factor
            - jnp.log2(t_sum)
            + jnp.log2(s_sum)
        )
        total = jnp.sum(jnp.sum(total, axis=0, keepdims=True), axis=1, keepdims=True) * (
            math.log(2.0) / (rows * n)
        )
        first = total.astype(jnp.bfloat16).astype(jnp.float32)
        second = (total - first).astype(jnp.bfloat16).astype(jnp.float32)
        note_row = lax.broadcasted_iota(jnp.int32, (NOTE_ROWS, LANES), 0)
        note = jnp.where(
            note_row == 0,
            first,
            jnp.where(
                note_row == 1, second, jnp.where(note_row == 2, total - first - second, 0.0)
            ),
        ).astype(jnp.bfloat16)

        def gap_of(entry, col, row):
            at = pl.ds(entry, 1)
            if keep:
                t_exp, s_exp = exps[entry, 0], exps[entry, 1]
            else:
                t_raw, s_raw = scores(col, row)
                t_exp = jnp.exp2((t_raw - stats[0, at, :]) * score_factor)
                s_exp = jnp.exp2((s_raw - stats[1, at, :]) * score_factor)
            return (s_exp * weights[1, at, :] - t_exp * weights[0, at, :]).astype(jnp.bfloat16)

        def product(query, gap, back):
            return jnp.dot(query, gap, preferred_element_type=jnp.float32) + lax.dot_general(
                query, back, (((1,), (1,)), ((), ())), preferred_element_type=jnp.float32
            )

        def share_pair(pair, carry):
            high, low = edge_row[2 * pair], edge_col[2 * pair]
            gap = gap_of(2 * pair, low, high)
            back = gap_of(2 * pair + 1, high, low)
            shares[2 * pair] = product(turned[low], gap, back)
            shares[2 * pair + 1] = product(turned[high], back, gap)
            return carry

        def share_own(slot, carry):
            gap = gap_of(own + slot, slot, slot)
            shares[own + slot] = product(turned[slot], gap, gap)
            return carry

        repeat(n, share_own)
        repeat(most // 2, share_pair)

        def finish(step, carry):
            slot = n - 1 - step

            def add_share(turn, line):
                return line + shares[edge_of[slot * n + (slot + turn + 1) % n]]

            line = repeat(n - 1, add_share, shares[own + slot])
            out_grad[slot, pl.ds(0, HEAD_DIM), :] = (
                line * (distill_weight * HEAD_DIM ** (-0.5))
            ).astype(jnp.bfloat16)
            out_grad[slot, pl.ds(HEAD_DIM, NOTE_ROWS), :] = note

            @pl.when(slot > 0)
            def send_grad():
                grad_copy(slot, place(slot)).start()

            return carry

        repeat(n, finish)
        in_grad[head] = out_grad[0]
        drain_queries()
        take_grads(True)

        def drain_grads(step, carry):
            grad_copy(step + 1, place(step + 1)).wait_send()
            return carry

        repeat(n - 1, drain_grads)


def unpack(in_grad, grad_ref, div_ref):
    heads = in_grad.shape[0]
    group = LANES // HEAD_DIM
    for pair in range(heads // group):
        both = jnp.concatenate(
            [in_grad[pair * group + inner, pl.ds(0, HEAD_DIM), :] for inner in range(group)], axis=0
        )
        grad_ref[:, pl.ds(pair * LANES, LANES)] = both.T
    div_lane = lax.broadcasted_iota(jnp.int32, (1, LANES), 1)
    div_row = jnp.zeros((1, LANES), jnp.float32)
    for slot in range(heads):
        note = in_grad[slot, pl.ds(HEAD_DIM, NOTE_ROWS), :].astype(jnp.float32)
        div_row = jnp.where(div_lane == slot, jnp.sum(note, axis=0, keepdims=True), div_row)
    div_ref[...] = div_row[:, :heads]


def per_device(n, teacher_q, student_q, owner_table):
    rows, width = teacher_q.shape
    heads = width // HEAD_DIM
    owned = n // heads
    most = 2 * (n * owned - n)
    entries = most + 1 + n
    keep = entries * 2 * rows * rows * 4 <= KEEP_BYTES
    hbm = pl.BlockSpec(memory_space=pl.ANY)
    message = HEAD_DIM + NOTE_ROWS
    packed = pl.pallas_call(
        functools.partial(kernel, n, most, keep),
        out_shape=pltpu.VMEM((heads, message, rows), jnp.bfloat16),
        in_specs=[hbm, hbm, hbm],
        out_specs=pl.BlockSpec(memory_space=pltpu.VMEM),
        scratch_shapes=[
            pltpu.VMEM((rows, width), jnp.bfloat16),
            pltpu.VMEM((rows, width), jnp.bfloat16),
            pltpu.VMEM((heads, rows, LANES), jnp.bfloat16),
            pltpu.VMEM((n, rows, LANES), jnp.bfloat16),
            pltpu.VMEM((n, HEAD_DIM, rows), jnp.bfloat16),
            pltpu.SMEM((n, n), jnp.int32),
            pltpu.SMEM((n * n + 2,), jnp.int32),
            pltpu.SMEM((n * n,), jnp.int32),
            pltpu.SMEM((most,), jnp.int32),
            pltpu.SMEM((most,), jnp.int32),
            pltpu.SMEM((most,), jnp.int32),
            pltpu.VMEM((5, entries, rows), jnp.float32),
            pltpu.VMEM((2, n, rows), jnp.float32),
            pltpu.VMEM((2, n, rows), jnp.float32),
            pltpu.VMEM((2, entries, rows), jnp.float32),
            pltpu.VMEM((entries if keep else 1, 2, rows, rows), jnp.float32),
            pltpu.VMEM((entries, HEAD_DIM, rows), jnp.float32),
            pltpu.VMEM((n, message, rows), jnp.bfloat16),
            pltpu.SemaphoreType.DMA((2,)),
            pltpu.SemaphoreType.DMA,
            pltpu.SemaphoreType.DMA((heads,)),
            pltpu.SemaphoreType.DMA((n,)),
            pltpu.SemaphoreType.DMA((n,)),
            pltpu.SemaphoreType.DMA((heads,)),
        ],
        compiler_params=pltpu.CompilerParams(
            collective_id=0, has_side_effects=True, vmem_limit_bytes=60 * 1024 * 1024
        ),
        name="distill",
    )(*[pltpu.with_memory_space_constraint(x, pltpu.HBM) for x in (teacher_q, student_q, owner_table)])
    grad, divergence = pl.pallas_call(
        unpack,
        out_shape=(
            jax.ShapeDtypeStruct((rows, width), jnp.bfloat16),
            jax.ShapeDtypeStruct((1, heads), jnp.float32),
        ),
        in_specs=[pl.BlockSpec(memory_space=pltpu.VMEM)],
        out_specs=(pl.BlockSpec(memory_space=pltpu.VMEM),) * 2,
        compiler_params=pltpu.CompilerParams(vmem_limit_bytes=4 * 1024 * 1024),
        name="unpack",
    )(packed)
    return (grad, divergence.reshape(heads))


def solution(mesh):
    placed = (P("tok", "head"), P("tok", "head"), P())
    return jax.shard_map(
        functools.partial(per_device, mesh.shape["tok"]),
        mesh=mesh,
        in_specs=placed,
        out_specs=(P("tok", "head"), P("head")),
        check_vma=False,
    )
```

```python
import functools
import math

import jax
import jax.numpy as jnp
from jax import lax
from jax.experimental import pallas as pl
from jax.experimental.pallas import tpu as pltpu
from jax.sharding import PartitionSpec as P

HEAD_DIM = 64
LANES = 128
NOTE_ROWS = 16
KEEP_BYTES = 16 * 1024 * 1024
floor_value = -3e38
distill_weight = 32.0
score_factor = HEAD_DIM ** (-0.5) * math.log2(math.e)
MESH = pl.DeviceIdType.MESH


def repeat(count, body, init=None):
    if count <= 16:
        for step in range(count):
            init = body(step, init)
        return init
    return lax.fori_loop(0, count, body, init)


def kernel(
    n, most, keep, teacher_hbm, student_hbm, table_hbm, grad_out, div_out,
    teacher, student, outbox, own_turned, own_exps, own_stats, inbox, left, turned, arrived,
    table, following, edge_of, edge_row, edge_col, edge_tag,
    stats, peaks, inverses, weights, pieces, exps, shares, out_note, in_note, out_grad, in_grad, near,
    load_sem, table_sem, send_sem, recv_sem, stat_send, stat_recv, note_send, note_recv,
    back_send, back_recv,
):
    rows, width = teacher_hbm.shape
    pairs = width // LANES
    heads = width // HEAD_DIM
    group = LANES // HEAD_DIM
    parts = n // heads
    chips = n // 2
    side = math.isqrt(chips)
    side = side if side * side == chips else 1
    span = chips // side
    me = lax.axis_index("tok")
    head_at = lax.axis_index("head")
    chip, core = me // 2, me % 2
    head = me // parts
    is_worker = me % parts == 0

    def place(step):
        shift, flip = step // 2, step % 2
        high = (chip // span + shift // span) % side
        low = (chip % span + shift % span) % span
        return (high * span + low) * 2 + (core + flip) % 2

    def place_in(worker):
        worker_chip = worker // 2
        high = (chip // span - worker_chip // span + side) % side
        low = (chip % span - worker_chip % span + span) % span
        return (high * span + low) * 2 + (core - worker % 2 + 2) % 2

    def remote(src, dst, send, recv, target):
        return pltpu.make_async_remote_copy(
            src_ref=src, dst_ref=dst, send_sem=send, recv_sem=recv,
            device_id=(head_at, target), device_id_type=MESH,
        )

    barrier = pltpu.get_barrier_semaphore()
    loads = [
        pltpu.make_async_copy(teacher_hbm, teacher, load_sem.at[0]),
        pltpu.make_async_copy(student_hbm, student, load_sem.at[1]),
    ]
    for load in loads:
        load.start()
    table_load = pltpu.make_async_copy(table_hbm, table, table_sem)
    table_load.start()

    def greet(target):
        pl.semaphore_signal(barrier, inc=1, device_id=(head_at, target), device_id_type=MESH)

    @pl.when(is_worker)
    def greet_all():
        def greet_one(step, carry):
            greet(place(n - 1 - step))
            return carry

        repeat(n - 1, greet_one)

    @pl.when(jnp.logical_not(is_worker))
    def greet_workers():
        for step in range(heads):
            greet((head + heads - 1 - step) % heads * parts)

    for load in loads:
        load.wait()
    lane = lax.broadcasted_iota(jnp.int32, (rows, LANES), 1)
    lower = lane < HEAD_DIM
    none = jnp.zeros((), jnp.bfloat16)
    for pair in range(pairs):
        columns = pl.ds(pair * LANES, LANES)
        t_pair = teacher[:, columns].astype(jnp.float32)
        s_pair = student[:, columns].astype(jnp.float32)
        outbox[pair * group] = jnp.where(lower, t_pair, pltpu.roll(s_pair, HEAD_DIM, 1)).astype(
            jnp.bfloat16
        )
        outbox[pair * group + 1] = jnp.where(
            lower, pltpu.roll(t_pair, HEAD_DIM, 1), s_pair
        ).astype(jnp.bfloat16)

    def query_copy(to_head, slot):
        return remote(
            outbox.at[to_head], inbox.at[slot], send_sem.at[to_head], recv_sem.at[slot],
            to_head * parts,
        )

    def stat_copy(to_head, slot):
        return remote(
            own_stats.at[to_head], arrived.at[slot], stat_send.at[to_head], stat_recv.at[slot],
            to_head * parts,
        )

    def grad_copy(slot, target):
        return remote(
            out_grad.at[slot], in_grad.at[head], back_send.at[slot], back_recv.at[head], target
        )

    def note_copy(slot, target):
        return remote(
            out_note.at[slot], in_note.at[head], note_send.at[slot], note_recv.at[head], target
        )

    others = [(head + step) % heads for step in range(heads - 1, 0, -1)]
    pl.semaphore_wait(barrier, jnp.where(is_worker, n - 1, heads))
    for to_head in others:
        query_copy(to_head, place_in(to_head * parts)).start()

    @pl.when(jnp.logical_not(is_worker))
    def send_near():
        query_copy(head, place_in(head * parts)).start()

    def masked(block):
        return jnp.where(lower, block, none), jnp.where(lower, none, block)

    def tile(both, block):
        raw = lax.dot_general(
            both, block, (((1,), (1,)), ((), ())), preferred_element_type=jnp.float32
        )
        return raw[:rows], raw[rows:]

    def measured(t_raw, s_raw):
        t_top = jnp.max(t_raw, axis=0, keepdims=True)
        s_top = jnp.max(s_raw, axis=0, keepdims=True)
        t_exp = jnp.exp2((t_raw - t_top) * score_factor)
        s_exp = jnp.exp2((s_raw - s_top) * score_factor)
        lines = (
            t_top,
            s_top,
            jnp.sum(t_exp, axis=0, keepdims=True),
            jnp.sum(s_exp, axis=0, keepdims=True),
            jnp.sum(t_exp * (t_raw - s_raw), axis=0, keepdims=True),
        )
        return t_exp, s_exp, lines

    for turn in range(heads):
        block = outbox[turn]
        own_turned[turn] = block.T[HEAD_DIM:]
        t_exp, s_exp, lines = measured(*tile(jnp.concatenate(masked(block), axis=0), block))
        own_exps[turn, 0] = t_exp
        own_exps[turn, 1] = s_exp
        for line_at, line in enumerate(lines):
            own_stats[turn, pl.ds(line_at, 1), :] = line
        own_stats[turn, pl.ds(len(lines), 8 - len(lines)), :] = jnp.zeros(
            (8 - len(lines), rows), jnp.float32
        )
    for to_head in others:
        stat_copy(to_head, place_in(to_head * parts)).start()
    table_load.wait()

    @pl.when(jnp.logical_not(is_worker))
    def send_near_stats():
        stat_copy(head, place_in(head * parts)).start()

    @pl.when(is_worker)
    def work():
        inbox[0] = outbox[head]
        arrived[0] = own_stats[head]
        codes = n * n
        blank = most

        def lower_cells(row, body, init):
            if isinstance(row, int):
                for col in range(row):
                    init = body(col, init)
                return init
            return lax.fori_loop(0, row, body, init)

        def count_row(row, count):
            row_at = place(row)

            def count_cell(col, count):
                inside = table[row_at, place(col)] >= 0
                edge = jnp.minimum(2 * count, most - 2)
                edge_of[row * n + col] = jnp.where(inside, edge, blank)
                edge_of[col * n + row] = jnp.where(inside, edge + 1, blank)
                return count + jnp.where(inside, 1, 0)

            return lower_cells(row, count_cell, count)

        repeat(n, count_row, jnp.int32(0))
        following[codes] = jnp.int32(codes)
        following[codes + 1] = jnp.int32(codes)

        def link_row(step, after):
            row = n - 1 - step
            row_at = place(row)
            following[row * n + row] = after

            def link_cell(back, after):
                col = row - 1 - back
                code = row * n + col
                after = jnp.where(table[row_at, place(col)] >= 0, code, after)
                following[code] = after
                return after

            return lower_cells(row, link_cell, after)

        repeat(n, link_row, jnp.int32(codes))

        def list_pair(pair, code):
            code = following[code]
            held = jnp.minimum(code, codes - 1)
            high, low = held // n, held % n
            edge_row[2 * pair] = high
            edge_col[2 * pair] = low
            edge_tag[2 * pair] = jnp.where(code < codes, high, -1)
            edge_row[2 * pair + 1] = low
            edge_col[2 * pair + 1] = high
            edge_tag[2 * pair + 1] = jnp.where(code < codes, low, -1)
            return code + 1

        repeat(most // 2, list_pair, jnp.int32(0))
        shares[blank] = jnp.zeros((HEAD_DIM, rows), jnp.float32)

        def take_block(slot, carry):
            @pl.when(slot > 0)
            def wait_block():
                remote(
                    outbox.at[0], inbox.at[slot], send_sem.at[0], recv_sem.at[slot], place(slot)
                ).wait_recv()

            return carry

        def keep_block(slot, carry):
            block = inbox[slot]
            t_part, s_part = masked(block)
            left[slot, pl.ds(0, rows), :] = t_part
            left[slot, pl.ds(rows, rows), :] = s_part
            turned[slot] = block.T[HEAD_DIM:]
            return carry

        def take_chip(shift, carry):
            for inner in range(2):
                take_block(2 * shift + inner, None)
            for inner in range(2):
                keep_block(2 * shift + inner, None)
            return carry

        repeat(chips, take_chip)

        def measure_edge(edge, carry):
            t_exp, s_exp, lines = measured(*tile(left[edge_col[edge]], inbox[edge_row[edge]]))
            for line_at, line in enumerate(lines):
                stats[line_at, pl.ds(edge, 1), :] = line
            if keep:
                exps[edge, 0] = t_exp
                exps[edge, 1] = s_exp
            return carry

        repeat(most, measure_edge)

        def take_stats(step, carry):
            slot = step + 1
            remote(
                own_stats.at[0], arrived.at[slot], stat_send.at[0], stat_recv.at[slot], place(slot)
            ).wait_recv()
            return carry

        repeat(n - 1, take_stats)
        slot_row = lax.broadcasted_iota(jnp.int32, (n, rows), 0)

        def place_stats(slot, carry):
            return tuple(
                jnp.where(slot_row == slot, arrived[slot, pl.ds(line_at, 1), :], line)
                for line_at, line in enumerate(carry)
            )

        blank_lines = jnp.zeros((n, rows), jnp.float32)
        first_stats = repeat(n, place_stats, (blank_lines,) * 5)

        def raise_peaks(edge, carry):
            mine = slot_row == edge_tag[edge]
            at = pl.ds(edge, 1)
            return tuple(
                jnp.maximum(peak, jnp.where(mine, stats[which, at, :], floor_value))
                for which, peak in enumerate(carry)
            )

        tops = repeat(most, raise_peaks, first_stats[:2])
        for which in range(2):
            peaks[which] = tops[which]
        first_parts = [
            jnp.exp2((first_stats[which] - tops[which]) * score_factor) for which in range(2)
        ]
        sums = (
            first_parts[0] * first_stats[2],
            first_parts[0] * first_stats[4],
            first_parts[1] * first_stats[3],
        )

        def add_edge(edge, carry):
            tag = edge_tag[edge]
            mine = slot_row == tag
            at = pl.ds(edge, 1)
            fresh = []
            for which in range(2):
                peak = peaks[which, pl.ds(jnp.maximum(tag, 0), 1), :]
                part = jnp.exp2(jnp.minimum((stats[which, at, :] - peak) * score_factor, 0.0))
                weights[which, at, :] = part
                fresh.append(part * stats[2 + which, at, :])
                if which == 0:
                    fresh.append(part * stats[4, at, :])
            return tuple(
                total + jnp.where(mine, piece, 0.0)
                for total, piece in zip(carry, fresh, strict=True)
            )

        t_sum, cross, s_sum = repeat(most, add_edge, sums)
        t_inverse, s_inverse = 1.0 / t_sum, 1.0 / s_sum
        inverses[0] = t_inverse
        inverses[1] = s_inverse

        def weigh_edge(edge, carry):
            tag = edge_tag[edge]
            at, mine_at = pl.ds(edge, 1), pl.ds(jnp.maximum(tag, 0), 1)
            valid = jnp.where(tag >= 0, 1.0, 0.0)
            for which in range(2):
                weights[which, at, :] = weights[which, at, :] * (
                    inverses[which, mine_at, :] * valid
                )
            return carry

        repeat(most, weigh_edge)

        def split(value):
            first = value.astype(jnp.bfloat16).astype(jnp.float32)
            second = (value - first).astype(jnp.bfloat16).astype(jnp.float32)
            return [first, second, value - first - second]

        for which in range(2):
            for at, piece in enumerate(split(first_parts[which] * inverses[which])):
                pieces[3 * which + at] = piece
        total = (
            (cross * t_inverse - tops[0] + tops[1]) * score_factor
            - jnp.log2(t_sum)
            + jnp.log2(s_sum)
        )
        total = jnp.sum(jnp.sum(total, axis=0, keepdims=True), axis=1, keepdims=True) * (
            math.log(2.0) / (rows * n)
        )
        note_row = lax.broadcasted_iota(jnp.int32, (NOTE_ROWS, LANES), 0)
        base = jnp.zeros((NOTE_ROWS, LANES), jnp.float32)
        for at, piece in enumerate(split(total)):
            base = jnp.where(note_row == at, piece, base)

        def send_note(step, carry):
            slot = n - 1 - step
            note = base
            for at in range(6):
                note = jnp.where(note_row == 3 + at, pieces[at, pl.ds(slot, 1), :], note)
            out_note[slot] = note.astype(jnp.bfloat16)

            @pl.when(slot > 0)
            def start_note():
                note_copy(slot, place(slot)).start()

            return carry

        repeat(n, send_note)

        def gap_of(edge, col, row):
            at = pl.ds(edge, 1)
            if keep:
                t_exp, s_exp = exps[edge, 0], exps[edge, 1]
            else:
                t_raw, s_raw = tile(left[col], inbox[row])
                t_exp = jnp.exp2((t_raw - stats[0, at, :]) * score_factor)
                s_exp = jnp.exp2((s_raw - stats[1, at, :]) * score_factor)
            return s_exp * weights[1, at, :] - t_exp * weights[0, at, :]

        def share_pair(pair, carry):
            high, low = edge_row[2 * pair], edge_col[2 * pair]
            gap = gap_of(2 * pair, low, high)
            back = gap_of(2 * pair + 1, high, low)
            symmetric = (gap + back.T).astype(jnp.bfloat16)
            shares[2 * pair] = jnp.dot(turned[low], symmetric, preferred_element_type=jnp.float32)
            shares[2 * pair + 1] = lax.dot_general(
                turned[high], symmetric, (((1,), (1,)), ((), ())),
                preferred_element_type=jnp.float32,
            )
            return carry

        repeat(most // 2, share_pair)

        def finish(step, carry):
            slot = n - 1 - step

            def add_share(turn, line):
                fresh = shares[edge_of[slot * n + (slot + turn + 1) % n]]
                return fresh if line is None else line + fresh

            line = repeat(n - 1, add_share, None if n <= 16 else jnp.zeros((HEAD_DIM, rows), jnp.float32))
            out_grad[slot] = (line * (distill_weight * HEAD_DIM ** (-0.5))).astype(jnp.bfloat16)

            @pl.when(slot > 0)
            def send_grad():
                grad_copy(slot, place(slot)).start()

            return carry

        repeat(n, finish)
        in_note[head] = out_note[0]
        in_grad[head] = out_grad[0]

    def take(kind, sends, receives, buffers, step):
        from_head = (head + step) % heads

        def take_one():
            remote(
                kind.at[0], buffers.at[from_head], sends.at[0], receives.at[from_head],
                from_head * parts,
            ).wait_recv()

        if step == 0:
            pl.when(jnp.logical_not(is_worker))(take_one)
        else:
            take_one()
        return from_head

    for step in range(heads):
        take(out_note, note_send, note_recv, in_note, step)
    for turn in range(heads):
        note = in_note[turn].astype(jnp.float32)
        t_weight = note[3:4] + note[4:5] + note[5:6]
        s_weight = note[6:7] + note[7:8] + note[8:9]
        gap = own_exps[turn, 1] * s_weight - own_exps[turn, 0] * t_weight
        symmetric = (gap + gap.T).astype(jnp.bfloat16)
        near[turn] = jnp.dot(own_turned[turn], symmetric, preferred_element_type=jnp.float32) * (
            distill_weight * HEAD_DIM ** (-0.5)
        )
        div_out[pl.ds(turn, 1), :] = note[0:1] + note[1:2] + note[2:3]
    for step in range(heads):
        from_head = take(out_grad, back_send, back_recv, in_grad, step)
        grad_out[from_head] = (in_grad[from_head].astype(jnp.float32) + near[from_head]).astype(
            jnp.bfloat16
        )

    for to_head in others:
        query_copy(to_head, 0).wait_send()
        stat_copy(to_head, 0).wait_send()

    @pl.when(jnp.logical_not(is_worker))
    def drain_near():
        query_copy(head, 0).wait_send()
        stat_copy(head, 0).wait_send()

    @pl.when(is_worker)
    def drain_back():
        def drain_grads(step, carry):
            note_copy(step + 1, place(step + 1)).wait_send()
            grad_copy(step + 1, place(step + 1)).wait_send()
            return carry

        repeat(n - 1, drain_grads)


def unpack(in_grad, in_div, grad_ref, div_ref):
    heads = in_grad.shape[0]
    group = LANES // HEAD_DIM
    for pair in range(heads // group):
        both = jnp.concatenate([in_grad[pair * group + inner] for inner in range(group)], axis=0)
        grad_ref[:, pl.ds(pair * LANES, LANES)] = both.T
    div_lane = lax.broadcasted_iota(jnp.int32, (1, LANES), 1)
    div_row = jnp.zeros((1, LANES), jnp.float32)
    for slot in range(heads):
        div_row = jnp.where(div_lane == slot, in_div[pl.ds(slot, 1), :], div_row)
    div_ref[...] = div_row[:, :heads]


def per_device(n, teacher_q, student_q, owner_table):
    rows, width = teacher_q.shape
    heads = width // HEAD_DIM
    owned = n // heads
    most = 2 * (n * owned - n)
    keep = most * 2 * rows * rows * 4 <= KEEP_BYTES
    hbm = pl.BlockSpec(memory_space=pl.ANY)
    vmem = pl.BlockSpec(memory_space=pltpu.VMEM)
    packed = pl.pallas_call(
        functools.partial(kernel, n, most, keep),
        out_shape=(
            pltpu.VMEM((heads, HEAD_DIM, rows), jnp.bfloat16),
            pltpu.VMEM((heads, rows), jnp.float32),
        ),
        in_specs=[hbm, hbm, hbm],
        out_specs=(vmem, vmem),
        scratch_shapes=[
            pltpu.VMEM((rows, width), jnp.bfloat16),
            pltpu.VMEM((rows, width), jnp.bfloat16),
            pltpu.VMEM((heads, rows, LANES), jnp.bfloat16),
            pltpu.VMEM((heads, HEAD_DIM, rows), jnp.bfloat16),
            pltpu.VMEM((heads, 2, rows, rows), jnp.float32),
            pltpu.VMEM((heads, 8, rows), jnp.float32),
            pltpu.VMEM((n, rows, LANES), jnp.bfloat16),
            pltpu.VMEM((n, 2 * rows, LANES), jnp.bfloat16),
            pltpu.VMEM((n, HEAD_DIM, rows), jnp.bfloat16),
            pltpu.VMEM((n, 8, rows), jnp.float32),
            pltpu.SMEM((n, n), jnp.int32),
            pltpu.SMEM((n * n + 2,), jnp.int32),
            pltpu.SMEM((n * n,), jnp.int32),
            pltpu.SMEM((most,), jnp.int32),
            pltpu.SMEM((most,), jnp.int32),
            pltpu.SMEM((most,), jnp.int32),
            pltpu.VMEM((5, most, rows), jnp.float32),
            pltpu.VMEM((2, n, rows), jnp.float32),
            pltpu.VMEM((2, n, rows), jnp.float32),
            pltpu.VMEM((2, most, rows), jnp.float32),
            pltpu.VMEM((6, n, rows), jnp.float32),
            pltpu.VMEM((most if keep else 1, 2, rows, rows), jnp.float32),
            pltpu.VMEM((most + 1, HEAD_DIM, rows), jnp.float32),
            pltpu.VMEM((n, NOTE_ROWS, rows), jnp.bfloat16),
            pltpu.VMEM((heads, NOTE_ROWS, rows), jnp.bfloat16),
            pltpu.VMEM((n, HEAD_DIM, rows), jnp.bfloat16),
            pltpu.VMEM((heads, HEAD_DIM, rows), jnp.bfloat16),
            pltpu.VMEM((heads, HEAD_DIM, rows), jnp.float32),
            pltpu.SemaphoreType.DMA((2,)),
            pltpu.SemaphoreType.DMA,
            pltpu.SemaphoreType.DMA((heads,)),
            pltpu.SemaphoreType.DMA((n,)),
            pltpu.SemaphoreType.DMA((heads,)),
            pltpu.SemaphoreType.DMA((n,)),
            pltpu.SemaphoreType.DMA((n,)),
            pltpu.SemaphoreType.DMA((heads,)),
            pltpu.SemaphoreType.DMA((n,)),
            pltpu.SemaphoreType.DMA((heads,)),
        ],
        compiler_params=pltpu.CompilerParams(
            collective_id=0, has_side_effects=True, vmem_limit_bytes=60 * 1024 * 1024
        ),
        name="distill",
    )(*[pltpu.with_memory_space_constraint(x, pltpu.HBM) for x in (teacher_q, student_q, owner_table)])
    grad, divergence = pl.pallas_call(
        unpack,
        out_shape=(
            jax.ShapeDtypeStruct((rows, width), jnp.bfloat16),
            jax.ShapeDtypeStruct((1, heads), jnp.float32),
        ),
        in_specs=[vmem, vmem],
        out_specs=(vmem, vmem),
        compiler_params=pltpu.CompilerParams(vmem_limit_bytes=4 * 1024 * 1024),
        name="unpack",
    )(*packed)
    return (grad, divergence.reshape(heads))


def solution(mesh):
    placed = (P("tok", "head"), P("tok", "head"), P())
    return jax.shard_map(
        functools.partial(per_device, mesh.shape["tok"]),
        mesh=mesh,
        in_specs=placed,
        out_specs=(P("tok", "head"), P("head")),
        check_vma=False,
    )
```

```python
import functools
import math

import jax
import jax.numpy as jnp
from jax import lax
from jax.experimental import pallas as pl
from jax.experimental.pallas import tpu as pltpu
from jax.sharding import PartitionSpec as P

HEAD_DIM = 64
LANES = 128
NOTE_ROWS = 16
KEEP_BYTES = 16 * 1024 * 1024
floor_value = -3e38
distill_weight = 32.0
score_factor = HEAD_DIM ** (-0.5) * math.log2(math.e)
MESH = pl.DeviceIdType.MESH


def repeat(count, body, init=None):
    if count <= 16:
        for step in range(count):
            init = body(step, init)
        return init
    return lax.fori_loop(0, count, body, init)


def kernel(
    n, most, keep, teacher_hbm, student_hbm, table_hbm, grad_out, div_out,
    teacher, student, outbox, own_turned, own_exps, own_stats, inbox, left, turned, arrived,
    table, following, edge_of, edge_row, edge_col, edge_tag,
    stats, peaks, inverses, weights, pieces, exps, shares, out_note, in_note, out_grad, in_grad, near,
    load_sem, table_sem, send_sem, recv_sem, stat_send, stat_recv, note_send, note_recv,
    back_send, back_recv,
):
    rows, width = teacher_hbm.shape
    pairs = width // LANES
    heads = width // HEAD_DIM
    group = LANES // HEAD_DIM
    parts = n // heads
    chips = n // 2

    def worker_of(of_head):
        return of_head * parts + 1

    me = lax.axis_index("tok")
    head_at = lax.axis_index("head")
    chip, core = lax.div(me, 2), lax.rem(me, 2)
    head = lax.div(me, parts)
    is_worker = me == worker_of(head)
    way = 1 - 2 * lax.rem(chip, 2)

    def place(step):
        shift, flip = (step // 2, step % 2) if isinstance(step, int) else (lax.div(step, 2), lax.rem(step, 2))
        return 2 * lax.rem(chip + way * shift + chips, chips) + lax.rem(core + flip, 2)

    def place_in(worker):
        worker_chip = lax.div(worker, 2)
        worker_way = 1 - 2 * lax.rem(worker_chip, 2)
        shift = lax.rem(worker_way * (chip - worker_chip) + chips, chips)
        return 2 * shift + lax.rem(core + lax.rem(worker, 2), 2)

    def remote(src, dst, send, recv, target):
        return pltpu.make_async_remote_copy(
            src_ref=src, dst_ref=dst, send_sem=send, recv_sem=recv,
            device_id=(head_at, target), device_id_type=MESH,
        )

    barrier = pltpu.get_barrier_semaphore()
    loads = [
        pltpu.make_async_copy(teacher_hbm, teacher, load_sem.at[0]),
        pltpu.make_async_copy(student_hbm, student, load_sem.at[1]),
    ]
    for load in loads:
        load.start()
    table_load = pltpu.make_async_copy(table_hbm, table, table_sem)
    table_load.start()

    def greet(target):
        pl.semaphore_signal(barrier, inc=1, device_id=(head_at, target), device_id_type=MESH)

    @pl.when(is_worker)
    def greet_all():
        def greet_one(step, carry):
            greet(place(n - 1 - step))
            return carry

        repeat(n - 1, greet_one)

    @pl.when(jnp.logical_not(is_worker))
    def greet_workers():
        for step in range(heads):
            greet(worker_of(lax.rem(head + heads - 1 - step, heads)))

    for load in loads:
        load.wait()
    lane = lax.broadcasted_iota(jnp.int32, (rows, LANES), 1)
    lower = lane < HEAD_DIM
    none = jnp.zeros((), jnp.bfloat16)
    for pair in range(pairs):
        columns = pl.ds(pair * LANES, LANES)
        t_pair = teacher[:, columns].astype(jnp.float32)
        s_pair = student[:, columns].astype(jnp.float32)
        outbox[pair * group] = jnp.where(lower, t_pair, pltpu.roll(s_pair, HEAD_DIM, 1)).astype(
            jnp.bfloat16
        )
        outbox[pair * group + 1] = jnp.where(
            lower, pltpu.roll(t_pair, HEAD_DIM, 1), s_pair
        ).astype(jnp.bfloat16)

    def query_copy(to_head, slot):
        return remote(
            outbox.at[to_head], inbox.at[slot], send_sem.at[to_head], recv_sem.at[slot],
            worker_of(to_head),
        )

    def stat_copy(to_head, slot):
        return remote(
            own_stats.at[to_head], arrived.at[slot], stat_send.at[to_head], stat_recv.at[slot],
            worker_of(to_head),
        )

    def grad_copy(slot, target):
        return remote(
            out_grad.at[slot], in_grad.at[head], back_send.at[slot], back_recv.at[head], target
        )

    def note_copy(slot, target):
        return remote(
            out_note.at[slot], in_note.at[head], note_send.at[slot], note_recv.at[head], target
        )

    others = [lax.rem(head + step, heads) for step in range(heads - 1, 0, -1)]
    pl.semaphore_wait(barrier, jnp.where(is_worker, n - 1, heads))
    for to_head in others:
        query_copy(to_head, place_in(worker_of(to_head))).start()

    @pl.when(jnp.logical_not(is_worker))
    def send_near():
        query_copy(head, place_in(worker_of(head))).start()

    def masked(block):
        return jnp.where(lower, block, none), jnp.where(lower, none, block)

    def tile(both, block):
        raw = lax.dot_general(
            both, block, (((1,), (1,)), ((), ())), preferred_element_type=jnp.float32
        )
        return raw[:rows], raw[rows:]

    def measured(t_raw, s_raw):
        t_top = jnp.max(t_raw, axis=0, keepdims=True)
        s_top = jnp.max(s_raw, axis=0, keepdims=True)
        t_exp = jnp.exp2((t_raw - t_top) * score_factor)
        s_exp = jnp.exp2((s_raw - s_top) * score_factor)
        lines = (
            t_top,
            s_top,
            jnp.sum(t_exp, axis=0, keepdims=True),
            jnp.sum(s_exp, axis=0, keepdims=True),
            jnp.sum(t_exp * (t_raw - s_raw), axis=0, keepdims=True),
        )
        return t_exp, s_exp, lines

    for turn in range(heads):
        block = outbox[turn]
        own_turned[turn] = block.T[HEAD_DIM:]
        t_exp, s_exp, lines = measured(*tile(jnp.concatenate(masked(block), axis=0), block))
        own_exps[turn, 0] = t_exp
        own_exps[turn, 1] = s_exp
        for line_at, line in enumerate(lines):
            own_stats[turn, pl.ds(line_at, 1), :] = line
        own_stats[turn, pl.ds(len(lines), 8 - len(lines)), :] = jnp.zeros(
            (8 - len(lines), rows), jnp.float32
        )
    for to_head in others:
        stat_copy(to_head, place_in(worker_of(to_head))).start()
    table_load.wait()

    @pl.when(jnp.logical_not(is_worker))
    def send_near_stats():
        stat_copy(head, place_in(worker_of(head))).start()

    @pl.when(is_worker)
    def work():
        inbox[0] = outbox[head]
        arrived[0] = own_stats[head]
        codes = n * n
        blank = most

        def lower_cells(row, body, init):
            if isinstance(row, int):
                for col in range(row):
                    init = body(col, init)
                return init
            return lax.fori_loop(0, row, body, init)

        def count_row(row, count):
            row_at = place(row)

            def count_cell(col, count):
                inside = table[row_at, place(col)] >= 0
                edge = jnp.minimum(2 * count, most - 2)
                edge_of[row * n + col] = jnp.where(inside, edge, blank)
                edge_of[col * n + row] = jnp.where(inside, edge + 1, blank)
                return count + jnp.where(inside, 1, 0)

            return lower_cells(row, count_cell, count)

        repeat(n, count_row, jnp.int32(0))
        following[codes] = jnp.int32(codes)
        following[codes + 1] = jnp.int32(codes)

        def link_row(step, after):
            row = n - 1 - step
            row_at = place(row)
            following[row * n + row] = after

            def link_cell(back, after):
                col = row - 1 - back
                code = row * n + col
                after = jnp.where(table[row_at, place(col)] >= 0, code, after)
                following[code] = after
                return after

            return lower_cells(row, link_cell, after)

        repeat(n, link_row, jnp.int32(codes))

        def list_pair(pair, code):
            code = following[code]
            held = jnp.minimum(code, codes - 1)
            high, low = lax.div(held, n), lax.rem(held, n)
            edge_row[2 * pair] = high
            edge_col[2 * pair] = low
            edge_tag[2 * pair] = jnp.where(code < codes, high, -1)
            edge_row[2 * pair + 1] = low
            edge_col[2 * pair + 1] = high
            edge_tag[2 * pair + 1] = jnp.where(code < codes, low, -1)
            return code + 1

        repeat(most // 2, list_pair, jnp.int32(0))
        shares[blank] = jnp.zeros((HEAD_DIM, rows), jnp.float32)

        def take_block(slot, carry):
            @pl.when(slot > 0)
            def wait_block():
                remote(
                    outbox.at[0], inbox.at[slot], send_sem.at[0], recv_sem.at[slot], place(slot)
                ).wait_recv()

            return carry

        def keep_block(slot, carry):
            block = inbox[slot]
            t_part, s_part = masked(block)
            left[slot, pl.ds(0, rows), :] = t_part
            left[slot, pl.ds(rows, rows), :] = s_part
            turned[slot] = block.T[HEAD_DIM:]
            return carry

        def take_chip(shift, carry):
            for inner in range(2):
                take_block(2 * shift + inner, None)
            for inner in range(2):
                keep_block(2 * shift + inner, None)
            return carry

        repeat(chips, take_chip)

        def measure_edge(edge, carry):
            t_exp, s_exp, lines = measured(*tile(left[edge_col[edge]], inbox[edge_row[edge]]))
            for line_at, line in enumerate(lines):
                stats[line_at, pl.ds(edge, 1), :] = line
            if keep:
                exps[edge, 0] = t_exp
                exps[edge, 1] = s_exp
            return carry

        repeat(most, measure_edge)

        def take_stats(step, carry):
            slot = step + 1
            remote(
                own_stats.at[0], arrived.at[slot], stat_send.at[0], stat_recv.at[slot], place(slot)
            ).wait_recv()
            return carry

        repeat(n - 1, take_stats)
        slot_row = lax.broadcasted_iota(jnp.int32, (n, rows), 0)

        def place_stats(slot, carry):
            return tuple(
                jnp.where(slot_row == slot, arrived[slot, pl.ds(line_at, 1), :], line)
                for line_at, line in enumerate(carry)
            )

        blank_lines = jnp.zeros((n, rows), jnp.float32)
        first_stats = repeat(n, place_stats, (blank_lines,) * 5)

        def raise_peaks(edge, carry):
            mine = slot_row == edge_tag[edge]
            at = pl.ds(edge, 1)
            return tuple(
                jnp.maximum(peak, jnp.where(mine, stats[which, at, :], floor_value))
                for which, peak in enumerate(carry)
            )

        tops = repeat(most, raise_peaks, first_stats[:2])
        for which in range(2):
            peaks[which] = tops[which]
        first_parts = [
            jnp.exp2((first_stats[which] - tops[which]) * score_factor) for which in range(2)
        ]
        sums = (
            first_parts[0] * first_stats[2],
            first_parts[0] * first_stats[4],
            first_parts[1] * first_stats[3],
        )

        def add_edge(edge, carry):
            tag = edge_tag[edge]
            mine = slot_row == tag
            at = pl.ds(edge, 1)
            fresh = []
            for which in range(2):
                peak = peaks[which, pl.ds(jnp.maximum(tag, 0), 1), :]
                part = jnp.exp2(jnp.minimum((stats[which, at, :] - peak) * score_factor, 0.0))
                weights[which, at, :] = part
                fresh.append(part * stats[2 + which, at, :])
                if which == 0:
                    fresh.append(part * stats[4, at, :])
            return tuple(
                total + jnp.where(mine, piece, 0.0)
                for total, piece in zip(carry, fresh, strict=True)
            )

        t_sum, cross, s_sum = repeat(most, add_edge, sums)
        t_inverse, s_inverse = 1.0 / t_sum, 1.0 / s_sum
        inverses[0] = t_inverse
        inverses[1] = s_inverse

        def weigh_edge(edge, carry):
            tag = edge_tag[edge]
            at, mine_at = pl.ds(edge, 1), pl.ds(jnp.maximum(tag, 0), 1)
            valid = jnp.where(tag >= 0, 1.0, 0.0)
            for which in range(2):
                weights[which, at, :] = weights[which, at, :] * (
                    inverses[which, mine_at, :] * valid
                )
            return carry

        repeat(most, weigh_edge)

        def split(value):
            first = value.astype(jnp.bfloat16).astype(jnp.float32)
            second = (value - first).astype(jnp.bfloat16).astype(jnp.float32)
            return [first, second, value - first - second]

        for which in range(2):
            for at, piece in enumerate(split(first_parts[which] * inverses[which])):
                pieces[3 * which + at] = piece
        total = (
            (cross * t_inverse - tops[0] + tops[1]) * score_factor
            - jnp.log2(t_sum)
            + jnp.log2(s_sum)
        )
        total = jnp.sum(jnp.sum(total, axis=0, keepdims=True), axis=1, keepdims=True) * (
            math.log(2.0) / (rows * n)
        )
        note_row = lax.broadcasted_iota(jnp.int32, (NOTE_ROWS, LANES), 0)
        base = jnp.zeros((NOTE_ROWS, LANES), jnp.float32)
        for at, piece in enumerate(split(total)):
            base = jnp.where(note_row == at, piece, base)

        def send_note(step, carry):
            slot = n - 1 - step
            note = base
            for at in range(6):
                note = jnp.where(note_row == 3 + at, pieces[at, pl.ds(slot, 1), :], note)
            out_note[slot] = note.astype(jnp.bfloat16)

            @pl.when(slot > 0)
            def start_note():
                note_copy(slot, place(slot)).start()

            return carry

        repeat(n, send_note)

        def gap_of(edge, col, row):
            at = pl.ds(edge, 1)
            if keep:
                t_exp, s_exp = exps[edge, 0], exps[edge, 1]
            else:
                t_raw, s_raw = tile(left[col], inbox[row])
                t_exp = jnp.exp2((t_raw - stats[0, at, :]) * score_factor)
                s_exp = jnp.exp2((s_raw - stats[1, at, :]) * score_factor)
            return s_exp * weights[1, at, :] - t_exp * weights[0, at, :]

        def share_pair(pair, carry):
            high, low = edge_row[2 * pair], edge_col[2 * pair]
            gap = gap_of(2 * pair, low, high)
            back = gap_of(2 * pair + 1, high, low)
            symmetric = (gap + back.T).astype(jnp.bfloat16)
            shares[2 * pair] = jnp.dot(turned[low], symmetric, preferred_element_type=jnp.float32)
            shares[2 * pair + 1] = lax.dot_general(
                turned[high], symmetric, (((1,), (1,)), ((), ())),
                preferred_element_type=jnp.float32,
            )
            return carry

        repeat(most // 2, share_pair)

        def finish(step, carry):
            slot = n - 1 - step

            def add_share(turn, line):
                fresh = shares[edge_of[slot * n + (slot + turn + 1) % n]]
                return fresh if line is None else line + fresh

            line = repeat(n - 1, add_share, None if n <= 16 else jnp.zeros((HEAD_DIM, rows), jnp.float32))
            out_grad[slot] = (line * (distill_weight * HEAD_DIM ** (-0.5))).astype(jnp.bfloat16)

            @pl.when(slot > 0)
            def send_grad():
                grad_copy(slot, place(slot)).start()

            return carry

        repeat(n, finish)
        in_note[head] = out_note[0]
        in_grad[head] = out_grad[0]

    def take(kind, sends, receives, buffers, step):
        from_head = lax.rem(head + step, heads)

        def take_one():
            remote(
                kind.at[0], buffers.at[from_head], sends.at[0], receives.at[from_head],
                worker_of(from_head),
            ).wait_recv()

        if step == 0:
            pl.when(jnp.logical_not(is_worker))(take_one)
        else:
            take_one()
        return from_head

    for step in range(heads):
        take(out_note, note_send, note_recv, in_note, step)
    for turn in range(heads):
        note = in_note[turn].astype(jnp.float32)
        t_weight = note[3:4] + note[4:5] + note[5:6]
        s_weight = note[6:7] + note[7:8] + note[8:9]
        gap = own_exps[turn, 1] * s_weight - own_exps[turn, 0] * t_weight
        symmetric = (gap + gap.T).astype(jnp.bfloat16)
        near[turn] = jnp.dot(own_turned[turn], symmetric, preferred_element_type=jnp.float32) * (
            distill_weight * HEAD_DIM ** (-0.5)
        )
        div_out[pl.ds(turn, 1), :] = note[0:1] + note[1:2] + note[2:3]
    for step in range(heads):
        from_head = take(out_grad, back_send, back_recv, in_grad, step)
        grad_out[from_head] = (in_grad[from_head].astype(jnp.float32) + near[from_head]).astype(
            jnp.bfloat16
        )

    for to_head in others:
        query_copy(to_head, 0).wait_send()
        stat_copy(to_head, 0).wait_send()

    @pl.when(jnp.logical_not(is_worker))
    def drain_near():
        query_copy(head, 0).wait_send()
        stat_copy(head, 0).wait_send()

    @pl.when(is_worker)
    def drain_back():
        def drain_grads(step, carry):
            note_copy(step + 1, place(step + 1)).wait_send()
            grad_copy(step + 1, place(step + 1)).wait_send()
            return carry

        repeat(n - 1, drain_grads)


def unpack(in_grad, in_div, grad_ref, div_ref):
    heads = in_grad.shape[0]
    group = LANES // HEAD_DIM
    for pair in range(heads // group):
        both = jnp.concatenate([in_grad[pair * group + inner] for inner in range(group)], axis=0)
        grad_ref[:, pl.ds(pair * LANES, LANES)] = both.T
    div_lane = lax.broadcasted_iota(jnp.int32, (1, LANES), 1)
    div_row = jnp.zeros((1, LANES), jnp.float32)
    for slot in range(heads):
        div_row = jnp.where(div_lane == slot, in_div[pl.ds(slot, 1), :], div_row)
    div_ref[...] = div_row[:, :heads]


def per_device(n, teacher_q, student_q, owner_table):
    rows, width = teacher_q.shape
    heads = width // HEAD_DIM
    owned = n // heads
    most = 2 * (n * owned - n)
    keep = most * 2 * rows * rows * 4 <= KEEP_BYTES
    hbm = pl.BlockSpec(memory_space=pl.ANY)
    vmem = pl.BlockSpec(memory_space=pltpu.VMEM)
    packed = pl.pallas_call(
        functools.partial(kernel, n, most, keep),
        out_shape=(
            pltpu.VMEM((heads, HEAD_DIM, rows), jnp.bfloat16),
            pltpu.VMEM((heads, rows), jnp.float32),
        ),
        in_specs=[hbm, hbm, hbm],
        out_specs=(vmem, vmem),
        scratch_shapes=[
            pltpu.VMEM((rows, width), jnp.bfloat16),
            pltpu.VMEM((rows, width), jnp.bfloat16),
            pltpu.VMEM((heads, rows, LANES), jnp.bfloat16),
            pltpu.VMEM((heads, HEAD_DIM, rows), jnp.bfloat16),
            pltpu.VMEM((heads, 2, rows, rows), jnp.float32),
            pltpu.VMEM((heads, 8, rows), jnp.float32),
            pltpu.VMEM((n, rows, LANES), jnp.bfloat16),
            pltpu.VMEM((n, 2 * rows, LANES), jnp.bfloat16),
            pltpu.VMEM((n, HEAD_DIM, rows), jnp.bfloat16),
            pltpu.VMEM((n, 8, rows), jnp.float32),
            pltpu.SMEM((n, n), jnp.int32),
            pltpu.SMEM((n * n + 2,), jnp.int32),
            pltpu.SMEM((n * n,), jnp.int32),
            pltpu.SMEM((most,), jnp.int32),
            pltpu.SMEM((most,), jnp.int32),
            pltpu.SMEM((most,), jnp.int32),
            pltpu.VMEM((5, most, rows), jnp.float32),
            pltpu.VMEM((2, n, rows), jnp.float32),
            pltpu.VMEM((2, n, rows), jnp.float32),
            pltpu.VMEM((2, most, rows), jnp.float32),
            pltpu.VMEM((6, n, rows), jnp.float32),
            pltpu.VMEM((most if keep else 1, 2, rows, rows), jnp.float32),
            pltpu.VMEM((most + 1, HEAD_DIM, rows), jnp.float32),
            pltpu.VMEM((n, NOTE_ROWS, rows), jnp.bfloat16),
            pltpu.VMEM((heads, NOTE_ROWS, rows), jnp.bfloat16),
            pltpu.VMEM((n, HEAD_DIM, rows), jnp.bfloat16),
            pltpu.VMEM((heads, HEAD_DIM, rows), jnp.bfloat16),
            pltpu.VMEM((heads, HEAD_DIM, rows), jnp.float32),
            pltpu.SemaphoreType.DMA((2,)),
            pltpu.SemaphoreType.DMA,
            pltpu.SemaphoreType.DMA((heads,)),
            pltpu.SemaphoreType.DMA((n,)),
            pltpu.SemaphoreType.DMA((heads,)),
            pltpu.SemaphoreType.DMA((n,)),
            pltpu.SemaphoreType.DMA((n,)),
            pltpu.SemaphoreType.DMA((heads,)),
            pltpu.SemaphoreType.DMA((n,)),
            pltpu.SemaphoreType.DMA((heads,)),
        ],
        compiler_params=pltpu.CompilerParams(
            collective_id=0, has_side_effects=True, vmem_limit_bytes=60 * 1024 * 1024
        ),
        name="distill",
    )(*[pltpu.with_memory_space_constraint(x, pltpu.HBM) for x in (teacher_q, student_q, owner_table)])
    grad, divergence = pl.pallas_call(
        unpack,
        out_shape=(
            jax.ShapeDtypeStruct((rows, width), jnp.bfloat16),
            jax.ShapeDtypeStruct((1, heads), jnp.float32),
        ),
        in_specs=[vmem, vmem],
        out_specs=(vmem, vmem),
        compiler_params=pltpu.CompilerParams(vmem_limit_bytes=4 * 1024 * 1024),
        name="unpack",
    )(*packed)
    return (grad, divergence.reshape(heads))


def solution(mesh):
    placed = (P("tok", "head"), P("tok", "head"), P())
    return jax.shard_map(
        functools.partial(per_device, mesh.shape["tok"]),
        mesh=mesh,
        in_specs=placed,
        out_specs=(P("tok", "head"), P("head")),
        check_vma=False,
    )
```

```python
import functools
import math

import jax
import jax.numpy as jnp
from jax import lax
from jax.experimental import pallas as pl
from jax.experimental.pallas import tpu as pltpu
from jax.sharding import PartitionSpec as P

HEAD_DIM = 64
LANES = 128
NOTE_ROWS = 16
KEEP_BYTES = 16 * 1024 * 1024
floor_value = -3e38
distill_weight = 32.0
score_factor = HEAD_DIM ** (-0.5) * math.log2(math.e)
MESH = pl.DeviceIdType.MESH


def repeat(count, body, init=None):
    if count <= 16:
        for step in range(count):
            init = body(step, init)
        return init
    return lax.fori_loop(0, count, body, init)


def kernel(
    n, most, keep, teacher_hbm, student_hbm, table_hbm, grad_out, div_out,
    teacher, student, outbox, own_turned, own_exps, own_stats, inbox, left, turned, arrived,
    table, following, edge_of, edge_row, edge_col, edge_tag,
    stats, peaks, inverses, weights, pieces, exps, shares, out_note, in_note, out_grad, in_grad, near,
    load_sem, table_sem, send_sem, recv_sem, stat_send, stat_recv, note_send, note_recv,
    back_send, back_recv,
):
    rows, width = teacher_hbm.shape
    pairs = width // LANES
    heads = width // HEAD_DIM
    group = LANES // HEAD_DIM
    parts = n // heads
    chips = n // 2

    def worker_of(of_head):
        return of_head * parts + 1

    me = lax.axis_index("tok")
    head_at = lax.axis_index("head")
    chip, core = lax.div(me, 2), lax.rem(me, 2)
    head = lax.div(me, parts)
    is_worker = me == worker_of(head)
    way = 1 - 2 * lax.rem(chip, 2)

    def place(step):
        shift, flip = (step // 2, step % 2) if isinstance(step, int) else (lax.div(step, 2), lax.rem(step, 2))
        return 2 * lax.rem(chip + way * shift + chips, chips) + lax.rem(core + flip, 2)

    def place_in(worker):
        worker_chip = lax.div(worker, 2)
        worker_way = 1 - 2 * lax.rem(worker_chip, 2)
        shift = lax.rem(worker_way * (chip - worker_chip) + chips, chips)
        return 2 * shift + lax.rem(core + lax.rem(worker, 2), 2)

    def remote(src, dst, send, recv, target):
        return pltpu.make_async_remote_copy(
            src_ref=src, dst_ref=dst, send_sem=send, recv_sem=recv,
            device_id=(head_at, target), device_id_type=MESH,
        )

    barrier = pltpu.get_barrier_semaphore()
    loads = [
        pltpu.make_async_copy(teacher_hbm, teacher, load_sem.at[0]),
        pltpu.make_async_copy(student_hbm, student, load_sem.at[1]),
    ]
    for load in loads:
        load.start()
    table_load = pltpu.make_async_copy(table_hbm, table, table_sem)
    table_load.start()

    def greet(target):
        pl.semaphore_signal(barrier, inc=1, device_id=(head_at, target), device_id_type=MESH)

    @pl.when(is_worker)
    def greet_all():
        def greet_one(step, carry):
            greet(place(n - 1 - step))
            return carry

        repeat(n - 1, greet_one)

    @pl.when(jnp.logical_not(is_worker))
    def greet_workers():
        for step in range(heads):
            greet(worker_of(lax.rem(head + heads - 1 - step, heads)))

    for load in loads:
        load.wait()
    lane = lax.broadcasted_iota(jnp.int32, (rows, LANES), 1)
    lower = lane < HEAD_DIM
    none = jnp.zeros((), jnp.bfloat16)
    for pair in range(pairs):
        columns = pl.ds(pair * LANES, LANES)
        t_pair = teacher[:, columns].astype(jnp.float32)
        s_pair = student[:, columns].astype(jnp.float32)
        outbox[pair * group] = jnp.where(lower, t_pair, pltpu.roll(s_pair, HEAD_DIM, 1)).astype(
            jnp.bfloat16
        )
        outbox[pair * group + 1] = jnp.where(
            lower, pltpu.roll(t_pair, HEAD_DIM, 1), s_pair
        ).astype(jnp.bfloat16)

    def query_copy(to_head, slot):
        return remote(
            outbox.at[to_head], inbox.at[slot], send_sem, recv_sem.at[lax.div(slot, 2)],
            worker_of(to_head),
        )

    def stat_copy(to_head, slot):
        return remote(
            own_stats.at[to_head], arrived.at[slot], stat_send, stat_recv,
            worker_of(to_head),
        )

    def grad_copy(slot, target):
        return remote(
            out_grad.at[slot], in_grad.at[head], back_send, back_recv, target
        )

    def note_copy(slot, target):
        return remote(
            out_note.at[slot], in_note.at[head], note_send, note_recv, target
        )

    def all_of(ref, first, count, sem):
        whole = ref.at[pl.ds(first, count)]
        return remote(whole, whole, sem, sem, me)

    others = [lax.rem(head + step, heads) for step in range(heads - 1, 0, -1)]
    pl.semaphore_wait(barrier, jnp.where(is_worker, n - 1, heads))
    for to_head in others:
        query_copy(to_head, place_in(worker_of(to_head))).start()

    @pl.when(jnp.logical_not(is_worker))
    def send_near():
        query_copy(head, place_in(worker_of(head))).start()

    def masked(block):
        return jnp.where(lower, block, none), jnp.where(lower, none, block)

    def tile(both, block):
        raw = lax.dot_general(
            both, block, (((1,), (1,)), ((), ())), preferred_element_type=jnp.float32
        )
        return raw[:rows], raw[rows:]

    def measured(t_raw, s_raw):
        t_top = jnp.max(t_raw, axis=0, keepdims=True)
        s_top = jnp.max(s_raw, axis=0, keepdims=True)
        t_exp = jnp.exp2((t_raw - t_top) * score_factor)
        s_exp = jnp.exp2((s_raw - s_top) * score_factor)
        lines = (
            t_top,
            s_top,
            jnp.sum(t_exp, axis=0, keepdims=True),
            jnp.sum(s_exp, axis=0, keepdims=True),
            jnp.sum(t_exp * (t_raw - s_raw), axis=0, keepdims=True),
        )
        return t_exp, s_exp, lines

    for turn in range(heads):
        block = outbox[turn]
        own_turned[turn] = block.T[HEAD_DIM:]
        t_exp, s_exp, lines = measured(*tile(jnp.concatenate(masked(block), axis=0), block))
        own_exps[turn, 0] = t_exp
        own_exps[turn, 1] = s_exp
        for line_at, line in enumerate(lines):
            own_stats[turn, pl.ds(line_at, 1), :] = line
        own_stats[turn, pl.ds(len(lines), 8 - len(lines)), :] = jnp.zeros(
            (8 - len(lines), rows), jnp.float32
        )
    for to_head in others:
        stat_copy(to_head, place_in(worker_of(to_head))).start()
    table_load.wait()

    @pl.when(jnp.logical_not(is_worker))
    def send_near_stats():
        stat_copy(head, place_in(worker_of(head))).start()

    @pl.when(is_worker)
    def work():
        inbox[0] = outbox[head]
        arrived[0] = own_stats[head]
        codes = n * n
        blank = most

        def lower_cells(row, body, init):
            if isinstance(row, int):
                for col in range(row):
                    init = body(col, init)
                return init
            return lax.fori_loop(0, row, body, init)

        def count_row(row, count):
            row_at = place(row)

            def count_cell(col, count):
                inside = table[row_at, place(col)] >= 0
                edge = jnp.minimum(2 * count, most - 2)
                edge_of[row * n + col] = jnp.where(inside, edge, blank)
                edge_of[col * n + row] = jnp.where(inside, edge + 1, blank)
                return count + jnp.where(inside, 1, 0)

            return lower_cells(row, count_cell, count)

        repeat(n, count_row, jnp.int32(0))
        following[codes] = jnp.int32(codes)
        following[codes + 1] = jnp.int32(codes)

        def link_row(step, after):
            row = n - 1 - step
            row_at = place(row)
            following[row * n + row] = after

            def link_cell(back, after):
                col = row - 1 - back
                code = row * n + col
                after = jnp.where(table[row_at, place(col)] >= 0, code, after)
                following[code] = after
                return after

            return lower_cells(row, link_cell, after)

        repeat(n, link_row, jnp.int32(codes))

        def list_pair(pair, code):
            code = following[code]
            held = jnp.minimum(code, codes - 1)
            high, low = lax.div(held, n), lax.rem(held, n)
            edge_row[2 * pair] = high
            edge_col[2 * pair] = low
            edge_tag[2 * pair] = jnp.where(code < codes, high, -1)
            edge_row[2 * pair + 1] = low
            edge_col[2 * pair + 1] = high
            edge_tag[2 * pair + 1] = jnp.where(code < codes, low, -1)
            return code + 1

        repeat(most // 2, list_pair, jnp.int32(0))
        shares[blank] = jnp.zeros((HEAD_DIM, rows), jnp.float32)

        def keep_block(slot, carry):
            block = inbox[slot]
            t_part, s_part = masked(block)
            left[slot, pl.ds(0, rows), :] = t_part
            left[slot, pl.ds(rows, rows), :] = s_part
            turned[slot] = block.T[HEAD_DIM:]
            return carry

        def take_chip(shift, carry):
            if isinstance(shift, int) and shift == 0:
                all_of(inbox, 1, 1, recv_sem.at[0]).wait_recv()
            else:
                all_of(inbox, 2 * shift, 2, recv_sem.at[shift]).wait_recv()
            for inner in range(2):
                keep_block(2 * shift + inner, None)
            return carry

        take_chip(0, None)
        if chips > 16:
            lax.fori_loop(1, chips, take_chip, None)
        else:
            for shift in range(1, chips):
                take_chip(shift, None)

        def measure_edge(edge, carry):
            t_exp, s_exp, lines = measured(*tile(left[edge_col[edge]], inbox[edge_row[edge]]))
            for line_at, line in enumerate(lines):
                stats[line_at, pl.ds(edge, 1), :] = line
            if keep:
                exps[edge, 0] = t_exp
                exps[edge, 1] = s_exp
            return carry

        repeat(most, measure_edge)

        all_of(arrived, 1, n - 1, stat_recv).wait_recv()
        slot_row = lax.broadcasted_iota(jnp.int32, (n, rows), 0)

        def place_stats(slot, carry):
            return tuple(
                jnp.where(slot_row == slot, arrived[slot, pl.ds(line_at, 1), :], line)
                for line_at, line in enumerate(carry)
            )

        blank_lines = jnp.zeros((n, rows), jnp.float32)
        first_stats = repeat(n, place_stats, (blank_lines,) * 5)

        def raise_peaks(edge, carry):
            mine = slot_row == edge_tag[edge]
            at = pl.ds(edge, 1)
            return tuple(
                jnp.maximum(peak, jnp.where(mine, stats[which, at, :], floor_value))
                for which, peak in enumerate(carry)
            )

        tops = repeat(most, raise_peaks, first_stats[:2])
        for which in range(2):
            peaks[which] = tops[which]
        first_parts = [
            jnp.exp2((first_stats[which] - tops[which]) * score_factor) for which in range(2)
        ]
        sums = (
            first_parts[0] * first_stats[2],
            first_parts[0] * first_stats[4],
            first_parts[1] * first_stats[3],
        )

        def add_edge(edge, carry):
            tag = edge_tag[edge]
            mine = slot_row == tag
            at = pl.ds(edge, 1)
            fresh = []
            for which in range(2):
                peak = peaks[which, pl.ds(jnp.maximum(tag, 0), 1), :]
                part = jnp.exp2(jnp.minimum((stats[which, at, :] - peak) * score_factor, 0.0))
                weights[which, at, :] = part
                fresh.append(part * stats[2 + which, at, :])
                if which == 0:
                    fresh.append(part * stats[4, at, :])
            return tuple(
                total + jnp.where(mine, piece, 0.0)
                for total, piece in zip(carry, fresh, strict=True)
            )

        t_sum, cross, s_sum = repeat(most, add_edge, sums)
        t_inverse, s_inverse = 1.0 / t_sum, 1.0 / s_sum
        inverses[0] = t_inverse
        inverses[1] = s_inverse

        def weigh_edge(edge, carry):
            tag = edge_tag[edge]
            at, mine_at = pl.ds(edge, 1), pl.ds(jnp.maximum(tag, 0), 1)
            valid = jnp.where(tag >= 0, 1.0, 0.0)
            for which in range(2):
                weights[which, at, :] = weights[which, at, :] * (
                    inverses[which, mine_at, :] * valid
                )
            return carry

        repeat(most, weigh_edge)

        def split(value):
            first = value.astype(jnp.bfloat16).astype(jnp.float32)
            second = (value - first).astype(jnp.bfloat16).astype(jnp.float32)
            return [first, second, value - first - second]

        for which in range(2):
            for at, piece in enumerate(split(first_parts[which] * inverses[which])):
                pieces[3 * which + at] = piece
        total = (
            (cross * t_inverse - tops[0] + tops[1]) * score_factor
            - jnp.log2(t_sum)
            + jnp.log2(s_sum)
        )
        total = jnp.sum(jnp.sum(total, axis=0, keepdims=True), axis=1, keepdims=True) * (
            math.log(2.0) / (rows * n)
        )
        note_row = lax.broadcasted_iota(jnp.int32, (NOTE_ROWS, LANES), 0)
        base = jnp.zeros((NOTE_ROWS, LANES), jnp.float32)
        for at, piece in enumerate(split(total)):
            base = jnp.where(note_row == at, piece, base)

        def send_note(step, carry):
            slot = n - 1 - step
            note = base
            for at in range(6):
                note = jnp.where(note_row == 3 + at, pieces[at, pl.ds(slot, 1), :], note)
            out_note[slot] = note.astype(jnp.bfloat16)

            @pl.when(slot > 0)
            def start_note():
                note_copy(slot, place(slot)).start()

            return carry

        repeat(n, send_note)

        def gap_of(edge, col, row):
            at = pl.ds(edge, 1)
            if keep:
                t_exp, s_exp = exps[edge, 0], exps[edge, 1]
            else:
                t_raw, s_raw = tile(left[col], inbox[row])
                t_exp = jnp.exp2((t_raw - stats[0, at, :]) * score_factor)
                s_exp = jnp.exp2((s_raw - stats[1, at, :]) * score_factor)
            return s_exp * weights[1, at, :] - t_exp * weights[0, at, :]

        def share_pair(pair, carry):
            high, low = edge_row[2 * pair], edge_col[2 * pair]
            gap = gap_of(2 * pair, low, high)
            back = gap_of(2 * pair + 1, high, low)
            symmetric = (gap + back.T).astype(jnp.bfloat16)
            shares[2 * pair] = jnp.dot(turned[low], symmetric, preferred_element_type=jnp.float32)
            shares[2 * pair + 1] = lax.dot_general(
                turned[high], symmetric, (((1,), (1,)), ((), ())),
                preferred_element_type=jnp.float32,
            )
            return carry

        repeat(most // 2, share_pair)

        def finish(step, carry):
            slot = n - 1 - step

            def add_share(turn, line):
                fresh = shares[edge_of[slot * n + (slot + turn + 1) % n]]
                return fresh if line is None else line + fresh

            line = repeat(n - 1, add_share, None if n <= 16 else jnp.zeros((HEAD_DIM, rows), jnp.float32))
            out_grad[slot] = (line * (distill_weight * HEAD_DIM ** (-0.5))).astype(jnp.bfloat16)

            @pl.when(slot > 0)
            def send_grad():
                grad_copy(slot, place(slot)).start()

            return carry

        repeat(n, finish)
        in_note[head] = out_note[0]
        in_grad[head] = out_grad[0]

    def take(buffers, sem):
        @pl.when(is_worker)
        def take_others():
            all_of(buffers, 0, heads - 1, sem).wait_recv()

        @pl.when(jnp.logical_not(is_worker))
        def take_all():
            all_of(buffers, 0, heads, sem).wait_recv()

    take(in_note, note_recv)
    for turn in range(heads):
        note = in_note[turn].astype(jnp.float32)
        t_weight = note[3:4] + note[4:5] + note[5:6]
        s_weight = note[6:7] + note[7:8] + note[8:9]
        gap = own_exps[turn, 1] * s_weight - own_exps[turn, 0] * t_weight
        symmetric = (gap + gap.T).astype(jnp.bfloat16)
        near[turn] = jnp.dot(own_turned[turn], symmetric, preferred_element_type=jnp.float32) * (
            distill_weight * HEAD_DIM ** (-0.5)
        )
        div_out[pl.ds(turn, 1), :] = note[0:1] + note[1:2] + note[2:3]
    take(in_grad, back_recv)
    for turn in range(heads):
        grad_out[turn] = (in_grad[turn].astype(jnp.float32) + near[turn]).astype(jnp.bfloat16)

    @pl.when(is_worker)
    def drain_worker():
        all_of(outbox, 0, heads - 1, send_sem).wait_send()
        all_of(own_stats, 0, heads - 1, stat_send).wait_send()
        all_of(out_note, 1, n - 1, note_send).wait_send()
        all_of(out_grad, 1, n - 1, back_send).wait_send()

    @pl.when(jnp.logical_not(is_worker))
    def drain_server():
        all_of(outbox, 0, heads, send_sem).wait_send()
        all_of(own_stats, 0, heads, stat_send).wait_send()


def unpack(in_grad, in_div, grad_ref, div_ref):
    heads = in_grad.shape[0]
    group = LANES // HEAD_DIM
    for pair in range(heads // group):
        both = jnp.concatenate([in_grad[pair * group + inner] for inner in range(group)], axis=0)
        grad_ref[:, pl.ds(pair * LANES, LANES)] = both.T
    div_lane = lax.broadcasted_iota(jnp.int32, (1, LANES), 1)
    div_row = jnp.zeros((1, LANES), jnp.float32)
    for slot in range(heads):
        div_row = jnp.where(div_lane == slot, in_div[pl.ds(slot, 1), :], div_row)
    div_ref[...] = div_row[:, :heads]


def per_device(n, teacher_q, student_q, owner_table):
    rows, width = teacher_q.shape
    heads = width // HEAD_DIM
    chips = n // 2
    owned = n // heads
    most = 2 * (n * owned - n)
    keep = most * 2 * rows * rows * 4 <= KEEP_BYTES
    hbm = pl.BlockSpec(memory_space=pl.ANY)
    vmem = pl.BlockSpec(memory_space=pltpu.VMEM)
    packed = pl.pallas_call(
        functools.partial(kernel, n, most, keep),
        out_shape=(
            pltpu.VMEM((heads, HEAD_DIM, rows), jnp.bfloat16),
            pltpu.VMEM((heads, rows), jnp.float32),
        ),
        in_specs=[hbm, hbm, hbm],
        out_specs=(vmem, vmem),
        scratch_shapes=[
            pltpu.VMEM((rows, width), jnp.bfloat16),
            pltpu.VMEM((rows, width), jnp.bfloat16),
            pltpu.VMEM((heads, rows, LANES), jnp.bfloat16),
            pltpu.VMEM((heads, HEAD_DIM, rows), jnp.bfloat16),
            pltpu.VMEM((heads, 2, rows, rows), jnp.float32),
            pltpu.VMEM((heads, 8, rows), jnp.float32),
            pltpu.VMEM((n, rows, LANES), jnp.bfloat16),
            pltpu.VMEM((n, 2 * rows, LANES), jnp.bfloat16),
            pltpu.VMEM((n, HEAD_DIM, rows), jnp.bfloat16),
            pltpu.VMEM((n, 8, rows), jnp.float32),
            pltpu.SMEM((n, n), jnp.int32),
            pltpu.SMEM((n * n + 2,), jnp.int32),
            pltpu.SMEM((n * n,), jnp.int32),
            pltpu.SMEM((most,), jnp.int32),
            pltpu.SMEM((most,), jnp.int32),
            pltpu.SMEM((most,), jnp.int32),
            pltpu.VMEM((5, most, rows), jnp.float32),
            pltpu.VMEM((2, n, rows), jnp.float32),
            pltpu.VMEM((2, n, rows), jnp.float32),
            pltpu.VMEM((2, most, rows), jnp.float32),
            pltpu.VMEM((6, n, rows), jnp.float32),
            pltpu.VMEM((most if keep else 1, 2, rows, rows), jnp.float32),
            pltpu.VMEM((most + 1, HEAD_DIM, rows), jnp.float32),
            pltpu.VMEM((n, NOTE_ROWS, rows), jnp.bfloat16),
            pltpu.VMEM((heads, NOTE_ROWS, rows), jnp.bfloat16),
            pltpu.VMEM((n, HEAD_DIM, rows), jnp.bfloat16),
            pltpu.VMEM((heads, HEAD_DIM, rows), jnp.bfloat16),
            pltpu.VMEM((heads, HEAD_DIM, rows), jnp.float32),
            pltpu.SemaphoreType.DMA((2,)),
            pltpu.SemaphoreType.DMA,
            pltpu.SemaphoreType.DMA,
            pltpu.SemaphoreType.DMA((chips,)),
            pltpu.SemaphoreType.DMA,
            pltpu.SemaphoreType.DMA,
            pltpu.SemaphoreType.DMA,
            pltpu.SemaphoreType.DMA,
            pltpu.SemaphoreType.DMA,
            pltpu.SemaphoreType.DMA,
        ],
        compiler_params=pltpu.CompilerParams(
            collective_id=0, has_side_effects=True, vmem_limit_bytes=60 * 1024 * 1024
        ),
        name="distill",
    )(*[pltpu.with_memory_space_constraint(x, pltpu.HBM) for x in (teacher_q, student_q, owner_table)])
    grad, divergence = pl.pallas_call(
        unpack,
        out_shape=(
            jax.ShapeDtypeStruct((rows, width), jnp.bfloat16),
            jax.ShapeDtypeStruct((1, heads), jnp.float32),
        ),
        in_specs=[vmem, vmem],
        out_specs=(vmem, vmem),
        compiler_params=pltpu.CompilerParams(vmem_limit_bytes=4 * 1024 * 1024),
        name="unpack",
    )(*packed)
    return (grad, divergence.reshape(heads))


def solution(mesh):
    placed = (P("tok", "head"), P("tok", "head"), P())
    return jax.shard_map(
        functools.partial(per_device, mesh.shape["tok"]),
        mesh=mesh,
        in_specs=placed,
        out_specs=(P("tok", "head"), P("head")),
        check_vma=False,
    )
```

```python
import functools
import math

import jax
import jax.numpy as jnp
from jax import lax
from jax.experimental import pallas as pl
from jax.experimental.pallas import tpu as pltpu
from jax.sharding import PartitionSpec as P

HEAD_DIM = 64
LANES = 128
NOTE_ROWS = 16
KEEP_BYTES = 16 * 1024 * 1024
floor_value = -3e38
distill_weight = 32.0
score_factor = HEAD_DIM ** (-0.5) * math.log2(math.e)
MESH = pl.DeviceIdType.MESH


def repeat(count, body, init=None):
    if count <= 16:
        for step in range(count):
            init = body(step, init)
        return init
    return lax.fori_loop(0, count, body, init)


def kernel(
    n, most, keep, teacher_hbm, student_hbm, table_hbm, grad_out, div_out,
    teacher, student, outbox, own_turned, own_exps, own_stats, inbox, left, turned, arrived,
    table, following, edge_of, edge_row, edge_col, edge_tag,
    stats, peaks, inverses, weights, pieces, exps, shares, out_note, in_note, out_grad, in_grad, near,
    load_sem, table_sem, send_sem, recv_sem, stat_send, stat_recv, note_send, note_recv,
    back_send, back_recv,
):
    rows, width = teacher_hbm.shape
    pairs = width // LANES
    heads = width // HEAD_DIM
    group = LANES // HEAD_DIM
    parts = n // heads
    chips = n // 2

    def worker_of(of_head):
        return jnp.where(of_head == 0, 0, of_head * parts + 1)

    me = lax.axis_index("tok")
    head_at = lax.axis_index("head")
    chip, core = lax.div(me, 2), lax.rem(me, 2)
    head = lax.div(me, parts)
    is_worker = me == worker_of(head)
    way = 1 - 2 * lax.rem(chip, 2)

    def place(step):
        shift, flip = (step // 2, step % 2) if isinstance(step, int) else (lax.div(step, 2), lax.rem(step, 2))
        return 2 * lax.rem(chip + way * shift + chips, chips) + lax.rem(core + flip, 2)

    def place_in(worker):
        worker_chip = lax.div(worker, 2)
        worker_way = 1 - 2 * lax.rem(worker_chip, 2)
        shift = lax.rem(worker_way * (chip - worker_chip) + chips, chips)
        return 2 * shift + lax.rem(core + lax.rem(worker, 2), 2)

    def remote(src, dst, send, recv, target):
        return pltpu.make_async_remote_copy(
            src_ref=src, dst_ref=dst, send_sem=send, recv_sem=recv,
            device_id=(head_at, target), device_id_type=MESH,
        )

    barrier = pltpu.get_barrier_semaphore()
    loads = [
        pltpu.make_async_copy(teacher_hbm, teacher, load_sem.at[0]),
        pltpu.make_async_copy(student_hbm, student, load_sem.at[1]),
    ]
    for load in loads:
        load.start()
    table_load = pltpu.make_async_copy(table_hbm, table, table_sem)
    table_load.start()

    def greet(target):
        pl.semaphore_signal(barrier, inc=1, device_id=(head_at, target), device_id_type=MESH)

    @pl.when(is_worker)
    def greet_all():
        def greet_one(step, carry):
            greet(place(n - 1 - step))
            return carry

        repeat(n - 1, greet_one)

    @pl.when(jnp.logical_not(is_worker))
    def greet_workers():
        for step in range(heads):
            greet(worker_of(lax.rem(head + heads - 1 - step, heads)))

    for load in loads:
        load.wait()
    lane = lax.broadcasted_iota(jnp.int32, (rows, LANES), 1)
    lower = lane < HEAD_DIM
    none = jnp.zeros((), jnp.bfloat16)
    for pair in range(pairs):
        columns = pl.ds(pair * LANES, LANES)
        t_pair = teacher[:, columns].astype(jnp.float32)
        s_pair = student[:, columns].astype(jnp.float32)
        outbox[pair * group] = jnp.where(lower, t_pair, pltpu.roll(s_pair, HEAD_DIM, 1)).astype(
            jnp.bfloat16
        )
        outbox[pair * group + 1] = jnp.where(
            lower, pltpu.roll(t_pair, HEAD_DIM, 1), s_pair
        ).astype(jnp.bfloat16)

    def query_copy(to_head, slot):
        return remote(
            outbox.at[to_head], inbox.at[slot], send_sem, recv_sem.at[lax.div(slot, 2)],
            worker_of(to_head),
        )

    def stat_copy(to_head, slot):
        return remote(
            own_stats.at[to_head], arrived.at[slot], stat_send, stat_recv,
            worker_of(to_head),
        )

    def grad_copy(slot, target):
        return remote(
            out_grad.at[slot], in_grad.at[head], back_send, back_recv, target
        )

    def note_copy(slot, target):
        return remote(
            out_note.at[slot], in_note.at[head], note_send, note_recv, target
        )

    def all_of(ref, first, count, sem):
        whole = ref.at[pl.ds(first, count)]
        return remote(whole, whole, sem, sem, me)

    others = [lax.rem(head + way * step + heads, heads) for step in (3, 1, 2)]
    pl.semaphore_wait(barrier, jnp.where(is_worker, n - 1, heads))
    for to_head in others:
        query_copy(to_head, place_in(worker_of(to_head))).start()

    @pl.when(jnp.logical_not(is_worker))
    def send_near():
        query_copy(head, place_in(worker_of(head))).start()

    def masked(block):
        return jnp.where(lower, block, none), jnp.where(lower, none, block)

    def tile(both, block):
        raw = lax.dot_general(
            both, block, (((1,), (1,)), ((), ())), preferred_element_type=jnp.float32
        )
        return raw[:rows], raw[rows:]

    def measured(t_raw, s_raw):
        t_top = jnp.max(t_raw, axis=0, keepdims=True)
        s_top = jnp.max(s_raw, axis=0, keepdims=True)
        t_exp = jnp.exp2((t_raw - t_top) * score_factor)
        s_exp = jnp.exp2((s_raw - s_top) * score_factor)
        lines = (
            t_top,
            s_top,
            jnp.sum(t_exp, axis=0, keepdims=True),
            jnp.sum(s_exp, axis=0, keepdims=True),
            jnp.sum(t_exp * (t_raw - s_raw), axis=0, keepdims=True),
        )
        return t_exp, s_exp, lines

    for turn in range(heads):
        block = outbox[turn]
        own_turned[turn] = block.T[HEAD_DIM:]
        t_exp, s_exp, lines = measured(*tile(jnp.concatenate(masked(block), axis=0), block))
        own_exps[turn, 0] = t_exp
        own_exps[turn, 1] = s_exp
        for line_at, line in enumerate(lines):
            own_stats[turn, pl.ds(line_at, 1), :] = line
        own_stats[turn, pl.ds(len(lines), 8 - len(lines)), :] = jnp.zeros(
            (8 - len(lines), rows), jnp.float32
        )
    for to_head in others:
        stat_copy(to_head, place_in(worker_of(to_head))).start()
    table_load.wait()

    @pl.when(jnp.logical_not(is_worker))
    def send_near_stats():
        stat_copy(head, place_in(worker_of(head))).start()

    @pl.when(is_worker)
    def work():
        inbox[0] = outbox[head]
        arrived[0] = own_stats[head]
        codes = n * n
        blank = most

        def lower_cells(row, body, init):
            if isinstance(row, int):
                for col in range(row):
                    init = body(col, init)
                return init
            return lax.fori_loop(0, row, body, init)

        def count_row(row, count):
            row_at = place(row)

            def count_cell(col, count):
                inside = table[row_at, place(col)] >= 0
                edge = jnp.minimum(2 * count, most - 2)
                edge_of[row * n + col] = jnp.where(inside, edge, blank)
                edge_of[col * n + row] = jnp.where(inside, edge + 1, blank)
                return count + jnp.where(inside, 1, 0)

            return lower_cells(row, count_cell, count)

        repeat(n, count_row, jnp.int32(0))
        following[codes] = jnp.int32(codes)
        following[codes + 1] = jnp.int32(codes)

        def link_row(step, after):
            row = n - 1 - step
            row_at = place(row)
            following[row * n + row] = after

            def link_cell(back, after):
                col = row - 1 - back
                code = row * n + col
                after = jnp.where(table[row_at, place(col)] >= 0, code, after)
                following[code] = after
                return after

            return lower_cells(row, link_cell, after)

        repeat(n, link_row, jnp.int32(codes))

        def list_pair(pair, code):
            code = following[code]
            held = jnp.minimum(code, codes - 1)
            high, low = lax.div(held, n), lax.rem(held, n)
            edge_row[2 * pair] = high
            edge_col[2 * pair] = low
            edge_tag[2 * pair] = jnp.where(code < codes, high, -1)
            edge_row[2 * pair + 1] = low
            edge_col[2 * pair + 1] = high
            edge_tag[2 * pair + 1] = jnp.where(code < codes, low, -1)
            return code + 1

        repeat(most // 2, list_pair, jnp.int32(0))
        shares[blank] = jnp.zeros((HEAD_DIM, rows), jnp.float32)

        def keep_block(slot, carry):
            block = inbox[slot]
            t_part, s_part = masked(block)
            left[slot, pl.ds(0, rows), :] = t_part
            left[slot, pl.ds(rows, rows), :] = s_part
            turned[slot] = block.T[HEAD_DIM:]
            return carry

        def take_chip(shift, carry):
            if isinstance(shift, int) and shift == 0:
                all_of(inbox, 1, 1, recv_sem.at[0]).wait_recv()
            else:
                all_of(inbox, 2 * shift, 2, recv_sem.at[shift]).wait_recv()
            for inner in range(2):
                keep_block(2 * shift + inner, None)
            return carry

        take_chip(0, None)
        if chips > 16:
            lax.fori_loop(1, chips, take_chip, None)
        else:
            for shift in range(1, chips):
                take_chip(shift, None)

        def measure_edge(edge, carry):
            t_exp, s_exp, lines = measured(*tile(left[edge_col[edge]], inbox[edge_row[edge]]))
            for line_at, line in enumerate(lines):
                stats[line_at, pl.ds(edge, 1), :] = line
            if keep:
                exps[edge, 0] = t_exp
                exps[edge, 1] = s_exp
            return carry

        repeat(most, measure_edge)

        all_of(arrived, 1, n - 1, stat_recv).wait_recv()
        slot_row = lax.broadcasted_iota(jnp.int32, (n, rows), 0)

        def place_stats(slot, carry):
            return tuple(
                jnp.where(slot_row == slot, arrived[slot, pl.ds(line_at, 1), :], line)
                for line_at, line in enumerate(carry)
            )

        blank_lines = jnp.zeros((n, rows), jnp.float32)
        first_stats = repeat(n, place_stats, (blank_lines,) * 5)

        def raise_peaks(edge, carry):
            mine = slot_row == edge_tag[edge]
            at = pl.ds(edge, 1)
            return tuple(
                jnp.maximum(peak, jnp.where(mine, stats[which, at, :], floor_value))
                for which, peak in enumerate(carry)
            )

        tops = repeat(most, raise_peaks, first_stats[:2])
        for which in range(2):
            peaks[which] = tops[which]
        first_parts = [
            jnp.exp2((first_stats[which] - tops[which]) * score_factor) for which in range(2)
        ]
        sums = (
            first_parts[0] * first_stats[2],
            first_parts[0] * first_stats[4],
            first_parts[1] * first_stats[3],
        )

        def add_edge(edge, carry):
            tag = edge_tag[edge]
            mine = slot_row == tag
            at = pl.ds(edge, 1)
            fresh = []
            for which in range(2):
                peak = peaks[which, pl.ds(jnp.maximum(tag, 0), 1), :]
                part = jnp.exp2(jnp.minimum((stats[which, at, :] - peak) * score_factor, 0.0))
                weights[which, at, :] = part
                fresh.append(part * stats[2 + which, at, :])
                if which == 0:
                    fresh.append(part * stats[4, at, :])
            return tuple(
                total + jnp.where(mine, piece, 0.0)
                for total, piece in zip(carry, fresh, strict=True)
            )

        t_sum, cross, s_sum = repeat(most, add_edge, sums)
        t_inverse, s_inverse = 1.0 / t_sum, 1.0 / s_sum
        inverses[0] = t_inverse
        inverses[1] = s_inverse

        def weigh_edge(edge, carry):
            tag = edge_tag[edge]
            at, mine_at = pl.ds(edge, 1), pl.ds(jnp.maximum(tag, 0), 1)
            valid = jnp.where(tag >= 0, 1.0, 0.0)
            for which in range(2):
                weights[which, at, :] = weights[which, at, :] * (
                    inverses[which, mine_at, :] * valid
                )
            return carry

        repeat(most, weigh_edge)

        def split(value):
            first = value.astype(jnp.bfloat16).astype(jnp.float32)
            second = (value - first).astype(jnp.bfloat16).astype(jnp.float32)
            return [first, second, value - first - second]

        for which in range(2):
            for at, piece in enumerate(split(first_parts[which] * inverses[which])):
                pieces[3 * which + at] = piece
        total = (
            (cross * t_inverse - tops[0] + tops[1]) * score_factor
            - jnp.log2(t_sum)
            + jnp.log2(s_sum)
        )
        total = jnp.sum(jnp.sum(total, axis=0, keepdims=True), axis=1, keepdims=True) * (
            math.log(2.0) / (rows * n)
        )
        note_row = lax.broadcasted_iota(jnp.int32, (NOTE_ROWS, LANES), 0)
        base = jnp.zeros((NOTE_ROWS, LANES), jnp.float32)
        for at, piece in enumerate(split(total)):
            base = jnp.where(note_row == at, piece, base)

        def send_note(step, carry):
            slot = n - 1 - step
            note = base
            for at in range(6):
                note = jnp.where(note_row == 3 + at, pieces[at, pl.ds(slot, 1), :], note)
            out_note[slot] = note.astype(jnp.bfloat16)

            @pl.when(slot > 0)
            def start_note():
                note_copy(slot, place(slot)).start()

            return carry

        repeat(n, send_note)

        def gap_of(edge, col, row):
            at = pl.ds(edge, 1)
            if keep:
                t_exp, s_exp = exps[edge, 0], exps[edge, 1]
            else:
                t_raw, s_raw = tile(left[col], inbox[row])
                t_exp = jnp.exp2((t_raw - stats[0, at, :]) * score_factor)
                s_exp = jnp.exp2((s_raw - stats[1, at, :]) * score_factor)
            return s_exp * weights[1, at, :] - t_exp * weights[0, at, :]

        def share_pair(pair, carry):
            high, low = edge_row[2 * pair], edge_col[2 * pair]
            gap = gap_of(2 * pair, low, high)
            back = gap_of(2 * pair + 1, high, low)
            symmetric = (gap + back.T).astype(jnp.bfloat16)
            shares[2 * pair] = jnp.dot(turned[low], symmetric, preferred_element_type=jnp.float32)
            shares[2 * pair + 1] = lax.dot_general(
                turned[high], symmetric, (((1,), (1,)), ((), ())),
                preferred_element_type=jnp.float32,
            )
            return carry

        repeat(most // 2, share_pair)

        def finish(step, carry):
            slot = n - 1 - step

            def add_share(turn, line):
                fresh = shares[edge_of[slot * n + (slot + turn + 1) % n]]
                return fresh if line is None else line + fresh

            line = repeat(n - 1, add_share, None if n <= 16 else jnp.zeros((HEAD_DIM, rows), jnp.float32))
            out_grad[slot] = (line * (distill_weight * HEAD_DIM ** (-0.5))).astype(jnp.bfloat16)

            @pl.when(slot > 0)
            def send_grad():
                grad_copy(slot, place(slot)).start()

            return carry

        repeat(n, finish)
        in_note[head] = out_note[0]
        in_grad[head] = out_grad[0]

    def take(buffers, sem):
        @pl.when(is_worker)
        def take_others():
            all_of(buffers, 0, heads - 1, sem).wait_recv()

        @pl.when(jnp.logical_not(is_worker))
        def take_all():
            all_of(buffers, 0, heads, sem).wait_recv()

    take(in_note, note_recv)
    for turn in range(heads):
        note = in_note[turn].astype(jnp.float32)
        t_weight = note[3:4] + note[4:5] + note[5:6]
        s_weight = note[6:7] + note[7:8] + note[8:9]
        gap = own_exps[turn, 1] * s_weight - own_exps[turn, 0] * t_weight
        symmetric = (gap + gap.T).astype(jnp.bfloat16)
        near[turn] = jnp.dot(own_turned[turn], symmetric, preferred_element_type=jnp.float32) * (
            distill_weight * HEAD_DIM ** (-0.5)
        )
        div_out[pl.ds(turn, 1), :] = note[0:1] + note[1:2] + note[2:3]
    @pl.when(is_worker)
    def drain_worker():
        all_of(outbox, 0, heads - 1, send_sem).wait_send()
        all_of(own_stats, 0, heads - 1, stat_send).wait_send()
        all_of(out_note, 1, n - 1, note_send).wait_send()
        all_of(out_grad, 1, n - 1, back_send).wait_send()

    @pl.when(jnp.logical_not(is_worker))
    def drain_server():
        all_of(outbox, 0, heads, send_sem).wait_send()
        all_of(own_stats, 0, heads, stat_send).wait_send()

    take(in_grad, back_recv)
    for turn in range(heads):
        grad_out[turn] = (in_grad[turn].astype(jnp.float32) + near[turn]).astype(jnp.bfloat16)


def unpack(in_grad, in_div, grad_ref, div_ref):
    heads = in_grad.shape[0]
    group = LANES // HEAD_DIM
    for pair in range(heads // group):
        both = jnp.concatenate([in_grad[pair * group + inner] for inner in range(group)], axis=0)
        grad_ref[:, pl.ds(pair * LANES, LANES)] = both.T
    div_lane = lax.broadcasted_iota(jnp.int32, (1, LANES), 1)
    div_row = jnp.zeros((1, LANES), jnp.float32)
    for slot in range(heads):
        div_row = jnp.where(div_lane == slot, in_div[pl.ds(slot, 1), :], div_row)
    div_ref[...] = div_row[:, :heads]


def per_device(n, teacher_q, student_q, owner_table):
    rows, width = teacher_q.shape
    heads = width // HEAD_DIM
    chips = n // 2
    owned = n // heads
    most = 2 * (n * owned - n)
    keep = most * 2 * rows * rows * 4 <= KEEP_BYTES
    hbm = pl.BlockSpec(memory_space=pl.ANY)
    vmem = pl.BlockSpec(memory_space=pltpu.VMEM)
    packed = pl.pallas_call(
        functools.partial(kernel, n, most, keep),
        out_shape=(
            pltpu.VMEM((heads, HEAD_DIM, rows), jnp.bfloat16),
            pltpu.VMEM((heads, rows), jnp.float32),
        ),
        in_specs=[hbm, hbm, hbm],
        out_specs=(vmem, vmem),
        scratch_shapes=[
            pltpu.VMEM((rows, width), jnp.bfloat16),
            pltpu.VMEM((rows, width), jnp.bfloat16),
            pltpu.VMEM((heads, rows, LANES), jnp.bfloat16),
            pltpu.VMEM((heads, HEAD_DIM, rows), jnp.bfloat16),
            pltpu.VMEM((heads, 2, rows, rows), jnp.float32),
            pltpu.VMEM((heads, 8, rows), jnp.float32),
            pltpu.VMEM((n, rows, LANES), jnp.bfloat16),
            pltpu.VMEM((n, 2 * rows, LANES), jnp.bfloat16),
            pltpu.VMEM((n, HEAD_DIM, rows), jnp.bfloat16),
            pltpu.VMEM((n, 8, rows), jnp.float32),
            pltpu.SMEM((n, n), jnp.int32),
            pltpu.SMEM((n * n + 2,), jnp.int32),
            pltpu.SMEM((n * n,), jnp.int32),
            pltpu.SMEM((most,), jnp.int32),
            pltpu.SMEM((most,), jnp.int32),
            pltpu.SMEM((most,), jnp.int32),
            pltpu.VMEM((5, most, rows), jnp.float32),
            pltpu.VMEM((2, n, rows), jnp.float32),
            pltpu.VMEM((2, n, rows), jnp.float32),
            pltpu.VMEM((2, most, rows), jnp.float32),
            pltpu.VMEM((6, n, rows), jnp.float32),
            pltpu.VMEM((most if keep else 1, 2, rows, rows), jnp.float32),
            pltpu.VMEM((most + 1, HEAD_DIM, rows), jnp.float32),
            pltpu.VMEM((n, NOTE_ROWS, rows), jnp.bfloat16),
            pltpu.VMEM((heads, NOTE_ROWS, rows), jnp.bfloat16),
            pltpu.VMEM((n, HEAD_DIM, rows), jnp.bfloat16),
            pltpu.VMEM((heads, HEAD_DIM, rows), jnp.bfloat16),
            pltpu.VMEM((heads, HEAD_DIM, rows), jnp.float32),
            pltpu.SemaphoreType.DMA((2,)),
            pltpu.SemaphoreType.DMA,
            pltpu.SemaphoreType.DMA,
            pltpu.SemaphoreType.DMA((chips,)),
            pltpu.SemaphoreType.DMA,
            pltpu.SemaphoreType.DMA,
            pltpu.SemaphoreType.DMA,
            pltpu.SemaphoreType.DMA,
            pltpu.SemaphoreType.DMA,
            pltpu.SemaphoreType.DMA,
        ],
        compiler_params=pltpu.CompilerParams(
            collective_id=0, has_side_effects=True, vmem_limit_bytes=60 * 1024 * 1024
        ),
        name="distill",
    )(*[pltpu.with_memory_space_constraint(x, pltpu.HBM) for x in (teacher_q, student_q, owner_table)])
    grad, divergence = pl.pallas_call(
        unpack,
        out_shape=(
            jax.ShapeDtypeStruct((rows, width), jnp.bfloat16),
            jax.ShapeDtypeStruct((1, heads), jnp.float32),
        ),
        in_specs=[vmem, vmem],
        out_specs=(vmem, vmem),
        compiler_params=pltpu.CompilerParams(vmem_limit_bytes=4 * 1024 * 1024),
        name="unpack",
    )(*packed)
    return (grad, divergence.reshape(heads))


def solution(mesh):
    placed = (P("tok", "head"), P("tok", "head"), P())
    return jax.shard_map(
        functools.partial(per_device, mesh.shape["tok"]),
        mesh=mesh,
        in_specs=placed,
        out_specs=(P("tok", "head"), P("head")),
        check_vma=False,
    )
```

```python
import functools
import math

import jax
import jax.numpy as jnp
from jax import lax
from jax.experimental import pallas as pl
from jax.experimental.pallas import tpu as pltpu
from jax.sharding import PartitionSpec as P

HEAD_DIM = 64
LANES = 128
NOTE_ROWS = 16
KEEP_BYTES = 16 * 1024 * 1024
floor_value = -3e38
distill_weight = 32.0
score_factor = HEAD_DIM ** (-0.5) * math.log2(math.e)
MESH = pl.DeviceIdType.MESH


def repeat(count, body, init=None):
    if count <= 16:
        for step in range(count):
            init = body(step, init)
        return init
    return lax.fori_loop(0, count, body, init)


def kernel(
    n, most, keep, teacher_hbm, student_hbm, table_hbm, grad_out, div_out,
    queries, outbox, own_turned, own_exps, own_stats, inbox, left, turned, arrived,
    table, following, edge_of, edge_row, edge_col, edge_tag,
    stats, peaks, inverses, weights, pieces, exps, shares, out_note, in_note, out_grad, in_grad, near,
    load_sem, table_sem, send_sem, recv_sem, stat_send, stat_recv, note_send, note_recv,
    back_send, back_recv,
):
    rows, width = teacher_hbm.shape
    pairs = width // LANES
    heads = width // HEAD_DIM
    group = LANES // HEAD_DIM
    parts = n // heads
    chips = n // 2

    def worker_of(of_head):
        return jnp.where(of_head == 0, 0, of_head * parts + 1)

    me = lax.axis_index("tok")
    head_at = lax.axis_index("head")
    chip, core = lax.div(me, 2), lax.rem(me, 2)
    head = lax.div(me, parts)
    is_worker = me == worker_of(head)
    way = 1 - 2 * lax.rem(chip, 2)

    def place(step):
        shift, flip = (step // 2, step % 2) if isinstance(step, int) else (lax.div(step, 2), lax.rem(step, 2))
        return 2 * lax.rem(chip + way * shift + chips, chips) + lax.rem(core + flip, 2)

    def place_in(worker):
        worker_chip = lax.div(worker, 2)
        worker_way = 1 - 2 * lax.rem(worker_chip, 2)
        shift = lax.rem(worker_way * (chip - worker_chip) + chips, chips)
        return 2 * shift + lax.rem(core + lax.rem(worker, 2), 2)

    def remote(src, dst, send, recv, target):
        return pltpu.make_async_remote_copy(
            src_ref=src, dst_ref=dst, send_sem=send, recv_sem=recv,
            device_id=(head_at, target), device_id_type=MESH,
        )

    barrier = pltpu.get_barrier_semaphore()
    loads = [
        pltpu.make_async_copy(source, queries.at[at], load_sem)
        for at, source in enumerate((teacher_hbm, student_hbm))
    ]
    for load in loads:
        load.start()
    table_load = pltpu.make_async_copy(table_hbm, table, table_sem)
    table_load.start()

    def greet(target):
        pl.semaphore_signal(barrier, inc=1, device_id=(head_at, target), device_id_type=MESH)

    @pl.when(is_worker)
    def greet_all():
        def greet_one(step, carry):
            greet(place(n - 1 - step))
            return carry

        repeat(n - 1, greet_one)

    @pl.when(jnp.logical_not(is_worker))
    def greet_workers():
        for step in range(heads):
            greet(worker_of(lax.rem(head + heads - 1 - step, heads)))

    pltpu.make_async_copy(queries, queries, load_sem).wait()
    teacher, student = queries.at[0], queries.at[1]
    lane = lax.broadcasted_iota(jnp.int32, (rows, LANES), 1)
    lower = lane < HEAD_DIM
    none = jnp.zeros((), jnp.bfloat16)
    for pair in range(pairs):
        columns = pl.ds(pair * LANES, LANES)
        t_pair = teacher[:, columns].astype(jnp.float32)
        s_pair = student[:, columns].astype(jnp.float32)
        outbox[pair * group] = jnp.where(lower, t_pair, pltpu.roll(s_pair, HEAD_DIM, 1)).astype(
            jnp.bfloat16
        )
        outbox[pair * group + 1] = jnp.where(
            lower, pltpu.roll(t_pair, HEAD_DIM, 1), s_pair
        ).astype(jnp.bfloat16)

    def query_copy(to_head, slot):
        return remote(
            outbox.at[to_head], inbox.at[slot], send_sem, recv_sem.at[lax.div(slot, n // 2)],
            worker_of(to_head),
        )

    def stat_copy(to_head, slot):
        return remote(
            own_stats.at[to_head], arrived.at[slot], stat_send, stat_recv,
            worker_of(to_head),
        )

    def grad_copy(slot, target):
        return remote(
            out_grad.at[slot], in_grad.at[head], back_send, back_recv, target
        )

    def note_copy(slot, target):
        return remote(
            out_note.at[slot], in_note.at[head], note_send, note_recv, target
        )

    def all_of(ref, first, count, sem):
        whole = ref.at[pl.ds(first, count)]
        return remote(whole, whole, sem, sem, me)

    others = [lax.rem(head + way * step + heads, heads) for step in (3, 1, 2)]
    slots = [place_in(worker_of(to_head)) for to_head in others]
    pl.semaphore_wait(barrier, jnp.where(is_worker, n - 1, heads))
    for to_head, slot in zip(others, slots, strict=True):
        query_copy(to_head, slot).start()

    @pl.when(jnp.logical_not(is_worker))
    def send_near():
        query_copy(head, place_in(worker_of(head))).start()

    def masked(block):
        return jnp.where(lower, block, none), jnp.where(lower, none, block)

    def tile(both, block):
        raw = lax.dot_general(
            both, block, (((1,), (1,)), ((), ())), preferred_element_type=jnp.float32
        )
        return raw[:rows], raw[rows:]

    def measured(t_raw, s_raw):
        t_top = jnp.max(t_raw, axis=0, keepdims=True)
        s_top = jnp.max(s_raw, axis=0, keepdims=True)
        t_exp = jnp.exp2((t_raw - t_top) * score_factor)
        s_exp = jnp.exp2((s_raw - s_top) * score_factor)
        lines = (
            t_top,
            s_top,
            jnp.sum(t_exp, axis=0, keepdims=True),
            jnp.sum(s_exp, axis=0, keepdims=True),
            jnp.sum(t_exp * (t_raw - s_raw), axis=0, keepdims=True),
        )
        return t_exp, s_exp, lines

    for turn in range(heads):
        block = outbox[turn]
        own_turned[turn] = block.T[HEAD_DIM:]
        t_exp, s_exp, lines = measured(*tile(jnp.concatenate(masked(block), axis=0), block))
        own_exps[turn, 0] = t_exp
        own_exps[turn, 1] = s_exp
        for line_at, line in enumerate(lines):
            own_stats[turn, pl.ds(line_at, 1), :] = line
        own_stats[turn, pl.ds(len(lines), 8 - len(lines)), :] = jnp.zeros(
            (8 - len(lines), rows), jnp.float32
        )
    for to_head, slot in zip(others, slots, strict=True):
        stat_copy(to_head, slot).start()
    table_load.wait()

    @pl.when(jnp.logical_not(is_worker))
    def send_near_stats():
        stat_copy(head, place_in(worker_of(head))).start()

    @pl.when(is_worker)
    def work():
        inbox[0] = outbox[head]
        arrived[0] = own_stats[head]
        codes = n * n
        blank = most

        def lower_cells(row, body, init):
            if isinstance(row, int):
                for col in range(row):
                    init = body(col, init)
                return init
            return lax.fori_loop(0, row, body, init)

        def count_row(row, count):
            row_at = place(row)

            def count_cell(col, count):
                inside = table[row_at, place(col)] >= 0
                edge = jnp.minimum(2 * count, most - 2)
                edge_of[row * n + col] = jnp.where(inside, edge, blank)
                edge_of[col * n + row] = jnp.where(inside, edge + 1, blank)
                return count + jnp.where(inside, 1, 0)

            return lower_cells(row, count_cell, count)

        repeat(n, count_row, jnp.int32(0))
        following[codes] = jnp.int32(codes)
        following[codes + 1] = jnp.int32(codes)

        def link_row(step, after):
            row = n - 1 - step
            row_at = place(row)
            following[row * n + row] = after

            def link_cell(back, after):
                col = row - 1 - back
                code = row * n + col
                after = jnp.where(table[row_at, place(col)] >= 0, code, after)
                following[code] = after
                return after

            return lower_cells(row, link_cell, after)

        repeat(n, link_row, jnp.int32(codes))

        def list_pair(pair, code):
            code = following[code]
            held = jnp.minimum(code, codes - 1)
            high, low = lax.div(held, n), lax.rem(held, n)
            edge_row[2 * pair] = high
            edge_col[2 * pair] = low
            edge_tag[2 * pair] = jnp.where(code < codes, high, -1)
            edge_row[2 * pair + 1] = low
            edge_col[2 * pair + 1] = high
            edge_tag[2 * pair + 1] = jnp.where(code < codes, low, -1)
            return code + 1

        repeat(most // 2, list_pair, jnp.int32(0))
        shares[blank] = jnp.zeros((HEAD_DIM, rows), jnp.float32)

        def keep_block(slot, carry):
            block = inbox[slot]
            t_part, s_part = masked(block)
            left[slot, pl.ds(0, rows), :] = t_part
            left[slot, pl.ds(rows, rows), :] = s_part
            turned[slot] = block.T[HEAD_DIM:]
            return carry

        half = n // 2
        all_of(inbox, 1, half - 1, recv_sem.at[0]).wait_recv()
        repeat(half, keep_block)
        all_of(inbox, half, half, recv_sem.at[1]).wait_recv()
        repeat(half, lambda step, carry: keep_block(half + step, carry))

        def measure_edge(edge, carry):
            t_exp, s_exp, lines = measured(*tile(left[edge_col[edge]], inbox[edge_row[edge]]))
            for line_at, line in enumerate(lines):
                stats[line_at, pl.ds(edge, 1), :] = line
            if keep:
                exps[edge, 0] = t_exp
                exps[edge, 1] = s_exp
            return carry

        repeat(most, measure_edge)

        all_of(arrived, 1, n - 1, stat_recv).wait_recv()
        slot_row = lax.broadcasted_iota(jnp.int32, (n, rows), 0)

        def place_stats(slot, carry):
            return tuple(
                jnp.where(slot_row == slot, arrived[slot, pl.ds(line_at, 1), :], line)
                for line_at, line in enumerate(carry)
            )

        blank_lines = jnp.zeros((n, rows), jnp.float32)
        first_stats = repeat(n, place_stats, (blank_lines,) * 5)

        def raise_peaks(edge, carry):
            mine = slot_row == edge_tag[edge]
            at = pl.ds(edge, 1)
            return tuple(
                jnp.maximum(peak, jnp.where(mine, stats[which, at, :], floor_value))
                for which, peak in enumerate(carry)
            )

        tops = repeat(most, raise_peaks, first_stats[:2])
        for which in range(2):
            peaks[which] = tops[which]
        first_parts = [
            jnp.exp2((first_stats[which] - tops[which]) * score_factor) for which in range(2)
        ]
        sums = (
            first_parts[0] * first_stats[2],
            first_parts[0] * first_stats[4],
            first_parts[1] * first_stats[3],
        )

        def add_edge(edge, carry):
            tag = edge_tag[edge]
            mine = slot_row == tag
            at = pl.ds(edge, 1)
            fresh = []
            for which in range(2):
                peak = peaks[which, pl.ds(jnp.maximum(tag, 0), 1), :]
                part = jnp.exp2(jnp.minimum((stats[which, at, :] - peak) * score_factor, 0.0))
                weights[which, at, :] = part
                fresh.append(part * stats[2 + which, at, :])
                if which == 0:
                    fresh.append(part * stats[4, at, :])
            return tuple(
                total + jnp.where(mine, piece, 0.0)
                for total, piece in zip(carry, fresh, strict=True)
            )

        t_sum, cross, s_sum = repeat(most, add_edge, sums)
        t_inverse, s_inverse = 1.0 / t_sum, 1.0 / s_sum
        inverses[0] = t_inverse
        inverses[1] = s_inverse

        def weigh_edge(edge, carry):
            tag = edge_tag[edge]
            at, mine_at = pl.ds(edge, 1), pl.ds(jnp.maximum(tag, 0), 1)
            valid = jnp.where(tag >= 0, 1.0, 0.0)
            for which in range(2):
                weights[which, at, :] = weights[which, at, :] * (
                    inverses[which, mine_at, :] * valid
                )
            return carry

        repeat(most, weigh_edge)

        def split(value):
            first = value.astype(jnp.bfloat16).astype(jnp.float32)
            second = (value - first).astype(jnp.bfloat16).astype(jnp.float32)
            return [first, second, value - first - second]

        for which in range(2):
            for at, piece in enumerate(split(first_parts[which] * inverses[which])):
                pieces[3 * which + at] = piece
        total = (
            (cross * t_inverse - tops[0] + tops[1]) * score_factor
            - jnp.log2(t_sum)
            + jnp.log2(s_sum)
        )
        total = jnp.sum(jnp.sum(total, axis=0, keepdims=True), axis=1, keepdims=True) * (
            math.log(2.0) / (rows * n)
        )
        note_row = lax.broadcasted_iota(jnp.int32, (NOTE_ROWS, LANES), 0)
        base = jnp.zeros((NOTE_ROWS, LANES), jnp.float32)
        for at, piece in enumerate(split(total)):
            base = jnp.where(note_row == at, piece, base)

        def send_note(step, carry):
            slot = n - 1 - step
            note = base
            for at in range(6):
                note = jnp.where(note_row == 3 + at, pieces[at, pl.ds(slot, 1), :], note)
            out_note[slot] = note.astype(jnp.bfloat16)

            @pl.when(slot > 0)
            def start_note():
                note_copy(slot, place(slot)).start()

            return carry

        repeat(n, send_note)

        def gap_of(edge, col, row):
            at = pl.ds(edge, 1)
            if keep:
                t_exp, s_exp = exps[edge, 0], exps[edge, 1]
            else:
                t_raw, s_raw = tile(left[col], inbox[row])
                t_exp = jnp.exp2((t_raw - stats[0, at, :]) * score_factor)
                s_exp = jnp.exp2((s_raw - stats[1, at, :]) * score_factor)
            return s_exp * weights[1, at, :] - t_exp * weights[0, at, :]

        def share_pair(pair, carry):
            high, low = edge_row[2 * pair], edge_col[2 * pair]
            gap = gap_of(2 * pair, low, high)
            back = gap_of(2 * pair + 1, high, low)
            symmetric = (gap + back.T).astype(jnp.bfloat16)
            shares[2 * pair] = jnp.dot(turned[low], symmetric, preferred_element_type=jnp.float32)
            shares[2 * pair + 1] = lax.dot_general(
                turned[high], symmetric, (((1,), (1,)), ((), ())),
                preferred_element_type=jnp.float32,
            )
            return carry

        repeat(most // 2, share_pair)

        def finish(step, carry):
            slot = n - 1 - step

            def add_share(turn, line):
                fresh = shares[edge_of[slot * n + (slot + turn + 1) % n]]
                return fresh if line is None else line + fresh

            line = repeat(n - 1, add_share, None if n <= 16 else jnp.zeros((HEAD_DIM, rows), jnp.float32))
            out_grad[slot] = (line * (distill_weight * HEAD_DIM ** (-0.5))).astype(jnp.bfloat16)

            @pl.when(slot > 0)
            def send_grad():
                grad_copy(slot, place(slot)).start()

            return carry

        repeat(n, finish)
        in_note[head] = out_note[0]
        in_grad[head] = out_grad[0]

    def take(buffers, sem):
        @pl.when(is_worker)
        def take_others():
            all_of(buffers, 0, heads - 1, sem).wait_recv()

        @pl.when(jnp.logical_not(is_worker))
        def take_all():
            all_of(buffers, 0, heads, sem).wait_recv()

    take(in_note, note_recv)
    for turn in range(heads):
        note = in_note[turn].astype(jnp.float32)
        t_weight = note[3:4] + note[4:5] + note[5:6]
        s_weight = note[6:7] + note[7:8] + note[8:9]
        gap = own_exps[turn, 1] * s_weight - own_exps[turn, 0] * t_weight
        symmetric = (gap + gap.T).astype(jnp.bfloat16)
        near[turn] = jnp.dot(own_turned[turn], symmetric, preferred_element_type=jnp.float32) * (
            distill_weight * HEAD_DIM ** (-0.5)
        )
        div_out[pl.ds(turn, 1), :] = note[0:1] + note[1:2] + note[2:3]
    @pl.when(is_worker)
    def drain_worker():
        all_of(outbox, 0, heads - 1, send_sem).wait_send()
        all_of(own_stats, 0, heads - 1, stat_send).wait_send()
        all_of(out_note, 1, n - 1, note_send).wait_send()
        all_of(out_grad, 1, n - 1, back_send).wait_send()

    @pl.when(jnp.logical_not(is_worker))
    def drain_server():
        all_of(outbox, 0, heads, send_sem).wait_send()
        all_of(own_stats, 0, heads, stat_send).wait_send()

    take(in_grad, back_recv)
    for turn in range(heads):
        grad_out[turn] = (in_grad[turn].astype(jnp.float32) + near[turn]).astype(jnp.bfloat16)


def unpack(in_grad, in_div, grad_ref, div_ref):
    heads = in_grad.shape[0]
    group = LANES // HEAD_DIM
    for pair in range(heads // group):
        both = jnp.concatenate([in_grad[pair * group + inner] for inner in range(group)], axis=0)
        grad_ref[:, pl.ds(pair * LANES, LANES)] = both.T
    div_lane = lax.broadcasted_iota(jnp.int32, (1, LANES), 1)
    div_row = jnp.zeros((1, LANES), jnp.float32)
    for slot in range(heads):
        div_row = jnp.where(div_lane == slot, in_div[pl.ds(slot, 1), :], div_row)
    div_ref[...] = div_row[:, :heads]


def per_device(n, teacher_q, student_q, owner_table):
    rows, width = teacher_q.shape
    heads = width // HEAD_DIM
    owned = n // heads
    most = 2 * (n * owned - n)
    keep = most * 2 * rows * rows * 4 <= KEEP_BYTES
    hbm = pl.BlockSpec(memory_space=pl.ANY)
    vmem = pl.BlockSpec(memory_space=pltpu.VMEM)
    packed = pl.pallas_call(
        functools.partial(kernel, n, most, keep),
        out_shape=(
            pltpu.VMEM((heads, HEAD_DIM, rows), jnp.bfloat16),
            pltpu.VMEM((heads, rows), jnp.float32),
        ),
        in_specs=[hbm, hbm, hbm],
        out_specs=(vmem, vmem),
        scratch_shapes=[
            pltpu.VMEM((2, rows, width), jnp.bfloat16),
            pltpu.VMEM((heads, rows, LANES), jnp.bfloat16),
            pltpu.VMEM((heads, HEAD_DIM, rows), jnp.bfloat16),
            pltpu.VMEM((heads, 2, rows, rows), jnp.float32),
            pltpu.VMEM((heads, 8, rows), jnp.float32),
            pltpu.VMEM((n, rows, LANES), jnp.bfloat16),
            pltpu.VMEM((n, 2 * rows, LANES), jnp.bfloat16),
            pltpu.VMEM((n, HEAD_DIM, rows), jnp.bfloat16),
            pltpu.VMEM((n, 8, rows), jnp.float32),
            pltpu.SMEM((n, n), jnp.int32),
            pltpu.SMEM((n * n + 2,), jnp.int32),
            pltpu.SMEM((n * n,), jnp.int32),
            pltpu.SMEM((most,), jnp.int32),
            pltpu.SMEM((most,), jnp.int32),
            pltpu.SMEM((most,), jnp.int32),
            pltpu.VMEM((5, most, rows), jnp.float32),
            pltpu.VMEM((2, n, rows), jnp.float32),
            pltpu.VMEM((2, n, rows), jnp.float32),
            pltpu.VMEM((2, most, rows), jnp.float32),
            pltpu.VMEM((6, n, rows), jnp.float32),
            pltpu.VMEM((most if keep else 1, 2, rows, rows), jnp.float32),
            pltpu.VMEM((most + 1, HEAD_DIM, rows), jnp.float32),
            pltpu.VMEM((n, NOTE_ROWS, rows), jnp.bfloat16),
            pltpu.VMEM((heads, NOTE_ROWS, rows), jnp.bfloat16),
            pltpu.VMEM((n, HEAD_DIM, rows), jnp.bfloat16),
            pltpu.VMEM((heads, HEAD_DIM, rows), jnp.bfloat16),
            pltpu.VMEM((heads, HEAD_DIM, rows), jnp.float32),
            pltpu.SemaphoreType.DMA,
            pltpu.SemaphoreType.DMA,
            pltpu.SemaphoreType.DMA,
            pltpu.SemaphoreType.DMA((2,)),
            pltpu.SemaphoreType.DMA,
            pltpu.SemaphoreType.DMA,
            pltpu.SemaphoreType.DMA,
            pltpu.SemaphoreType.DMA,
            pltpu.SemaphoreType.DMA,
            pltpu.SemaphoreType.DMA,
        ],
        compiler_params=pltpu.CompilerParams(
            collective_id=0, has_side_effects=True, vmem_limit_bytes=60 * 1024 * 1024
        ),
        name="distill",
    )(*[pltpu.with_memory_space_constraint(x, pltpu.HBM) for x in (teacher_q, student_q, owner_table)])
    grad, divergence = pl.pallas_call(
        unpack,
        out_shape=(
            jax.ShapeDtypeStruct((rows, width), jnp.bfloat16),
            jax.ShapeDtypeStruct((1, heads), jnp.float32),
        ),
        in_specs=[vmem, vmem],
        out_specs=(vmem, vmem),
        compiler_params=pltpu.CompilerParams(vmem_limit_bytes=4 * 1024 * 1024),
        name="unpack",
    )(*packed)
    return (grad, divergence.reshape(heads))


def solution(mesh):
    placed = (P("tok", "head"), P("tok", "head"), P())
    return jax.shard_map(
        functools.partial(per_device, mesh.shape["tok"]),
        mesh=mesh,
        in_specs=placed,
        out_specs=(P("tok", "head"), P("head")),
        check_vma=False,
    )
```

```python
import functools
import math

import jax
import jax.numpy as jnp
from jax import lax
from jax.experimental import pallas as pl
from jax.experimental.pallas import tpu as pltpu
from jax.sharding import PartitionSpec as P

HEAD_DIM = 64
LANES = 128
NOTE_ROWS = 16
KEEP_BYTES = 16 * 1024 * 1024
floor_value = -3e38
distill_weight = 32.0
score_factor = HEAD_DIM ** (-0.5) * math.log2(math.e)
MESH = pl.DeviceIdType.MESH


def repeat(count, body, init=None):
    if count <= 16:
        for step in range(count):
            init = body(step, init)
        return init
    return lax.fori_loop(0, count, body, init)


def kernel(
    n, most, keep, teacher_hbm, student_hbm, table_hbm, grad_out, div_out,
    teacher, student, outbox, own_turned, own_exps, own_stats, inbox, left, turned, arrived,
    table, following, edge_of, edge_row, edge_col, edge_tag,
    stats, peaks, inverses, weights, pieces, exps, shares, out_note, in_note, out_grad, in_grad, near,
    load_sem, table_sem, send_sem, recv_sem, stat_send, stat_recv, note_send, note_recv,
    back_send, back_recv,
):
    rows, width = teacher_hbm.shape
    pairs = width // LANES
    heads = width // HEAD_DIM
    group = LANES // HEAD_DIM
    parts = n // heads
    chips = n // 2

    def worker_of(of_head):
        return jnp.where(of_head == 0, 0, of_head * parts + 1)

    me = lax.axis_index("tok")
    head_at = lax.axis_index("head")
    chip, core = lax.div(me, 2), lax.rem(me, 2)
    head = lax.div(me, parts)
    is_worker = me == worker_of(head)
    way = 1 - 2 * lax.rem(chip, 2)

    def place(step):
        shift, flip = (step // 2, step % 2) if isinstance(step, int) else (lax.div(step, 2), lax.rem(step, 2))
        return 2 * lax.rem(chip + way * shift + chips, chips) + lax.rem(core + flip, 2)

    def place_in(worker):
        worker_chip = lax.div(worker, 2)
        worker_way = 1 - 2 * lax.rem(worker_chip, 2)
        shift = lax.rem(worker_way * (chip - worker_chip) + chips, chips)
        return 2 * shift + lax.rem(core + lax.rem(worker, 2), 2)

    def remote(src, dst, send, recv, target):
        return pltpu.make_async_remote_copy(
            src_ref=src, dst_ref=dst, send_sem=send, recv_sem=recv,
            device_id=(head_at, target), device_id_type=MESH,
        )

    barrier = pltpu.get_barrier_semaphore()
    loads = [
        pltpu.make_async_copy(teacher_hbm, teacher, load_sem.at[0]),
        pltpu.make_async_copy(student_hbm, student, load_sem.at[1]),
    ]
    for load in loads:
        load.start()
    table_load = pltpu.make_async_copy(table_hbm, table, table_sem)
    table_load.start()

    def greet(target):
        pl.semaphore_signal(barrier, inc=1, device_id=(head_at, target), device_id_type=MESH)

    @pl.when(is_worker)
    def greet_all():
        def greet_one(step, carry):
            greet(place(n - 1 - step))
            return carry

        repeat(n - 1, greet_one)

    @pl.when(jnp.logical_not(is_worker))
    def greet_workers():
        for step in range(heads):
            greet(worker_of(lax.rem(head + heads - 1 - step, heads)))

    for load in loads:
        load.wait()
    lane = lax.broadcasted_iota(jnp.int32, (rows, LANES), 1)
    lower = lane < HEAD_DIM
    none = jnp.zeros((), jnp.bfloat16)
    for pair in range(pairs):
        columns = pl.ds(pair * LANES, LANES)
        t_pair = teacher[:, columns].astype(jnp.float32)
        s_pair = student[:, columns].astype(jnp.float32)
        outbox[pair * group] = jnp.where(lower, t_pair, pltpu.roll(s_pair, HEAD_DIM, 1)).astype(
            jnp.bfloat16
        )
        outbox[pair * group + 1] = jnp.where(
            lower, pltpu.roll(t_pair, HEAD_DIM, 1), s_pair
        ).astype(jnp.bfloat16)

    def query_copy(to_head, slot):
        return remote(
            outbox.at[to_head], inbox.at[slot], send_sem, recv_sem.at[lax.div(slot, 2)],
            worker_of(to_head),
        )

    def stat_copy(to_head, slot):
        return remote(
            own_stats.at[to_head], arrived.at[slot], stat_send, stat_recv,
            worker_of(to_head),
        )

    def grad_copy(slot, target):
        return remote(
            out_grad.at[slot], in_grad.at[head], back_send, back_recv, target
        )

    def note_copy(slot, target):
        return remote(
            out_note.at[slot], in_note.at[head], note_send, note_recv, target
        )

    def all_of(ref, first, count, sem):
        whole = ref.at[pl.ds(first, count)]
        return remote(whole, whole, sem, sem, me)

    def masked(block):
        return jnp.where(lower, block, none), jnp.where(lower, none, block)

    def tile(both, block):
        raw = lax.dot_general(
            both, block, (((1,), (1,)), ((), ())), preferred_element_type=jnp.float32
        )
        return raw[:rows], raw[rows:]

    def measured(t_raw, s_raw):
        t_top = jnp.max(t_raw, axis=0, keepdims=True)
        s_top = jnp.max(s_raw, axis=0, keepdims=True)
        t_exp = jnp.exp2((t_raw - t_top) * score_factor)
        s_exp = jnp.exp2((s_raw - s_top) * score_factor)
        lines = (
            t_top,
            s_top,
            jnp.sum(t_exp, axis=0, keepdims=True),
            jnp.sum(s_exp, axis=0, keepdims=True),
            jnp.sum(t_exp * (t_raw - s_raw), axis=0, keepdims=True),
        )
        return t_exp, s_exp, lines

    for turn in range(heads):
        block = outbox[turn]
        own_turned[turn] = block.T[HEAD_DIM:]
        t_exp, s_exp, lines = measured(*tile(jnp.concatenate(masked(block), axis=0), block))
        own_exps[turn, 0] = t_exp
        own_exps[turn, 1] = s_exp
        for line_at, line in enumerate(lines):
            own_stats[turn, pl.ds(line_at, 1), :] = line
        own_stats[turn, pl.ds(len(lines), 8 - len(lines)), :] = jnp.zeros(
            (8 - len(lines), rows), jnp.float32
        )
    others = [lax.rem(head + way * step + heads, heads) for step in (3, 1, 2)]
    slots = [place_in(worker_of(to_head)) for to_head in others]
    pl.semaphore_wait(barrier, jnp.where(is_worker, n - 1, heads))
    for to_head, slot in zip(others, slots, strict=True):
        query_copy(to_head, slot).start()

    @pl.when(jnp.logical_not(is_worker))
    def send_near():
        query_copy(head, place_in(worker_of(head))).start()

    for to_head, slot in zip(others, slots, strict=True):
        stat_copy(to_head, slot).start()
    table_load.wait()

    @pl.when(jnp.logical_not(is_worker))
    def send_near_stats():
        stat_copy(head, place_in(worker_of(head))).start()

    @pl.when(is_worker)
    def work():
        inbox[0] = outbox[head]
        arrived[0] = own_stats[head]
        codes = n * n
        blank = most

        def lower_cells(row, body, init):
            if isinstance(row, int):
                for col in range(row):
                    init = body(col, init)
                return init
            return lax.fori_loop(0, row, body, init)

        def count_row(row, count):
            row_at = place(row)

            def count_cell(col, count):
                inside = table[row_at, place(col)] >= 0
                edge = jnp.minimum(2 * count, most - 2)
                edge_of[row * n + col] = jnp.where(inside, edge, blank)
                edge_of[col * n + row] = jnp.where(inside, edge + 1, blank)
                return count + jnp.where(inside, 1, 0)

            return lower_cells(row, count_cell, count)

        repeat(n, count_row, jnp.int32(0))
        following[codes] = jnp.int32(codes)
        following[codes + 1] = jnp.int32(codes)

        def link_row(step, after):
            row = n - 1 - step
            row_at = place(row)
            following[row * n + row] = after

            def link_cell(back, after):
                col = row - 1 - back
                code = row * n + col
                after = jnp.where(table[row_at, place(col)] >= 0, code, after)
                following[code] = after
                return after

            return lower_cells(row, link_cell, after)

        repeat(n, link_row, jnp.int32(codes))

        def list_pair(pair, code):
            code = following[code]
            held = jnp.minimum(code, codes - 1)
            high, low = lax.div(held, n), lax.rem(held, n)
            edge_row[2 * pair] = high
            edge_col[2 * pair] = low
            edge_tag[2 * pair] = jnp.where(code < codes, high, -1)
            edge_row[2 * pair + 1] = low
            edge_col[2 * pair + 1] = high
            edge_tag[2 * pair + 1] = jnp.where(code < codes, low, -1)
            return code + 1

        repeat(most // 2, list_pair, jnp.int32(0))
        shares[blank] = jnp.zeros((HEAD_DIM, rows), jnp.float32)

        def keep_block(slot, carry):
            block = inbox[slot]
            t_part, s_part = masked(block)
            left[slot, pl.ds(0, rows), :] = t_part
            left[slot, pl.ds(rows, rows), :] = s_part
            turned[slot] = block.T[HEAD_DIM:]
            return carry

        def take_chip(shift, carry):
            if isinstance(shift, int) and shift == 0:
                all_of(inbox, 1, 1, recv_sem.at[0]).wait_recv()
            else:
                all_of(inbox, 2 * shift, 2, recv_sem.at[shift]).wait_recv()
            for inner in range(2):
                keep_block(2 * shift + inner, None)
            return carry

        take_chip(0, None)
        if chips > 16:
            lax.fori_loop(1, chips, take_chip, None)
        else:
            for shift in range(1, chips):
                take_chip(shift, None)

        def measure_edge(edge, carry):
            t_exp, s_exp, lines = measured(*tile(left[edge_col[edge]], inbox[edge_row[edge]]))
            for line_at, line in enumerate(lines):
                stats[line_at, pl.ds(edge, 1), :] = line
            if keep:
                exps[edge, 0] = t_exp
                exps[edge, 1] = s_exp
            return carry

        repeat(most, measure_edge)

        all_of(arrived, 1, n - 1, stat_recv).wait_recv()
        slot_row = lax.broadcasted_iota(jnp.int32, (n, rows), 0)

        def place_stats(slot, carry):
            return tuple(
                jnp.where(slot_row == slot, arrived[slot, pl.ds(line_at, 1), :], line)
                for line_at, line in enumerate(carry)
            )

        blank_lines = jnp.zeros((n, rows), jnp.float32)
        first_stats = repeat(n, place_stats, (blank_lines,) * 5)

        def raise_peaks(edge, carry):
            mine = slot_row == edge_tag[edge]
            at = pl.ds(edge, 1)
            return tuple(
                jnp.maximum(peak, jnp.where(mine, stats[which, at, :], floor_value))
                for which, peak in enumerate(carry)
            )

        tops = repeat(most, raise_peaks, first_stats[:2])
        for which in range(2):
            peaks[which] = tops[which]
        first_parts = [
            jnp.exp2((first_stats[which] - tops[which]) * score_factor) for which in range(2)
        ]
        sums = (
            first_parts[0] * first_stats[2],
            first_parts[0] * first_stats[4],
            first_parts[1] * first_stats[3],
        )

        def add_edge(edge, carry):
            tag = edge_tag[edge]
            mine = slot_row == tag
            at = pl.ds(edge, 1)
            fresh = []
            for which in range(2):
                peak = peaks[which, pl.ds(jnp.maximum(tag, 0), 1), :]
                part = jnp.exp2(jnp.minimum((stats[which, at, :] - peak) * score_factor, 0.0))
                weights[which, at, :] = part
                fresh.append(part * stats[2 + which, at, :])
                if which == 0:
                    fresh.append(part * stats[4, at, :])
            return tuple(
                total + jnp.where(mine, piece, 0.0)
                for total, piece in zip(carry, fresh, strict=True)
            )

        t_sum, cross, s_sum = repeat(most, add_edge, sums)
        t_inverse, s_inverse = 1.0 / t_sum, 1.0 / s_sum
        inverses[0] = t_inverse
        inverses[1] = s_inverse

        def weigh_edge(edge, carry):
            tag = edge_tag[edge]
            at, mine_at = pl.ds(edge, 1), pl.ds(jnp.maximum(tag, 0), 1)
            valid = jnp.where(tag >= 0, 1.0, 0.0)
            for which in range(2):
                weights[which, at, :] = weights[which, at, :] * (
                    inverses[which, mine_at, :] * valid
                )
            return carry

        repeat(most, weigh_edge)

        def split(value):
            first = value.astype(jnp.bfloat16).astype(jnp.float32)
            second = (value - first).astype(jnp.bfloat16).astype(jnp.float32)
            return [first, second, value - first - second]

        for which in range(2):
            for at, piece in enumerate(split(first_parts[which] * inverses[which])):
                pieces[3 * which + at] = piece
        total = (
            (cross * t_inverse - tops[0] + tops[1]) * score_factor
            - jnp.log2(t_sum)
            + jnp.log2(s_sum)
        )
        total = jnp.sum(jnp.sum(total, axis=0, keepdims=True), axis=1, keepdims=True) * (
            math.log(2.0) / (rows * n)
        )
        note_row = lax.broadcasted_iota(jnp.int32, (NOTE_ROWS, LANES), 0)
        base = jnp.zeros((NOTE_ROWS, LANES), jnp.float32)
        for at, piece in enumerate(split(total)):
            base = jnp.where(note_row == at, piece, base)

        def send_note(step, carry):
            slot = n - 1 - step
            note = base
            for at in range(6):
                note = jnp.where(note_row == 3 + at, pieces[at, pl.ds(slot, 1), :], note)
            out_note[slot] = note.astype(jnp.bfloat16)

            @pl.when(slot > 0)
            def start_note():
                note_copy(slot, place(slot)).start()

            return carry

        repeat(n, send_note)

        def gap_of(edge, col, row):
            at = pl.ds(edge, 1)
            if keep:
                t_exp, s_exp = exps[edge, 0], exps[edge, 1]
            else:
                t_raw, s_raw = tile(left[col], inbox[row])
                t_exp = jnp.exp2((t_raw - stats[0, at, :]) * score_factor)
                s_exp = jnp.exp2((s_raw - stats[1, at, :]) * score_factor)
            return s_exp * weights[1, at, :] - t_exp * weights[0, at, :]

        def share_pair(pair, carry):
            high, low = edge_row[2 * pair], edge_col[2 * pair]
            gap = gap_of(2 * pair, low, high)
            back = gap_of(2 * pair + 1, high, low)
            symmetric = gap.astype(jnp.bfloat16) + back.astype(jnp.bfloat16).T
            shares[2 * pair] = jnp.dot(turned[low], symmetric, preferred_element_type=jnp.float32)
            shares[2 * pair + 1] = lax.dot_general(
                turned[high], symmetric, (((1,), (1,)), ((), ())),
                preferred_element_type=jnp.float32,
            )
            return carry

        repeat(most // 2, share_pair)

        def finish(step, carry):
            slot = n - 1 - step

            def add_share(turn, line):
                fresh = shares[edge_of[slot * n + (slot + turn + 1) % n]]
                return fresh if line is None else line + fresh

            line = repeat(n - 1, add_share, None if n <= 16 else jnp.zeros((HEAD_DIM, rows), jnp.float32))
            out_grad[slot] = (line * (distill_weight * HEAD_DIM ** (-0.5))).astype(jnp.bfloat16)

            @pl.when(slot > 0)
            def send_grad():
                grad_copy(slot, place(slot)).start()

            return carry

        repeat(n, finish)
        in_note[head] = out_note[0]
        in_grad[head] = out_grad[0]

    def take(buffers, sem):
        @pl.when(is_worker)
        def take_others():
            all_of(buffers, 0, heads - 1, sem).wait_recv()

        @pl.when(jnp.logical_not(is_worker))
        def take_all():
            all_of(buffers, 0, heads, sem).wait_recv()

    take(in_note, note_recv)
    for turn in range(heads):
        note = in_note[turn].astype(jnp.float32)
        t_weight = note[3:4] + note[4:5] + note[5:6]
        s_weight = note[6:7] + note[7:8] + note[8:9]
        gap = own_exps[turn, 1] * s_weight - own_exps[turn, 0] * t_weight
        symmetric = (gap + gap.T).astype(jnp.bfloat16)
        near[turn] = jnp.dot(own_turned[turn], symmetric, preferred_element_type=jnp.float32) * (
            distill_weight * HEAD_DIM ** (-0.5)
        )
        div_out[pl.ds(turn, 1), :] = note[0:1] + note[1:2] + note[2:3]
    @pl.when(is_worker)
    def drain_worker():
        all_of(outbox, 0, heads - 1, send_sem).wait_send()
        all_of(own_stats, 0, heads - 1, stat_send).wait_send()
        all_of(out_note, 1, n - 1, note_send).wait_send()
        all_of(out_grad, 1, n - 1, back_send).wait_send()

    @pl.when(jnp.logical_not(is_worker))
    def drain_server():
        all_of(outbox, 0, heads, send_sem).wait_send()
        all_of(own_stats, 0, heads, stat_send).wait_send()

    take(in_grad, back_recv)
    for turn in range(heads):
        grad_out[turn] = (in_grad[turn].astype(jnp.float32) + near[turn]).astype(jnp.bfloat16)


def unpack(in_grad, in_div, grad_ref, div_ref):
    heads = in_grad.shape[0]
    group = LANES // HEAD_DIM
    for pair in range(heads // group):
        both = jnp.concatenate([in_grad[pair * group + inner] for inner in range(group)], axis=0)
        grad_ref[:, pl.ds(pair * LANES, LANES)] = both.T
    div_lane = lax.broadcasted_iota(jnp.int32, (1, LANES), 1)
    div_row = jnp.zeros((1, LANES), jnp.float32)
    for slot in range(heads):
        div_row = jnp.where(div_lane == slot, in_div[pl.ds(slot, 1), :], div_row)
    div_ref[...] = div_row[:, :heads]


def per_device(n, teacher_q, student_q, owner_table):
    rows, width = teacher_q.shape
    heads = width // HEAD_DIM
    chips = n // 2
    owned = n // heads
    most = 2 * (n * owned - n)
    keep = most * 2 * rows * rows * 4 <= KEEP_BYTES
    hbm = pl.BlockSpec(memory_space=pl.ANY)
    vmem = pl.BlockSpec(memory_space=pltpu.VMEM)
    packed = pl.pallas_call(
        functools.partial(kernel, n, most, keep),
        out_shape=(
            pltpu.VMEM((heads, HEAD_DIM, rows), jnp.bfloat16),
            pltpu.VMEM((heads, rows), jnp.float32),
        ),
        in_specs=[hbm, hbm, hbm],
        out_specs=(vmem, vmem),
        scratch_shapes=[
            pltpu.VMEM((rows, width), jnp.bfloat16),
            pltpu.VMEM((rows, width), jnp.bfloat16),
            pltpu.VMEM((heads, rows, LANES), jnp.bfloat16),
            pltpu.VMEM((heads, HEAD_DIM, rows), jnp.bfloat16),
            pltpu.VMEM((heads, 2, rows, rows), jnp.float32),
            pltpu.VMEM((heads, 8, rows), jnp.float32),
            pltpu.VMEM((n, rows, LANES), jnp.bfloat16),
            pltpu.VMEM((n, 2 * rows, LANES), jnp.bfloat16),
            pltpu.VMEM((n, HEAD_DIM, rows), jnp.bfloat16),
            pltpu.VMEM((n, 8, rows), jnp.float32),
            pltpu.SMEM((n, n), jnp.int32),
            pltpu.SMEM((n * n + 2,), jnp.int32),
            pltpu.SMEM((n * n,), jnp.int32),
            pltpu.SMEM((most,), jnp.int32),
            pltpu.SMEM((most,), jnp.int32),
            pltpu.SMEM((most,), jnp.int32),
            pltpu.VMEM((5, most, rows), jnp.float32),
            pltpu.VMEM((2, n, rows), jnp.float32),
            pltpu.VMEM((2, n, rows), jnp.float32),
            pltpu.VMEM((2, most, rows), jnp.float32),
            pltpu.VMEM((6, n, rows), jnp.float32),
            pltpu.VMEM((most if keep else 1, 2, rows, rows), jnp.float32),
            pltpu.VMEM((most + 1, HEAD_DIM, rows), jnp.float32),
            pltpu.VMEM((n, NOTE_ROWS, rows), jnp.bfloat16),
            pltpu.VMEM((heads, NOTE_ROWS, rows), jnp.bfloat16),
            pltpu.VMEM((n, HEAD_DIM, rows), jnp.bfloat16),
            pltpu.VMEM((heads, HEAD_DIM, rows), jnp.bfloat16),
            pltpu.VMEM((heads, HEAD_DIM, rows), jnp.float32),
            pltpu.SemaphoreType.DMA((2,)),
            pltpu.SemaphoreType.DMA,
            pltpu.SemaphoreType.DMA,
            pltpu.SemaphoreType.DMA((chips,)),
            pltpu.SemaphoreType.DMA,
            pltpu.SemaphoreType.DMA,
            pltpu.SemaphoreType.DMA,
            pltpu.SemaphoreType.DMA,
            pltpu.SemaphoreType.DMA,
            pltpu.SemaphoreType.DMA,
        ],
        compiler_params=pltpu.CompilerParams(
            collective_id=0, has_side_effects=True, vmem_limit_bytes=60 * 1024 * 1024
        ),
        name="distill",
    )(*[pltpu.with_memory_space_constraint(x, pltpu.HBM) for x in (teacher_q, student_q, owner_table)])
    grad, divergence = pl.pallas_call(
        unpack,
        out_shape=(
            jax.ShapeDtypeStruct((rows, width), jnp.bfloat16),
            jax.ShapeDtypeStruct((1, heads), jnp.float32),
        ),
        in_specs=[vmem, vmem],
        out_specs=(vmem, vmem),
        compiler_params=pltpu.CompilerParams(vmem_limit_bytes=4 * 1024 * 1024),
        name="unpack",
    )(*packed)
    return (grad, divergence.reshape(heads))


def solution(mesh):
    placed = (P("tok", "head"), P("tok", "head"), P())
    return jax.shard_map(
        functools.partial(per_device, mesh.shape["tok"]),
        mesh=mesh,
        in_specs=placed,
        out_specs=(P("tok", "head"), P("head")),
        check_vma=False,
    )
```

```python
import functools
import math

import jax
import jax.numpy as jnp
from jax import lax
from jax.experimental import pallas as pl
from jax.experimental.pallas import tpu as pltpu
from jax.sharding import PartitionSpec as P

HEAD_DIM = 64
LANES = 128
NOTE_ROWS = 16
KEEP_BYTES = 16 * 1024 * 1024
floor_value = -3e38
distill_weight = 32.0
score_factor = HEAD_DIM ** (-0.5) * math.log2(math.e)
MESH = pl.DeviceIdType.MESH


def repeat(count, body, init=None):
    if count <= 16:
        for step in range(count):
            init = body(step, init)
        return init
    return lax.fori_loop(0, count, body, init)


def kernel(
    n, most, keep, teacher_hbm, student_hbm, table_hbm, grad_out, div_out,
    teacher, student, outbox, own_turned, own_exps, own_stats, inbox, left, turned, arrived,
    table, following, edge_of, edge_row, edge_col, edge_tag,
    stats, peaks, inverses, weights, pieces, exps, shares, out_note, in_note, out_grad, in_grad, near,
    load_sem, table_sem, send_sem, recv_sem, stat_send, stat_recv, note_send, note_recv,
    back_send, back_recv,
):
    rows, width = teacher_hbm.shape
    pairs = width // LANES
    heads = width // HEAD_DIM
    group = LANES // HEAD_DIM
    parts = n // heads
    chips = n // 2

    def worker_of(of_head):
        return jnp.where(of_head == 0, 0, of_head * parts + 1)

    me = lax.axis_index("tok")
    head_at = lax.axis_index("head")
    chip, core = lax.div(me, 2), lax.rem(me, 2)
    head = lax.div(me, parts)
    is_worker = me == worker_of(head)
    way = 1 - 2 * lax.rem(chip, 2)

    def place(step):
        shift, flip = (step // 2, step % 2) if isinstance(step, int) else (lax.div(step, 2), lax.rem(step, 2))
        return 2 * lax.rem(chip + way * shift + chips, chips) + lax.rem(core + flip, 2)

    def place_in(worker):
        worker_chip = lax.div(worker, 2)
        worker_way = 1 - 2 * lax.rem(worker_chip, 2)
        shift = lax.rem(worker_way * (chip - worker_chip) + chips, chips)
        return 2 * shift + lax.rem(core + lax.rem(worker, 2), 2)

    def remote(src, dst, send, recv, target):
        return pltpu.make_async_remote_copy(
            src_ref=src, dst_ref=dst, send_sem=send, recv_sem=recv,
            device_id=(head_at, target), device_id_type=MESH,
        )

    barrier = pltpu.get_barrier_semaphore()
    loads = [
        pltpu.make_async_copy(teacher_hbm, teacher, load_sem.at[0]),
        pltpu.make_async_copy(student_hbm, student, load_sem.at[1]),
    ]
    for load in loads:
        load.start()
    table_load = pltpu.make_async_copy(table_hbm, table, table_sem)
    table_load.start()

    def greet(target):
        pl.semaphore_signal(barrier, inc=1, device_id=(head_at, target), device_id_type=MESH)

    @pl.when(is_worker)
    def greet_all():
        def greet_one(step, carry):
            greet(place(n - 1 - step))
            return carry

        repeat(n - 1, greet_one)

    @pl.when(jnp.logical_not(is_worker))
    def greet_workers():
        for step in range(heads):
            greet(worker_of(lax.rem(head + heads - 1 - step, heads)))

    for load in loads:
        load.wait()
    lane = lax.broadcasted_iota(jnp.int32, (rows, LANES), 1)
    lower = lane < HEAD_DIM
    none = jnp.zeros((), jnp.bfloat16)
    for pair in range(pairs):
        columns = pl.ds(pair * LANES, LANES)
        t_pair = teacher[:, columns].astype(jnp.float32)
        s_pair = student[:, columns].astype(jnp.float32)
        outbox[pair * group] = jnp.where(lower, t_pair, pltpu.roll(s_pair, HEAD_DIM, 1)).astype(
            jnp.bfloat16
        )
        outbox[pair * group + 1] = jnp.where(
            lower, pltpu.roll(t_pair, HEAD_DIM, 1), s_pair
        ).astype(jnp.bfloat16)

    def query_copy(to_head, slot):
        return remote(
            outbox.at[to_head], inbox.at[slot], send_sem, recv_sem.at[lax.div(slot, 2)],
            worker_of(to_head),
        )

    def stat_copy(to_head, slot):
        return remote(
            own_stats.at[to_head], arrived.at[slot], stat_send, stat_recv,
            worker_of(to_head),
        )

    def grad_copy(slot, target):
        return remote(
            out_grad.at[slot], in_grad.at[head], back_send, back_recv, target
        )

    def note_copy(slot, target):
        return remote(
            out_note.at[slot], in_note.at[head], note_send, note_recv, target
        )

    def all_of(ref, first, count, sem):
        whole = ref.at[pl.ds(first, count)]
        return remote(whole, whole, sem, sem, me)

    others = [lax.rem(head + way * step + heads, heads) for step in (3, 1, 2)]
    slots = [place_in(worker_of(to_head)) for to_head in others]
    pl.semaphore_wait(barrier, jnp.where(is_worker, n - 1, heads))
    for to_head, slot in zip(others, slots, strict=True):
        query_copy(to_head, slot).start()

    @pl.when(jnp.logical_not(is_worker))
    def send_near():
        query_copy(head, place_in(worker_of(head))).start()

    def masked(block):
        return jnp.where(lower, block, none), jnp.where(lower, none, block)

    def tile(both, block):
        raw = lax.dot_general(
            both, block, (((1,), (1,)), ((), ())), preferred_element_type=jnp.float32
        )
        return raw[:rows], raw[rows:]

    def measured(t_raw, s_raw):
        t_top = jnp.max(t_raw, axis=0, keepdims=True)
        s_top = jnp.max(s_raw, axis=0, keepdims=True)
        t_exp = jnp.exp2((t_raw - t_top) * score_factor)
        s_exp = jnp.exp2((s_raw - s_top) * score_factor)
        lines = (
            t_top,
            s_top,
            jnp.sum(t_exp, axis=0, keepdims=True),
            jnp.sum(s_exp, axis=0, keepdims=True),
            jnp.sum(t_exp * (t_raw - s_raw), axis=0, keepdims=True),
        )
        return t_exp, s_exp, lines

    for turn in range(heads):
        block = outbox[turn]
        own_turned[turn] = block.T[HEAD_DIM:]
        t_exp, s_exp, lines = measured(*tile(jnp.concatenate(masked(block), axis=0), block))
        own_exps[turn, 0] = t_exp
        own_exps[turn, 1] = s_exp
        for line_at, line in enumerate(lines):
            own_stats[turn, pl.ds(line_at, 1), :] = line
        own_stats[turn, pl.ds(len(lines), 8 - len(lines)), :] = jnp.zeros(
            (8 - len(lines), rows), jnp.float32
        )
    for to_head, slot in zip(others, slots, strict=True):
        stat_copy(to_head, slot).start()
    table_load.wait()

    @pl.when(jnp.logical_not(is_worker))
    def send_near_stats():
        stat_copy(head, place_in(worker_of(head))).start()

    @pl.when(is_worker)
    def work():
        inbox[0] = outbox[head]
        arrived[0] = own_stats[head]
        codes = n * n
        blank = most

        def lower_cells(row, body, init):
            if isinstance(row, int):
                for col in range(row):
                    init = body(col, init)
                return init
            return lax.fori_loop(0, row, body, init)

        def count_row(row, count):
            row_at = place(row)

            def count_cell(col, count):
                inside = table[row_at, place(col)] >= 0
                edge = jnp.minimum(2 * count, most - 2)
                edge_of[row * n + col] = jnp.where(inside, edge, blank)
                edge_of[col * n + row] = jnp.where(inside, edge + 1, blank)
                return count + jnp.where(inside, 1, 0)

            return lower_cells(row, count_cell, count)

        repeat(n, count_row, jnp.int32(0))
        following[codes] = jnp.int32(codes)
        following[codes + 1] = jnp.int32(codes)

        def link_row(step, after):
            row = n - 1 - step
            row_at = place(row)
            following[row * n + row] = after

            def link_cell(back, after):
                col = row - 1 - back
                code = row * n + col
                after = jnp.where(table[row_at, place(col)] >= 0, code, after)
                following[code] = after
                return after

            return lower_cells(row, link_cell, after)

        repeat(n, link_row, jnp.int32(codes))

        def list_pair(pair, code):
            code = following[code]
            held = jnp.minimum(code, codes - 1)
            high, low = lax.div(held, n), lax.rem(held, n)
            edge_row[2 * pair] = high
            edge_col[2 * pair] = low
            edge_tag[2 * pair] = jnp.where(code < codes, high, -1)
            edge_row[2 * pair + 1] = low
            edge_col[2 * pair + 1] = high
            edge_tag[2 * pair + 1] = jnp.where(code < codes, low, -1)
            return code + 1

        repeat(most // 2, list_pair, jnp.int32(0))
        shares[blank] = jnp.zeros((HEAD_DIM, rows), jnp.float32)

        def keep_block(slot, carry):
            block = inbox[slot]
            t_part, s_part = masked(block)
            left[slot, pl.ds(0, rows), :] = t_part
            left[slot, pl.ds(rows, rows), :] = s_part
            turned[slot] = block.T[HEAD_DIM:]
            return carry

        def take_chip(shift, carry):
            if isinstance(shift, int) and shift == 0:
                all_of(inbox, 1, 1, recv_sem.at[0]).wait_recv()
            else:
                all_of(inbox, 2 * shift, 2, recv_sem.at[shift]).wait_recv()
            for inner in range(2):
                keep_block(2 * shift + inner, None)
            return carry

        take_chip(0, None)
        if chips > 16:
            lax.fori_loop(1, chips, take_chip, None)
        else:
            for shift in range(1, chips):
                take_chip(shift, None)

        def measure_edge(edge, carry):
            t_exp, s_exp, lines = measured(*tile(left[edge_col[edge]], inbox[edge_row[edge]]))
            for line_at, line in enumerate(lines):
                stats[line_at, pl.ds(edge, 1), :] = line
            if keep:
                exps[edge, 0] = t_exp
                exps[edge, 1] = s_exp
            return carry

        repeat(most, measure_edge)

        all_of(arrived, 1, n - 1, stat_recv).wait_recv()
        slot_row = lax.broadcasted_iota(jnp.int32, (n, rows), 0)

        def place_stats(slot, carry):
            return tuple(
                jnp.where(slot_row == slot, arrived[slot, pl.ds(line_at, 1), :], line)
                for line_at, line in enumerate(carry)
            )

        blank_lines = jnp.zeros((n, rows), jnp.float32)
        first_stats = repeat(n, place_stats, (blank_lines,) * 5)

        def raise_peaks(edge, carry):
            mine = slot_row == edge_tag[edge]
            at = pl.ds(edge, 1)
            return tuple(
                jnp.maximum(peak, jnp.where(mine, stats[which, at, :], floor_value))
                for which, peak in enumerate(carry)
            )

        tops = repeat(most, raise_peaks, first_stats[:2])
        for which in range(2):
            peaks[which] = tops[which]
        first_parts = [
            jnp.exp2((first_stats[which] - tops[which]) * score_factor) for which in range(2)
        ]
        sums = (
            first_parts[0] * first_stats[2],
            first_parts[0] * first_stats[4],
            first_parts[1] * first_stats[3],
        )

        def add_edge(edge, carry):
            tag = edge_tag[edge]
            mine = slot_row == tag
            at = pl.ds(edge, 1)
            fresh = []
            for which in range(2):
                peak = peaks[which, pl.ds(jnp.maximum(tag, 0), 1), :]
                part = jnp.exp2(jnp.minimum((stats[which, at, :] - peak) * score_factor, 0.0))
                weights[which, at, :] = part
                fresh.append(part * stats[2 + which, at, :])
                if which == 0:
                    fresh.append(part * stats[4, at, :])
            return tuple(
                total + jnp.where(mine, piece, 0.0)
                for total, piece in zip(carry, fresh, strict=True)
            )

        t_sum, cross, s_sum = repeat(most, add_edge, sums)
        t_inverse, s_inverse = 1.0 / t_sum, 1.0 / s_sum
        inverses[0] = t_inverse
        inverses[1] = s_inverse

        def weigh_edge(edge, carry):
            tag = edge_tag[edge]
            at, mine_at = pl.ds(edge, 1), pl.ds(jnp.maximum(tag, 0), 1)
            valid = jnp.where(tag >= 0, 1.0, 0.0)
            for which in range(2):
                weights[which, at, :] = weights[which, at, :] * (
                    inverses[which, mine_at, :] * valid
                )
            return carry

        repeat(most, weigh_edge)

        def split(value):
            first = value.astype(jnp.bfloat16).astype(jnp.float32)
            second = (value - first).astype(jnp.bfloat16).astype(jnp.float32)
            return [first, second, value - first - second]

        for which in range(2):
            for at, piece in enumerate(split(first_parts[which] * inverses[which])):
                pieces[3 * which + at] = piece
        total = (
            (cross * t_inverse - tops[0] + tops[1]) * score_factor
            - jnp.log2(t_sum)
            + jnp.log2(s_sum)
        )
        total = jnp.sum(jnp.sum(total, axis=0, keepdims=True), axis=1, keepdims=True) * (
            math.log(2.0) / (rows * n)
        )
        note_row = lax.broadcasted_iota(jnp.int32, (NOTE_ROWS, LANES), 0)
        base = jnp.zeros((NOTE_ROWS, LANES), jnp.float32)
        for at, piece in enumerate(split(total)):
            base = jnp.where(note_row == at, piece, base)

        def send_note(step, carry):
            slot = n - 1 - step
            note = base
            for at in range(6):
                note = jnp.where(note_row == 3 + at, pieces[at, pl.ds(slot, 1), :], note)
            out_note[slot] = note.astype(jnp.bfloat16)

            @pl.when(slot > 0)
            def start_note():
                note_copy(slot, place(slot)).start()

            return carry

        repeat(n, send_note)

        def gap_of(edge, col, row):
            at = pl.ds(edge, 1)
            if keep:
                t_exp, s_exp = exps[edge, 0], exps[edge, 1]
            else:
                t_raw, s_raw = tile(left[col], inbox[row])
                t_exp = jnp.exp2((t_raw - stats[0, at, :]) * score_factor)
                s_exp = jnp.exp2((s_raw - stats[1, at, :]) * score_factor)
            return s_exp * weights[1, at, :] - t_exp * weights[0, at, :]

        def share_pair(pair, carry):
            high, low = edge_row[2 * pair], edge_col[2 * pair]
            gap = gap_of(2 * pair, low, high)
            back = gap_of(2 * pair + 1, high, low)
            symmetric = (gap + back.T).astype(jnp.bfloat16)
            shares[2 * pair] = jnp.dot(turned[low], symmetric, preferred_element_type=jnp.float32)
            shares[2 * pair + 1] = lax.dot_general(
                turned[high], symmetric, (((1,), (1,)), ((), ())),
                preferred_element_type=jnp.float32,
            )
            return carry

        repeat(most // 2, share_pair)

        def finish(step, carry):
            slot = n - 1 - step

            def add_share(turn, line):
                fresh = shares[edge_of[slot * n + (slot + turn + 1) % n]]
                return fresh if line is None else line + fresh

            line = repeat(n - 1, add_share, None if n <= 16 else jnp.zeros((HEAD_DIM, rows), jnp.float32))
            out_grad[slot] = (line * (distill_weight * HEAD_DIM ** (-0.5))).astype(jnp.bfloat16)

            @pl.when(slot > 0)
            def send_grad():
                grad_copy(slot, place(slot)).start()

            return carry

        repeat(n, finish)
        in_note[head] = out_note[0]
        in_grad[head] = out_grad[0]

    def take(buffers, sem):
        @pl.when(is_worker)
        def take_others():
            all_of(buffers, 0, heads - 1, sem).wait_recv()

        @pl.when(jnp.logical_not(is_worker))
        def take_all():
            all_of(buffers, 0, heads, sem).wait_recv()

    take(in_note, note_recv)
    for turn in range(heads):
        note = in_note[turn].astype(jnp.float32)
        t_weight = note[3:4] + note[4:5] + note[5:6]
        s_weight = note[6:7] + note[7:8] + note[8:9]
        gap = own_exps[turn, 1] * s_weight - own_exps[turn, 0] * t_weight
        symmetric = (gap + gap.T).astype(jnp.bfloat16)
        near[turn] = jnp.dot(own_turned[turn], symmetric, preferred_element_type=jnp.float32) * (
            distill_weight * HEAD_DIM ** (-0.5)
        )
        div_out[pl.ds(turn, 1), :] = note[0:1] + note[1:2] + note[2:3]
    @pl.when(is_worker)
    def drain_worker():
        all_of(outbox, 0, heads - 1, send_sem).wait_send()
        all_of(own_stats, 0, heads - 1, stat_send).wait_send()
        all_of(out_note, 1, n - 1, note_send).wait_send()
        all_of(out_grad, 1, n - 1, back_send).wait_send()

    @pl.when(jnp.logical_not(is_worker))
    def drain_server():
        all_of(outbox, 0, heads, send_sem).wait_send()
        all_of(own_stats, 0, heads, stat_send).wait_send()

    take(in_grad, back_recv)
    for turn in range(heads):
        grad_out[turn] = (in_grad[turn].astype(jnp.float32) + near[turn]).astype(jnp.bfloat16)


def unpack(in_grad, in_div, grad_ref, div_ref):
    heads = in_grad.shape[0]
    group = LANES // HEAD_DIM
    for pair in range(heads // group):
        both = jnp.concatenate([in_grad[pair * group + inner] for inner in range(group)], axis=0)
        grad_ref[:, pl.ds(pair * LANES, LANES)] = both.T
    div_lane = lax.broadcasted_iota(jnp.int32, (1, LANES), 1)
    div_row = jnp.zeros((1, LANES), jnp.float32)
    for slot in range(heads):
        div_row = jnp.where(div_lane == slot, in_div[pl.ds(slot, 1), :], div_row)
    div_ref[...] = div_row[:, :heads]


def per_device(n, teacher_q, student_q, owner_table):
    rows, width = teacher_q.shape
    heads = width // HEAD_DIM
    chips = n // 2
    owned = n // heads
    most = 2 * (n * owned - n)
    keep = most * 2 * rows * rows * 4 <= KEEP_BYTES
    hbm = pl.BlockSpec(memory_space=pl.ANY)
    vmem = pl.BlockSpec(memory_space=pltpu.VMEM)
    packed = pl.pallas_call(
        functools.partial(kernel, n, most, keep),
        out_shape=(
            pltpu.VMEM((heads, HEAD_DIM, rows), jnp.bfloat16),
            pltpu.VMEM((heads, rows), jnp.float32),
        ),
        in_specs=[hbm, hbm, hbm],
        out_specs=(vmem, vmem),
        scratch_shapes=[
            pltpu.VMEM((rows, width), jnp.bfloat16),
            pltpu.VMEM((rows, width), jnp.bfloat16),
            pltpu.VMEM((heads, rows, LANES), jnp.bfloat16),
            pltpu.VMEM((heads, HEAD_DIM, rows), jnp.bfloat16),
            pltpu.VMEM((heads, 2, rows, rows), jnp.float32),
            pltpu.VMEM((heads, 8, rows), jnp.float32),
            pltpu.VMEM((n, rows, LANES), jnp.bfloat16),
            pltpu.VMEM((n, 2 * rows, LANES), jnp.bfloat16),
            pltpu.VMEM((n, HEAD_DIM, rows), jnp.bfloat16),
            pltpu.VMEM((n, 8, rows), jnp.float32),
            pltpu.SMEM((n, n), jnp.int32),
            pltpu.SMEM((n * n + 2,), jnp.int32),
            pltpu.SMEM((n * n,), jnp.int32),
            pltpu.SMEM((most,), jnp.int32),
            pltpu.SMEM((most,), jnp.int32),
            pltpu.SMEM((most,), jnp.int32),
            pltpu.VMEM((5, most, rows), jnp.float32),
            pltpu.VMEM((2, n, rows), jnp.float32),
            pltpu.VMEM((2, n, rows), jnp.float32),
            pltpu.VMEM((2, most, rows), jnp.float32),
            pltpu.VMEM((6, n, rows), jnp.float32),
            pltpu.VMEM((most if keep else 1, 2, rows, rows), jnp.float32),
            pltpu.VMEM((most + 1, HEAD_DIM, rows), jnp.float32),
            pltpu.VMEM((n, NOTE_ROWS, rows), jnp.bfloat16),
            pltpu.VMEM((heads, NOTE_ROWS, rows), jnp.bfloat16),
            pltpu.VMEM((n, HEAD_DIM, rows), jnp.bfloat16),
            pltpu.VMEM((heads, HEAD_DIM, rows), jnp.bfloat16),
            pltpu.VMEM((heads, HEAD_DIM, rows), jnp.float32),
            pltpu.SemaphoreType.DMA((2,)),
            pltpu.SemaphoreType.DMA,
            pltpu.SemaphoreType.DMA,
            pltpu.SemaphoreType.DMA((chips,)),
            pltpu.SemaphoreType.DMA,
            pltpu.SemaphoreType.DMA,
            pltpu.SemaphoreType.DMA,
            pltpu.SemaphoreType.DMA,
            pltpu.SemaphoreType.DMA,
            pltpu.SemaphoreType.DMA,
        ],
        compiler_params=pltpu.CompilerParams(
            collective_id=0, has_side_effects=True, vmem_limit_bytes=60 * 1024 * 1024
        ),
        name="distill",
    )(*[pltpu.with_memory_space_constraint(x, pltpu.HBM) for x in (teacher_q, student_q, owner_table)])
    grad, divergence = pl.pallas_call(
        unpack,
        out_shape=(
            jax.ShapeDtypeStruct((rows, width), jnp.bfloat16),
            jax.ShapeDtypeStruct((1, heads), jnp.float32),
        ),
        in_specs=[vmem, vmem],
        out_specs=(vmem, vmem),
        compiler_params=pltpu.CompilerParams(vmem_limit_bytes=4 * 1024 * 1024),
        name="unpack",
    )(*packed)
    return (grad, divergence.reshape(heads))


def solution(mesh):
    placed = (P("tok", "head"), P("tok", "head"), P())
    return jax.shard_map(
        functools.partial(per_device, mesh.shape["tok"]),
        mesh=mesh,
        in_specs=placed,
        out_specs=(P("tok", "head"), P("head")),
        check_vma=False,
    )
```
